256 devices in a mesh: fsdp: 16 (over z_hi, x, core), dp: 16 (over z_lo, y).
Axes of the slice: x: 4, y: 4, z: 8 (z_hi: 2, z_lo: 4; z = z_hi * 4 + z_lo), core: 2. Of those that a mesh axis runs over, the one named last changes fastest.
Arguments:
- x_pre: bfloat16 [32768, 4096], P(('fsdp', 'dp')), may hold values from -6 to 6
- x_dec: bfloat16 [1024, 4096], P(('fsdp', 'dp')), may hold values from -6 to 6
- rec_hidden: bfloat16 [81920, 4096], P(('fsdp', 'dp')), may hold values from -6 to 6
- norm_gain: bfloat16 [4096], replicated, may hold values from 0.099609375 to 1.8984375
- w_query: bfloat16 [4096, 2048], P(('fsdp', 'dp')), may hold values from -1 to 1
- key_value_weight: bfloat16 [4096, 512], P(('fsdp', 'dp')), may hold values from -0.09375 to 0.09375
- cache_pool: bfloat16 [21504, 64, 512], P(('fsdp', 'dp')), may hold values from -12 to 12
- shared_kv: bfloat16 [131072, 512], P(('fsdp', 'dp')), may hold values from -12 to 12
- dec_len: int32 [256, 4], P(('fsdp', 'dp')), may hold values from 1 to 3072, as said below
- dec_table: int32 [256, 4, 48], P(('fsdp', 'dp')), may hold values from 0 to 83, as said below
- dec_group: int32 [256, 4], P(('fsdp', 'dp')), may hold values from 0 to 15, as said below
- prefix_len: int32 [16, 16], P('fsdp'), may hold values from 1 to 512, as said below
- pre_start: int32 [256], P(('fsdp', 'dp')), may hold values from 0 to 1024, as said below
- pre_table: int32 [256, 16], P(('fsdp', 'dp')), may hold values from 0 to 83, as said below
- rec_req: int32 [256, 320], P(('fsdp', 'dp')), may hold values from 0 to 3, as said below
- rec_off: int32 [256, 320], P(('fsdp', 'dp')), may hold values from 0 to 3071, as said below
Outputs:
- out_pre: bfloat16 [32768, 2048], P(('fsdp', 'dp'))
- out_dec: bfloat16 [1024, 2048], P(('fsdp', 'dp'))
The draws below stay inside these ranges and needn't reach their ends.
Inputs may be any that keep to these rules, and one draw needn't show every extreme that they name: `dec_len`: the private lengths of one device's decode requests sum to 4096; each device has one request of length exactly 3072. `dec_table`: the pages of one device's decode requests (the first ceil(dec_len / 64) entries of each row) and of its prefill history (the first pre_start / 64 entries) are all different; later entries are valid page numbers. `pre_table`: same pages as stated for dec_table. `dec_group`: A group names a device with the same fsdp index; a few groups along a line are far more common than the others. `prefix_len`: in every fsdp line some device holds a prefix of length exactly 512. `pre_start`: A multiple of 64; some device starts at exactly 1024. `rec_req`: the recomputed tokens of one device are different tokens of its decode requests. `rec_off`: below the request's dec_len.
All inputs are finite; a program needn't handle non-finite values.
Results may differ from the reference program's by a relative error of at most 0.0073.
Values may be sent and summed in bfloat16 or wider, within the bound.
No kernel may reach another device: no remote copies, remote signals or barrier semaphores. Data moves between devices by JAX's collectives and lax.ppermute only.
A program may use at most 192 MiB of HBM per device.

```python
import jax
import jax.numpy as jnp
from jax import lax

MODEL_WIDTH = 4096
QUERY_HEADS = 16
KEY_VALUE_HEADS = 2
HEAD_SIZE = 128
PAGE_TOKENS = 64
PREFILL_TOKENS = 128
DECODE_REQUESTS = 4
DEC_TOK = 4096
LMOST = 3072
HISTORY_LIMIT = 1024
SHARED_PREFIX = 512
REC = 320
POOL_PAGES = 84
N_FSDP = 16
N_DP = 16


def device_layout(key):
    source_generators = jax.random.split(key, 5)
    spare = DEC_TOK - LMOST - (DECODE_REQUESTS - 1)
    cuts = jnp.sort(jax.random.randint(source_generators[0], (DECODE_REQUESTS - 2,), 0, spare + 1)).astype(jnp.int32)
    edges = jnp.concatenate([jnp.zeros((1,), jnp.int32), cuts, jnp.full((1,), spare, jnp.int32)])
    others = edges[1:] - edges[:-1] + 1
    ordered = jnp.concatenate([jnp.full((1,), LMOST, jnp.int32), others])
    lengths = jnp.roll(ordered, jax.random.randint(source_generators[1], (), 0, DECODE_REQUESTS))
    counts = (lengths + PAGE_TOKENS - 1) // PAGE_TOKENS
    firsts = jnp.cumsum(counts) - counts
    shuffled = jax.random.permutation(source_generators[2], POOL_PAGES).astype(jnp.int32)
    page_table = shuffled[(firsts[:, None] + jnp.arange(LMOST // PAGE_TOKENS, dtype=jnp.int32)[None, :]) % POOL_PAGES]
    used_pages = jnp.sum(counts)
    prefill_pages = jax.random.randint(source_generators[3], (), 0, HISTORY_LIMIT // PAGE_TOKENS + 1)
    prefill_table = shuffled[(used_pages + jnp.arange(HISTORY_LIMIT // PAGE_TOKENS, dtype=jnp.int32)) % POOL_PAGES]
    chosen_rows = jax.random.permutation(source_generators[4], DEC_TOK)[:REC].astype(jnp.int32)
    endings = jnp.cumsum(lengths)
    request = jnp.sum((chosen_rows[:, None] >= endings[None, :]).astype(jnp.int32), axis=1)
    within = chosen_rows - (endings - lengths)[request]
    return (lengths, page_table, (prefill_pages * PAGE_TOKENS).astype(jnp.int32), prefill_table, request, within)


def line_layout(key):
    source_generators = jax.random.split(key, 4)
    owners = jax.random.permutation(source_generators[0], N_DP).astype(jnp.int32)
    lengths = jax.random.randint(source_generators[1], (N_DP,), 1, SHARED_PREFIX + 1)
    lengths = lengths.at[owners[0]].set(SHARED_PREFIX)
    first_pick = jax.random.randint(source_generators[2], (N_DP, DECODE_REQUESTS), 0, N_DP)
    second_pick = jax.random.randint(source_generators[3], (N_DP, DECODE_REQUESTS), 0, N_DP)
    return (lengths.astype(jnp.int32), owners[jnp.minimum(first_pick, second_pick)])


def layout(key):
    base = jax.random.fold_in(key, 4242)
    devices_all = N_FSDP * N_DP
    device_keys = jax.random.split(jax.random.fold_in(base, 1), devices_all)
    lengths, page_table, starts, prefill_table, request, within = jax.vmap(device_layout)(device_keys)
    busiest = jax.random.randint(jax.random.fold_in(base, 2), (), 0, devices_all)
    starts = starts.at[busiest].set(HISTORY_LIMIT)
    line_keys = jax.random.split(jax.random.fold_in(base, 3), N_FSDP)
    prefixes, groups = jax.vmap(line_layout)(line_keys)
    groups = groups.reshape(devices_all, DECODE_REQUESTS)
    return (lengths, page_table, groups, prefixes, starts, prefill_table, request, within)


def state_rows(key, salt, row_count):
    source_generators = jax.random.split(jax.random.fold_in(key, salt), 1)
    random_portion = jnp.clip(jax.random.normal(source_generators[0], (row_count, MODEL_WIDTH), jnp.float32), -6.0, 6.0)
    return random_portion


def draw_x_pre(key, part):
    random_portion = state_rows(key, 9201, N_FSDP * N_DP * PREFILL_TOKENS)
    return random_portion.astype(jnp.bfloat16)


def draw_x_dec(key, part):
    random_portion = state_rows(key, 9202, N_FSDP * N_DP * DECODE_REQUESTS)
    return random_portion.astype(jnp.bfloat16)


def draw_w_query(key, part):
    source_generator = jax.random.fold_in(key, 9301)
    random_portion = jnp.clip(jax.random.normal(source_generator, (MODEL_WIDTH, QUERY_HEADS * HEAD_SIZE), jnp.float32), -4.0, 4.0) * MODEL_WIDTH ** (-0.5)
    return random_portion.astype(jnp.bfloat16)


def draw_cache_pool(key, part):
    source_generator = jax.random.fold_in(key, 9401)
    random_portion = jnp.clip(jax.random.normal(source_generator, (N_FSDP * N_DP * POOL_PAGES, PAGE_TOKENS, 2 * KEY_VALUE_HEADS * HEAD_SIZE), jnp.float32), -6.0, 6.0)
    return random_portion.astype(jnp.bfloat16)


def draw_shared_kv(key, part):
    source_generator = jax.random.fold_in(key, 9501)
    random_portion = jnp.clip(jax.random.normal(source_generator, (N_FSDP * N_DP * SHARED_PREFIX, 2 * KEY_VALUE_HEADS * HEAD_SIZE), jnp.float32), -6.0, 6.0)
    return random_portion.astype(jnp.bfloat16)


def draw_dec_len(key, part):
    return layout(key)[0].astype(jnp.int32)


def draw_dec_table(key, part):
    return layout(key)[1].astype(jnp.int32)


def draw_dec_group(key, part):
    return layout(key)[2].astype(jnp.int32)


def draw_prefix_len(key, part):
    return layout(key)[3].astype(jnp.int32)


def draw_pre_start(key, part):
    return layout(key)[4].astype(jnp.int32)


def draw_pre_table(key, part):
    return layout(key)[5].astype(jnp.int32)


def draw_rec_req(key, part):
    return layout(key)[6].astype(jnp.int32)


def draw_rec_off(key, part):
    return layout(key)[7].astype(jnp.int32)


def level_of(key, shape, pieces, low, top_value):
    level, own = 1.0, jax.random.fold_in(key, 6)
    for dim, parts in pieces:
        steps = jnp.exp(jax.random.uniform(jax.random.fold_in(own, dim), (parts,), jnp.float32, low / len(pieces), top_value / len(pieces)))
        level = level * jnp.repeat(steps, shape[dim] // parts).reshape([-1 if axis == dim else 1 for axis in range(len(shape))])
    return level


def bell_draw(stream_key, shape, scale, limit, pieces=(), kind=jnp.bfloat16):
    level = level_of(stream_key, shape, pieces, -0.22, 0.18) if pieces else 1.0
    result = jax.random.normal(stream_key, shape, jnp.float32) * scale * level
    return jnp.minimum(jnp.maximum(result, -limit), limit).astype(kind)


def setup_inputs(seed: int = 0) -> dict:
    key_of = jax.random.split(jax.random.key(seed), 17)
    return {
        "x_pre": draw_x_pre(jax.random.fold_in(key_of[16], 71), 0),
        "x_dec": draw_x_dec(jax.random.fold_in(key_of[16], 71), 0),
        "rec_hidden": bell_draw(key_of[2], (N_FSDP * N_DP * REC, MODEL_WIDTH), 1.0, 6.0, ((0, 256),)),
        "norm_gain": jnp.clip(1.0 + 0.18 * jax.random.normal(key_of[3], (MODEL_WIDTH,), jnp.float32), 0.099609375, 1.8984375).astype(jnp.bfloat16),
        "w_query": draw_w_query(jax.random.fold_in(key_of[16], 71), 0),
        "key_value_weight": bell_draw(key_of[5], (MODEL_WIDTH, 2 * KEY_VALUE_HEADS * HEAD_SIZE), MODEL_WIDTH ** -0.5, 0.09375, ((0, 256),)),
        "cache_pool": draw_cache_pool(jax.random.fold_in(key_of[16], 71), 0),
        "shared_kv": draw_shared_kv(jax.random.fold_in(key_of[16], 71), 0),
        "dec_len": draw_dec_len(jax.random.fold_in(key_of[16], 71), 0),
        "dec_table": draw_dec_table(jax.random.fold_in(key_of[16], 71), 0),
        "dec_group": draw_dec_group(jax.random.fold_in(key_of[16], 71), 0),
        "prefix_len": draw_prefix_len(jax.random.fold_in(key_of[16], 71), 0),
        "pre_start": draw_pre_start(jax.random.fold_in(key_of[16], 71), 0),
        "pre_table": draw_pre_table(jax.random.fold_in(key_of[16], 71), 0),
        "rec_req": draw_rec_req(jax.random.fold_in(key_of[16], 71), 0),
        "rec_off": draw_rec_off(jax.random.fold_in(key_of[16], 71), 0),
    }


theta_base = 5000000.0
epsilon = 1e-05
negative_large = -1e+30

def rms_scaled(values, gain):
    widened = values.astype(jnp.float32)
    factor = lax.rsqrt(lax.optimization_barrier(jnp.mean(widened * widened, axis=-1, keepdims=True)) + epsilon)
    return (widened * factor * gain.astype(jnp.float32)).astype(jnp.bfloat16)

def rotate_halves(vectors, positions):
    half_dim = vectors.shape[-1] // 2
    frequency = theta_base ** (-jnp.arange(half_dim, dtype=jnp.float32) * 2.0 / vectors.shape[-1])
    angles = positions.astype(jnp.float32)[:, None, None] * frequency
    cosines = jnp.cos(angles)
    sines = jnp.sin(angles)
    first_half = vectors[..., :half_dim]
    second_half = vectors[..., half_dim:]
    return jnp.concatenate([first_half * cosines - second_half * sines, second_half * cosines + first_half * sines], axis=-1)

def reference(x_pre, x_dec, rec_hidden, norm_gain, w_query, key_value_weight, cache_pool, shared_kv, dec_len, dec_table, dec_group, prefix_len, pre_start, pre_table, rec_req, rec_off):
    devices_all = N_FSDP * N_DP
    group_share = QUERY_HEADS // KEY_VALUE_HEADS
    key_value_width = KEY_VALUE_HEADS * HEAD_SIZE
    scale_scores = HEAD_SIZE ** (-0.5)
    pool_all = cache_pool.reshape(devices_all, POOL_PAGES * PAGE_TOKENS, 2 * key_value_width)
    shared_all = shared_kv.reshape(N_FSDP, N_DP, SHARED_PREFIX, 2 * key_value_width)
    slot_range = jnp.arange(PAGE_TOKENS, dtype=jnp.int32)

    def one_device(device):
        line_index = device // N_DP
        pre_rows = rms_scaled(lax.dynamic_slice_in_dim(x_pre, device * PREFILL_TOKENS, PREFILL_TOKENS, 0), norm_gain)
        dec_rows = rms_scaled(lax.dynamic_slice_in_dim(x_dec, device * DECODE_REQUESTS, DECODE_REQUESTS, 0), norm_gain)
        rec_rows = rms_scaled(lax.dynamic_slice_in_dim(rec_hidden, device * REC, REC, 0), norm_gain)
        lengths = dec_len[device]
        page_table = dec_table[device]
        groups = dec_group[device]
        prefix_line = prefix_len[line_index]
        first_pos = pre_start[device]
        history_table = pre_table[device]
        request = rec_req[device]
        within = rec_off[device]
        query_rows = jnp.concatenate([pre_rows, dec_rows], axis=0)
        key_value_rows = jnp.concatenate([query_rows, rec_rows], axis=0)
        query_proj = jnp.dot(query_rows, w_query, preferred_element_type=jnp.float32).reshape(-1, QUERY_HEADS, HEAD_SIZE)
        key_value_projected = jnp.dot(key_value_rows, key_value_weight, preferred_element_type=jnp.float32).reshape(-1, 2 * KEY_VALUE_HEADS, HEAD_SIZE)
        pre_pos = first_pos + jnp.arange(PREFILL_TOKENS, dtype=jnp.int32)
        dec_pos = prefix_line[groups] + lengths
        rec_pos = prefix_line[groups[request]] + within
        query_pos = jnp.concatenate([pre_pos, dec_pos], axis=0)
        query_matrix = rotate_halves(query_proj, query_pos).astype(jnp.bfloat16)
        key_value_positions = jnp.concatenate([query_pos, rec_pos], axis=0)
        new_key_value = jnp.concatenate([rotate_halves(key_value_projected[:, :KEY_VALUE_HEADS], key_value_positions), key_value_projected[:, KEY_VALUE_HEADS:]], axis=1).astype(jnp.bfloat16)
        added_rows = new_key_value.reshape(-1, 2 * key_value_width)
        rec_page = page_table[request, within // PAGE_TOKENS]
        flattened_pool = pool_all[device].at[rec_page * PAGE_TOKENS + within % PAGE_TOKENS].set(added_rows[PREFILL_TOKENS + DECODE_REQUESTS:])
        private_lookup = (page_table[:, :, None] * PAGE_TOKENS + slot_range).reshape(DECODE_REQUESTS, LMOST)
        private_keys = flattened_pool[private_lookup]
        owned_pages = shared_all[line_index][groups]
        fresh_keys = added_rows[PREFILL_TOKENS:PREFILL_TOKENS + DECODE_REQUESTS][:, None, :]
        context_rows = jnp.concatenate([owned_pages, private_keys, fresh_keys], axis=1).reshape(DECODE_REQUESTS, -1, 2 * KEY_VALUE_HEADS, HEAD_SIZE)
        visible_mask = jnp.concatenate([jnp.arange(SHARED_PREFIX, dtype=jnp.int32)[None, :] < prefix_line[groups][:, None], jnp.arange(LMOST, dtype=jnp.int32)[None, :] < lengths[:, None], jnp.ones((DECODE_REQUESTS, 1), dtype=bool)], axis=1)
        decode_query = query_matrix[PREFILL_TOKENS:].reshape(DECODE_REQUESTS, KEY_VALUE_HEADS, group_share, HEAD_SIZE).astype(jnp.float32)
        score_matrix = jnp.einsum('qojv,qeov->qoje', decode_query, context_rows[:, :, :KEY_VALUE_HEADS].astype(jnp.float32), precision=lax.Precision.HIGHEST) * scale_scores
        allowed = visible_mask[:, None, None, :]
        masked = jnp.where(allowed, score_matrix, negative_large)
        maxima = lax.optimization_barrier(jnp.max(masked, axis=-1, keepdims=True))
        weight_matrix = jnp.where(allowed, jnp.exp(masked - maxima), 0.0)
        totals = lax.optimization_barrier(jnp.sum(weight_matrix, axis=-1))
        summed_output = jnp.einsum('wucm,wmuf->wucf', weight_matrix, context_rows[:, :, KEY_VALUE_HEADS:].astype(jnp.float32), precision=lax.Precision.HIGHEST)
        dec_out = (summed_output / totals[..., None]).astype(jnp.bfloat16).reshape(DECODE_REQUESTS, QUERY_HEADS * HEAD_SIZE)
        history_lookup = (history_table[:, None] * PAGE_TOKENS + slot_range).reshape(HISTORY_LIMIT)
        prefill_context = jnp.concatenate([flattened_pool[history_lookup], added_rows[:PREFILL_TOKENS]], axis=0).reshape(HISTORY_LIMIT + PREFILL_TOKENS, 2 * KEY_VALUE_HEADS, HEAD_SIZE)
        row_ids = jnp.arange(PREFILL_TOKENS, dtype=jnp.int32)
        pre_visible = jnp.concatenate([jnp.broadcast_to(jnp.arange(HISTORY_LIMIT, dtype=jnp.int32)[None, :] < first_pos, (PREFILL_TOKENS, HISTORY_LIMIT)), row_ids[None, :] <= row_ids[:, None]], axis=1)
        prefill_query = query_matrix[:PREFILL_TOKENS].reshape(PREFILL_TOKENS, KEY_VALUE_HEADS, group_share, HEAD_SIZE).astype(jnp.float32)
        prefill_scores = jnp.einsum('uwvm,owm->wvuo', prefill_query, prefill_context[:, :KEY_VALUE_HEADS].astype(jnp.float32), precision=lax.Precision.HIGHEST) * scale_scores
        pre_allowed = pre_visible[None, None]
        pre_masked = jnp.where(pre_allowed, prefill_scores, negative_large)
        pre_max = lax.optimization_barrier(jnp.max(pre_masked, axis=-1, keepdims=True))
        pre_weights = jnp.where(pre_allowed, jnp.exp(pre_masked - pre_max), 0.0)
        prefill_probabilities = (pre_weights / lax.optimization_barrier(jnp.sum(pre_weights, axis=-1, keepdims=True))).astype(jnp.bfloat16)
        prefill_output = jnp.einsum('jcse,eji->sjci', prefill_probabilities.astype(jnp.float32), prefill_context[:, KEY_VALUE_HEADS:].astype(jnp.float32), precision=lax.Precision.HIGHEST)
        return (prefill_output.astype(jnp.bfloat16).reshape(PREFILL_TOKENS, QUERY_HEADS * HEAD_SIZE), dec_out)
    pre_all, dec_all = lax.map(one_device, jnp.arange(devices_all, dtype=jnp.int32))
    return (pre_all.reshape(devices_all * PREFILL_TOKENS, QUERY_HEADS * HEAD_SIZE), dec_all.reshape(devices_all * DECODE_REQUESTS, QUERY_HEADS * HEAD_SIZE))
```

```python
import functools

import jax
import jax.numpy as jnp
from jax import lax
from jax.experimental import pallas as pl
from jax.experimental.pallas import tpu as pltpu
from jax.sharding import Mesh
from jax.sharding import PartitionSpec as P

QUERY_HEADS = 16
KEY_VALUE_HEADS = 2
GROUP = QUERY_HEADS // KEY_VALUE_HEADS
HEAD_SIZE = 128
PAGE_TOKENS = 64
PRE = 128
DEC = 4
REC = 320
LINE = 64
ROWS = PRE + LINE + REC
QROWS = PRE + LINE
DEC_SLOTS = 68
HIST_SLOTS = 16
HALF = GROUP * HEAD_SIZE
WIDE = HALF + 2 * HEAD_SIZE
MODEL = 4096
SPAN = 512
STAT = QUERY_HEADS * HEAD_SIZE

AXES = ("zh", "x", "c", "zl", "y")
DP = ("zl", "y")

theta_base = 5000000.0
epsilon = 1e-05
negative_large = -1e30
scale = HEAD_SIZE**-0.5

f32 = jnp.float32
bf16 = jnp.bfloat16
ANY = pl.BlockSpec(memory_space=pl.ANY)
VMEM = pl.BlockSpec(memory_space=pltpu.VMEM)
SMEM = pl.BlockSpec(memory_space=pltpu.SMEM)


def dot_t(a, b):
    return lax.dot_general(a, b, (((1,), (1,)), ((), ())), preferred_element_type=f32)


def dot(a, b):
    return lax.dot_general(a, b, (((1,), (0,)), ((), ())), preferred_element_type=f32)


def project_kernel(w_hbm, own_hbm, other_hbm, tab_own, tab_oth, q_own, kv_own, packed, w, x, w_sem, x_sem):
    copies = [
        pltpu.make_async_copy(own_hbm.at[0:QROWS], x.at[0:QROWS], x_sem.at[0]),
        pltpu.make_async_copy(other_hbm.at[0:QROWS], x.at[QROWS : 2 * QROWS], x_sem.at[1]),
        pltpu.make_async_copy(own_hbm.at[QROWS:ROWS], x.at[2 * QROWS : 2 * QROWS + REC], x_sem.at[2]),
        pltpu.make_async_copy(other_hbm.at[QROWS:ROWS], x.at[2 * QROWS + REC : 2 * ROWS], x_sem.at[3]),
    ]
    groups = [slice(g * 256, (g + 1) * 256) for g in range(WIDE // 256)]
    pieces = []
    for g, cols in enumerate(groups):
        for xi in range(4):
            for yi in range(4):
                pieces.append(
                    pltpu.make_async_copy(
                        w_hbm.at[xi * 4 + yi, :, :, :, :, cols],
                        w.at[:, xi, :, :, yi, :, cols],
                        w_sem.at[g, xi * 4 + yi],
                    )
                )
    for copy in copies[:2]:
        copy.start()
    for copy in pieces[:16]:
        copy.start()
    for copy in copies[2:]:
        copy.start()
    for copy in pieces[16:]:
        copy.start()
    for copy in copies[:2]:
        copy.wait()

    def turned(values, tab):
        return values * tab[:, :HEAD_SIZE] + pltpu.roll(values, HEAD_SIZE // 2, 1) * tab[:, HEAD_SIZE:]

    q_tab_own = tab_own[0:QROWS, :]
    q_tab_oth = tab_oth[0:QROWS, :]
    for g, cols in enumerate(groups):
        for copy in pieces[g * 16 : (g + 1) * 16]:
            copy.wait()
        wg = w[:, :, :, :, :, :, cols].reshape(MODEL, 256)
        if g < HALF // 256:
            acc = dot(x[0 : 2 * QROWS, :], wg)
            for h in range(2):
                at = slice(g * 256 + h * HEAD_SIZE, g * 256 + (h + 1) * HEAD_SIZE)
                part = acc[:, h * HEAD_SIZE : (h + 1) * HEAD_SIZE]
                q_own[:, at] = turned(part[:QROWS], q_tab_own).astype(bf16)
                packed[0:QROWS, at] = turned(part[QROWS:], q_tab_oth).astype(bf16)
        else:
            for copy in copies[2:]:
                copy.wait()
            acc = dot(x[...], wg)
            for own in (True, False):
                tab = (tab_own if own else tab_oth)[...]
                first = acc[0:QROWS] if own else acc[QROWS : 2 * QROWS]
                rest = acc[2 * QROWS : 2 * QROWS + REC] if own else acc[2 * QROWS + REC :]
                both = jnp.concatenate([first, rest], axis=0)
                keys = turned(both[:, :HEAD_SIZE], tab).astype(bf16)
                values = both[:, HEAD_SIZE:].astype(bf16)
                if own:
                    kv_own[:, :HEAD_SIZE] = keys
                    kv_own[:, HEAD_SIZE:] = values
                else:
                    for b in range(4):
                        rows = slice(b * 128, (b + 1) * 128)
                        packed[QROWS:, b * 256 : b * 256 + 128] = keys[rows]
                        packed[QROWS:, b * 256 + 128 : (b + 1) * 256] = values[rows]


def project(weights, own, other, tab_own, tab_oth):
    return pl.pallas_call(
        project_kernel,
        name="project",
        out_shape=(
            jax.ShapeDtypeStruct((QROWS, HALF), bf16),
            jax.ShapeDtypeStruct((ROWS, 2 * HEAD_SIZE), bf16),
            jax.ShapeDtypeStruct((QROWS + 128, HALF), bf16),
        ),
        in_specs=[ANY, ANY, ANY, VMEM, VMEM],
        out_specs=(VMEM, VMEM, VMEM),
        scratch_shapes=[
            pltpu.VMEM((2, 4, 2, 4, 4, 16, WIDE), bf16),
            pltpu.VMEM((2 * ROWS, MODEL), bf16),
            pltpu.SemaphoreType.DMA((WIDE // 256, 16)),
            pltpu.SemaphoreType.DMA((4,)),
        ],
        compiler_params=pltpu.CompilerParams(vmem_limit_bytes=40 << 20),
        cost_estimate=pl.CostEstimate(flops=6 * 10**9, bytes_accessed=20 * 10**6, transcendentals=0),
    )(weights, own, other, tab_own, tab_oth)


def shared_kernel(info, q_own, packed, kv, out, qs):
    core = info[0]
    qs[core] = q_own[PRE:QROWS, :]
    qs[1 - core] = packed[PRE:QROWS, :]
    limit = info[1]
    bias = jnp.where(lax.broadcasted_iota(jnp.int32, (1, SPAN), 1) < limit, 0.0, negative_large)
    lane = lax.broadcasted_iota(jnp.int32, (LINE, HEAD_SIZE), 1)
    stats = jnp.zeros((LINE, HEAD_SIZE), f32)
    for s in range(KEY_VALUE_HEADS):
        keys = kv[:, s * HEAD_SIZE : (s + 1) * HEAD_SIZE]
        values = kv[:, (2 + s) * HEAD_SIZE : (3 + s) * HEAD_SIZE]
        for h in range(GROUP):
            scores = dot_t(qs[s, :, h * HEAD_SIZE : (h + 1) * HEAD_SIZE], keys) + bias
            top = jnp.max(scores, axis=-1, keepdims=True)
            weights = jnp.exp((scores - top) * scale)
            total = jnp.sum(weights, axis=-1, keepdims=True)
            head = s * GROUP + h
            out[:, head * HEAD_SIZE : (head + 1) * HEAD_SIZE] = dot(weights.astype(bf16), values) / total
            stats = jnp.where(lane == head, top * scale + jnp.log(total), stats)
    out[:, STAT:] = stats


def shared_attention(info, q_own, packed, kv):
    return pl.pallas_call(
        shared_kernel,
        name="shared",
        out_shape=jax.ShapeDtypeStruct((LINE, STAT + 128), f32),
        in_specs=[SMEM, VMEM, VMEM, VMEM],
        out_specs=VMEM,
        scratch_shapes=[pltpu.VMEM((2, LINE, HALF), bf16)],
        compiler_params=pltpu.CompilerParams(vmem_limit_bytes=16 << 20),
        cost_estimate=pl.CostEstimate(flops=3 * 10**8, bytes_accessed=10**6, transcendentals=10**6),
    )(info, q_own, packed, kv)


def local_kernel(info, slots, q_own, kv_own, packed, bias_private, bias_new, pool, out_pre, out_dec, stat_dec, pages, qs, ks, sems):
    copies = []
    for i in list(range(DEC_SLOTS, DEC_SLOTS + HIST_SLOTS)) + list(range(DEC_SLOTS)):
        copies.append(pltpu.make_async_copy(pool.at[slots[i]], pages.at[i], sems.at[i]))
    for copy in copies:
        copy.start()
    core = info[0]
    start = info[2]
    place = info[3]
    qs[core] = q_own[...]
    qs[1 - core] = packed[0:QROWS, :]
    ks[core] = kv_own[...]
    for b in range(4):
        ks[1 - core, b * 128 : (b + 1) * 128, :] = packed[QROWS:, b * 256 : (b + 1) * 256]
    for copy in copies[:HIST_SLOTS]:
        copy.wait()
    history = HIST_SLOTS * PAGE_TOKENS
    seen = jnp.where(lax.broadcasted_iota(jnp.int32, (1, history), 1) < start, 0.0, negative_large)
    rows = lax.broadcasted_iota(jnp.int32, (PRE, PRE), 0)
    cols = lax.broadcasted_iota(jnp.int32, (PRE, PRE), 1)
    causal = jnp.where(cols <= rows, 0.0, negative_large)
    for s in range(KEY_VALUE_HEADS):
        old_keys = pages[DEC_SLOTS:, :, s * HEAD_SIZE : (s + 1) * HEAD_SIZE].reshape(history, HEAD_SIZE)
        old_values = pages[DEC_SLOTS:, :, (2 + s) * HEAD_SIZE : (3 + s) * HEAD_SIZE].reshape(history, HEAD_SIZE)
        new_keys = ks[s, 0:PRE, 0:HEAD_SIZE]
        new_values = ks[s, 0:PRE, HEAD_SIZE:]
        for h in range(GROUP):
            query = qs[s, 0:PRE, h * HEAD_SIZE : (h + 1) * HEAD_SIZE]
            first = dot_t(query, old_keys) + seen
            second = dot_t(query, new_keys) + causal
            top = jnp.maximum(jnp.max(first, axis=-1, keepdims=True), jnp.max(second, axis=-1, keepdims=True))
            first = jnp.exp((first - top) * scale)
            second = jnp.exp((second - top) * scale)
            total = jnp.sum(first, axis=-1, keepdims=True) + jnp.sum(second, axis=-1, keepdims=True)
            result = dot(first.astype(bf16), old_values) + dot(second.astype(bf16), new_values)
            head = s * GROUP + h
            out_pre[:, head * HEAD_SIZE : (head + 1) * HEAD_SIZE] = (result / total).astype(bf16)

    for copy in copies[HIST_SLOTS:]:
        copy.wait()
    private = DEC_SLOTS * PAGE_TOKENS
    pick = (
        lax.broadcasted_iota(jnp.int32, (8, LINE), 1)
        == lax.broadcasted_iota(jnp.int32, (8, LINE), 0) + place * DEC
    ) & (lax.broadcasted_iota(jnp.int32, (8, LINE), 0) < DEC)
    pick = jnp.where(pick, 1.0, 0.0).astype(bf16)
    lane = lax.broadcasted_iota(jnp.int32, (8, HEAD_SIZE), 1)
    stats = jnp.zeros((8, HEAD_SIZE), f32)
    for s in range(KEY_VALUE_HEADS):
        old_keys = pages[:DEC_SLOTS, :, s * HEAD_SIZE : (s + 1) * HEAD_SIZE].reshape(private, HEAD_SIZE)
        old_values = pages[:DEC_SLOTS, :, (2 + s) * HEAD_SIZE : (3 + s) * HEAD_SIZE].reshape(private, HEAD_SIZE)
        new_keys = ks[s, :, 0:HEAD_SIZE]
        new_values = ks[s, :, HEAD_SIZE:]
        line = dot(pick, qs[s, PRE:QROWS, :])
        query = jnp.concatenate([line[:, h * HEAD_SIZE : (h + 1) * HEAD_SIZE] for h in range(GROUP)], axis=0)
        query = query.astype(bf16)
        first = dot_t(query, old_keys).reshape(GROUP, 8, private) + bias_private[...][None]
        second = dot_t(query, new_keys).reshape(GROUP, 8, ROWS) + bias_new[...][None]
        first = first.reshape(GROUP * 8, private)
        second = second.reshape(GROUP * 8, ROWS)
        top = jnp.maximum(jnp.max(first, axis=-1, keepdims=True), jnp.max(second, axis=-1, keepdims=True))
        first = jnp.exp((first - top) * scale)
        second = jnp.exp((second - top) * scale)
        total = jnp.sum(first, axis=-1, keepdims=True) + jnp.sum(second, axis=-1, keepdims=True)
        result = dot(first.astype(bf16), old_values) + dot(second.astype(bf16), new_values)
        result = result / total
        level = top * scale + jnp.log(total)
        for h in range(GROUP):
            head = s * GROUP + h
            out_dec[:, head * HEAD_SIZE : (head + 1) * HEAD_SIZE] = result[h * 8 : (h + 1) * 8]
            stats = jnp.where(lane == head, level[h * 8 : (h + 1) * 8], stats)
    stat_dec[...] = stats


def local_attention(info, slots, q_own, kv_own, packed, bias_private, bias_new, pool):
    return pl.pallas_call(
        local_kernel,
        name="local",
        out_shape=(
            jax.ShapeDtypeStruct((PRE, QUERY_HEADS * HEAD_SIZE), bf16),
            jax.ShapeDtypeStruct((8, QUERY_HEADS * HEAD_SIZE), f32),
            jax.ShapeDtypeStruct((8, HEAD_SIZE), f32),
        ),
        in_specs=[SMEM, SMEM, VMEM, VMEM, VMEM, VMEM, VMEM, ANY],
        out_specs=(VMEM, VMEM, VMEM),
        scratch_shapes=[
            pltpu.VMEM((DEC_SLOTS + HIST_SLOTS, PAGE_TOKENS, 4 * HEAD_SIZE), bf16),
            pltpu.VMEM((2, QROWS, HALF), bf16),
            pltpu.VMEM((2, ROWS, 2 * HEAD_SIZE), bf16),
            pltpu.SemaphoreType.DMA((DEC_SLOTS + HIST_SLOTS,)),
        ],
        compiler_params=pltpu.CompilerParams(vmem_limit_bytes=32 << 20),
        cost_estimate=pl.CostEstimate(flops=10**10, bytes_accessed=8 * 10**6, transcendentals=3 * 10**6),
    )(info, slots, q_own, kv_own, packed, bias_private, bias_new, pool)


def finish_kernel(groups, shared, local, local_stat, out):
    for r in range(DEC):
        row = groups[r] * DEC + r
        eight = shared[pl.ds(pl.multiple_of(row // 8 * 8, 8), 8), :]
        hit = lax.broadcasted_iota(jnp.int32, eight.shape, 0) == row % 8
        chosen = jnp.sum(jnp.where(hit, eight, 0.0), axis=0, keepdims=True)
        far_stat = chosen[:, STAT:]
        near_stat = local_stat[r : r + 1, :]
        top = jnp.maximum(far_stat, near_stat)
        far = jnp.exp(far_stat - top)
        near = jnp.exp(near_stat - top)
        whole = far + near
        far = far / whole
        near = near / whole
        for head in range(QUERY_HEADS):
            at = slice(head * HEAD_SIZE, (head + 1) * HEAD_SIZE)
            mixed = chosen[:, at] * far[:, head : head + 1] + local[r : r + 1, at] * near[:, head : head + 1]
            out[r : r + 1, at] = mixed.astype(bf16)


def finish(groups, shared, local, local_stat):
    return pl.pallas_call(
        finish_kernel,
        name="finish",
        out_shape=jax.ShapeDtypeStruct((DEC, QUERY_HEADS * HEAD_SIZE), bf16),
        in_specs=[SMEM, VMEM, VMEM, VMEM],
        out_specs=VMEM,
        compiler_params=pltpu.CompilerParams(vmem_limit_bytes=8 << 20),
    )(groups, shared, local, local_stat)


def small_lookup(entries, indices):
    matches = indices[..., None] == jnp.arange(entries.shape[0], dtype=jnp.int32)
    return jnp.sum(jnp.where(matches, entries, 0), axis=-1)


def rms_scaled(values, gain):
    widened = values.astype(f32)
    factor = lax.rsqrt(jnp.mean(widened * widened, axis=-1, keepdims=True) + epsilon)
    return (widened * factor * gain.astype(f32)).astype(bf16)


def gather_weights(w_query, key_value_weight):
    key_half = key_value_weight.reshape(16, 2, 2, HEAD_SIZE)
    halves = [
        jnp.concatenate([w_query[:, c * HALF : (c + 1) * HALF], key_half[:, 0, c], key_half[:, 1, c]], axis=1)
        for c in range(2)
    ]
    block = jnp.stack(halves, axis=0)
    sent = jnp.broadcast_to(block[None, :, None], (2, 2, 4, 16, WIDE)).reshape(16, 16, WIDE)
    column = lax.all_to_all(sent, ("zh", "c", "zl"), 0, 0, tiled=True)
    whole = lax.all_gather(column.reshape(256, WIDE), ("x", "y"), axis=0, tiled=True)
    return whole.reshape(16, 2, 2, 4, 16, WIDE)


def on_device(
    x_pre, x_dec, rec_hidden, norm_gain, w_query, key_value_weight, cache_pool, shared_kv,
    dec_len, dec_table, dec_group, prefix_len, pre_start, pre_table, rec_req, rec_off,
):
    core = lax.axis_index("c")
    place = lax.axis_index("zl") * 4 + lax.axis_index("y")
    lengths = dec_len[0]
    page_table = dec_table[0]
    groups = dec_group[0]
    prefix_line = prefix_len[0]
    request = rec_req[0]
    within = rec_off[0]

    weights = gather_weights(w_query, key_value_weight)

    dec_pos = small_lookup(prefix_line, groups) + lengths
    parts = jnp.stack([dec_pos // 64, dec_pos % 64], axis=1).astype(bf16)
    extra = jnp.concatenate([x_dec, parts, jnp.zeros((DEC, 126), bf16)], axis=1)
    line = lax.all_to_all(
        jnp.broadcast_to(extra[None], (16, DEC, MODEL + 128)), DP, 0, 0, tiled=True
    ).reshape(LINE, MODEL + 128)
    line_parts = line[:, MODEL : MODEL + 2].astype(jnp.int32)
    line_pos = line_parts[:, 0] * 64 + line_parts[:, 1]

    rows = jnp.concatenate([x_pre, line[:, :MODEL], rec_hidden], axis=0)
    normed = rms_scaled(rows, norm_gain)
    pre_pos = pre_start[0] + jnp.arange(PRE, dtype=jnp.int32)
    rec_pos = small_lookup(prefix_line, small_lookup(groups, request)) + within
    positions = jnp.concatenate([pre_pos, line_pos, rec_pos], axis=0)
    half_dim = HEAD_SIZE // 2
    frequency = theta_base ** (-jnp.arange(half_dim, dtype=f32) * 2.0 / HEAD_SIZE)
    angles = positions.astype(f32)[:, None] * frequency
    cosines = jnp.cos(angles)
    sines = jnp.sin(angles)
    table = jnp.concatenate([cosines, cosines, -sines, sines], axis=1)
    swap = [(0, 1), (1, 0)]
    other = lax.ppermute(normed, "c", swap)
    other_table = lax.ppermute(table, "c", swap)

    counts = (lengths + PAGE_TOKENS - 1) // PAGE_TOKENS
    ends = jnp.cumsum(counts)
    firsts = ends - counts
    slot = jnp.arange(DEC_SLOTS, dtype=jnp.int32)
    slot_request = jnp.sum((slot[:, None] >= ends[None, :]).astype(jnp.int32), axis=1)
    used = slot_request < DEC
    slot_request = jnp.minimum(slot_request, DEC - 1)
    slot_page = jnp.where(used, slot - small_lookup(firsts, slot_request), 0)
    dec_pages = small_lookup(page_table.reshape(-1), slot_request * page_table.shape[1] + slot_page)
    slots = jnp.concatenate([dec_pages, pre_table[0]], axis=0)
    key_pos = slot_page[:, None] * PAGE_TOKENS + jnp.arange(PAGE_TOKENS, dtype=jnp.int32)[None, :]
    valid = used[:, None] & (key_pos < small_lookup(lengths, slot_request)[:, None])
    rec_slot = small_lookup(firsts, request) + within // PAGE_TOKENS
    slot_hot = (rec_slot[None, :] == slot[:, None]).astype(bf16)
    token_hot = (within[:, None] % PAGE_TOKENS == jnp.arange(PAGE_TOKENS, dtype=jnp.int32)[None, :]).astype(bf16)
    replaced = jnp.dot(slot_hot, token_hot, preferred_element_type=f32) > 0.5
    kept = (valid & ~replaced).reshape(-1)
    eight = jnp.arange(8, dtype=jnp.int32)
    key_request = jnp.repeat(slot_request, PAGE_TOKENS)
    junk = eight[:, None] >= DEC
    bias_private = jnp.where(junk | (kept[None, :] & (key_request[None, :] == eight[:, None])), 0.0, negative_large)
    new_request = jnp.concatenate(
        [jnp.full((PRE,), -1, jnp.int32), jnp.arange(LINE, dtype=jnp.int32) - place * DEC, request], axis=0
    )
    bias_new = jnp.where(junk | (new_request[None, :] == eight[:, None]), 0.0, negative_large)
    own_prefix = small_lookup(prefix_line, place[None])[0]
    info = jnp.stack([core, own_prefix, pre_start[0], place]).astype(jnp.int32)

    q_own, kv_own, packed = project(weights, normed, other, table, other_table)
    packed = lax.ppermute(packed, "c", swap)
    shared_part = shared_attention(info, q_own, packed, shared_kv)
    shared_part = lax.all_to_all(shared_part, DP, 0, 0, tiled=True)
    out_pre, dec_part, dec_stat = local_attention(
        info, slots, q_own, kv_own, packed, bias_private, bias_new, cache_pool
    )
    out_dec = finish(groups, shared_part, dec_part, dec_stat)
    return (out_pre, out_dec)


def solution(mesh):
    split = Mesh(mesh.devices.reshape(2, 4, 2, 4, 4), AXES)
    first = P(AXES, None)
    second = P(AXES, None, None)
    return jax.shard_map(
        on_device,
        mesh=split,
        in_specs=(
            first, first, first, P(), first, first, second, first,
            first, second, first, P(("zh", "x", "c"), None), P(AXES), first, first, first,
        ),
        out_specs=(first, first),
        check_vma=False,
    )
```

```python
import functools

import jax
import jax.numpy as jnp
from jax import lax
from jax.experimental import pallas as pl
from jax.experimental.pallas import tpu as pltpu
from jax.sharding import Mesh
from jax.sharding import PartitionSpec as P

QUERY_HEADS = 16
KEY_VALUE_HEADS = 2
GROUP = QUERY_HEADS // KEY_VALUE_HEADS
HEAD_SIZE = 128
PAGE_TOKENS = 64
PRE = 128
DEC = 4
REC = 320
LINE = 64
ROWS = PRE + LINE + REC
QROWS = PRE + LINE
DEC_SLOTS = 68
HIST_SLOTS = 16
HALF = GROUP * HEAD_SIZE
WIDE = HALF + 2 * HEAD_SIZE
MODEL = 4096
SPAN = 512
STAT = QUERY_HEADS * HEAD_SIZE
SPLIT = 512
HEADS_AT_ONCE = 2
LOG2E = 1.4426950408889634

AXES = ("zh", "x", "c", "zl", "y")
DP = ("zl", "y")

theta_base = 5000000.0
epsilon = 1e-05
negative_large = -1e30
scale = HEAD_SIZE**-0.5

f32 = jnp.float32
bf16 = jnp.bfloat16
ANY = pl.BlockSpec(memory_space=pl.ANY)
VMEM = pl.BlockSpec(memory_space=pltpu.VMEM)
HBM = pl.BlockSpec(memory_space=pltpu.HBM)
SMEM = pl.BlockSpec(memory_space=pltpu.SMEM)


def dot_t(a, b):
    return lax.dot_general(a, b, (((1,), (1,)), ((), ())), preferred_element_type=f32)


def dot(a, b):
    return lax.dot_general(a, b, (((1,), (0,)), ((), ())), preferred_element_type=f32)


def turned(values, tab):
    return values * tab[:, :HEAD_SIZE] + pltpu.roll(values, HEAD_SIZE // 2, 1) * tab[:, HEAD_SIZE:]

def project_kernel(w_hbm, own_hbm, other_hbm, tab_own, tab_oth, q_own, kv_own, packed, w, x, w_sem, x_sem):
    copies = [
        pltpu.make_async_copy(own_hbm.at[0:QROWS], x.at[0:QROWS], x_sem.at[0]),
        pltpu.make_async_copy(other_hbm.at[0:QROWS], x.at[QROWS : 2 * QROWS], x_sem.at[1]),
        pltpu.make_async_copy(own_hbm.at[QROWS:ROWS], x.at[2 * QROWS : 2 * QROWS + REC], x_sem.at[2]),
        pltpu.make_async_copy(other_hbm.at[QROWS:ROWS], x.at[2 * QROWS + REC : 2 * ROWS], x_sem.at[3]),
    ]
    groups = [(0, SPLIT), (SPLIT, WIDE)]
    pieces=[]
    for k,(lo,hi) in enumerate(groups):
        for xi in range(4):
            for yi in range(4):
                pieces.append(pltpu.make_async_copy(w_hbm.at[xi*4+yi, :, :, :, :, lo:hi], w.at[:, xi, :, :, yi, :, lo:hi], w_sem.at[k, xi*4+yi]))
    for copy in copies[:2]: copy.start()
    for copy in pieces: copy.start()
    for copy in copies[2:]: copy.start()
    for copy in copies[:2]: copy.wait()
    wf = w.reshape(MODEL, WIDE)
    for k,(lo,hi) in enumerate(groups):
        for copy in pieces[k*16:(k+1)*16]: copy.wait()
        for c0 in range(lo,hi,256):
            cols=slice(c0,c0+256)
            if c0<HALF:
                acc = dot(x[0:2*QROWS, :], wf[:, cols])
                for h in range(2):
                    at = slice(c0 + h * HEAD_SIZE, c0 + (h + 1) * HEAD_SIZE)
                    part = acc[:, h * HEAD_SIZE : (h + 1) * HEAD_SIZE]
                    q_own[:, at] = turned(part[:QROWS], tab_own[0:QROWS,:]).astype(bf16)
                    packed[0:QROWS, at] = turned(part[QROWS:], tab_oth[0:QROWS,:]).astype(bf16)
            else:
                for copy in copies[2:]: copy.wait()
                acc = dot(x[...], wf[:, cols])
                for own in (True, False):
                    tab = (tab_own if own else tab_oth)[...]
                    first = acc[0:QROWS] if own else acc[QROWS : 2 * QROWS]
                    rest = acc[2 * QROWS : 2 * QROWS + REC] if own else acc[2 * QROWS + REC :]
                    both = jnp.concatenate([first, rest], axis=0)
                    keys = turned(both[:, :HEAD_SIZE], tab).astype(bf16)
                    values = both[:, HEAD_SIZE:].astype(bf16)
                    if own:
                        kv_own[:, :HEAD_SIZE] = keys
                        kv_own[:, HEAD_SIZE:] = values
                    else:
                        for b in range(4):
                            rows = slice(b * 128, (b + 1) * 128)
                            packed[QROWS:, b * 256 : b * 256 + 128] = keys[rows]
                            packed[QROWS:, b * 256 + 128 : (b + 1) * 256] = values[rows]

def project(weights, own, other, tab_own, tab_oth):
    return pl.pallas_call(
        project_kernel, name="project",
        out_shape=(jax.ShapeDtypeStruct((QROWS, HALF), bf16), jax.ShapeDtypeStruct((ROWS, 2 * HEAD_SIZE), bf16), jax.ShapeDtypeStruct((QROWS + 128, HALF), bf16)),
        in_specs=[ANY, ANY, ANY, VMEM, VMEM], out_specs=(VMEM, VMEM, VMEM),
        scratch_shapes=[pltpu.VMEM((2, 4, 2, 4, 4, 16, WIDE), bf16), pltpu.VMEM((2 * ROWS, MODEL), bf16),
            pltpu.SemaphoreType.DMA((2, 16)), pltpu.SemaphoreType.DMA((4,))],
        compiler_params=pltpu.CompilerParams(vmem_limit_bytes=40 << 20),
        cost_estimate=pl.CostEstimate(flops=6 * 10**9, bytes_accessed=20 * 10**6, transcendentals=0),
    )(weights, own, other, tab_own, tab_oth)


def shared_kernel(info, q_own, packed, kv, out, qs):
    core = info[0]
    qs[core] = q_own[PRE:QROWS, :]
    qs[1 - core] = packed[PRE:QROWS, :]
    limit = info[1]
    bias = jnp.where(lax.broadcasted_iota(jnp.int32, (1, SPAN), 1) < limit, 0.0, negative_large)
    lane = lax.broadcasted_iota(jnp.int32, (LINE, HEAD_SIZE), 1)
    stats = jnp.zeros((LINE, HEAD_SIZE), f32)
    ones = jnp.ones((SPAN, HEAD_SIZE), bf16)
    c2 = scale*LOG2E
    for s in range(KEY_VALUE_HEADS):
        keys = kv[:, s * HEAD_SIZE : (s + 1) * HEAD_SIZE]
        values = jnp.concatenate([kv[:, (2 + s) * HEAD_SIZE : (3 + s) * HEAD_SIZE], ones], axis=1)
        query = jnp.concatenate([qs[s, :, h * HEAD_SIZE : (h + 1) * HEAD_SIZE] for h in range(GROUP)], axis=0)
        scores = dot_t(query, keys) + bias
        top = jnp.max(scores, axis=-1, keepdims=True)
        weights = jnp.exp2((scores - top) * c2)
        result = dot(weights.astype(bf16), values)
        total = result[:, HEAD_SIZE:]
        done = result[:, :HEAD_SIZE] / total
        level = top * scale + jnp.log(total)
        for h in range(GROUP):
            head = s * GROUP + h
            out[:, :, head * HEAD_SIZE : (head + 1) * HEAD_SIZE] = done[h*LINE:(h+1)*LINE].reshape(16,4,HEAD_SIZE)
            stats = jnp.where(lane == head, level[h*LINE:(h+1)*LINE], stats)
    out[:, :, STAT:] = stats.reshape(16,4,HEAD_SIZE)
def shared_attention(info, q_own, packed, kv):
    return pl.pallas_call(shared_kernel, name="shared", out_shape=jax.ShapeDtypeStruct((16,4, STAT + 128), f32),
        in_specs=[SMEM, VMEM, VMEM, VMEM], out_specs=VMEM, scratch_shapes=[pltpu.VMEM((2, LINE, HALF), bf16)],
        compiler_params=pltpu.CompilerParams(vmem_limit_bytes=16 << 20),
        cost_estimate=pl.CostEstimate(flops=3 * 10**8, bytes_accessed=10**6, transcendentals=10**6))(info, q_own, packed, kv)


def pages_kernel(slots, pool, pages, sems):
    copies=[pltpu.make_async_copy(pool.at[slots[i]], pages.at[i], sems.at[i]) for i in range(DEC_SLOTS+HIST_SLOTS)]
    for c in copies: c.start()
    for c in copies: c.wait()
def take_pages(slots,pool):
    return pl.pallas_call(pages_kernel,name="take_pages",out_shape=jax.ShapeDtypeStruct((DEC_SLOTS+HIST_SLOTS,PAGE_TOKENS,4*HEAD_SIZE),bf16),
      in_specs=[SMEM,HBM],out_specs=HBM,scratch_shapes=[pltpu.SemaphoreType.DMA((DEC_SLOTS+HIST_SLOTS,))],
      compiler_params=pltpu.CompilerParams(vmem_limit_bytes=60<<20),
      cost_estimate=pl.CostEstimate(flops=0, bytes_accessed=11 * 10**6, transcendentals=0))(slots,pool)

def local_kernel(info, q_own, kv_own, packed, bias_private, bias_new, pages_hbm, out_pre, out_dec, stat_dec, qs, ks, pages, sems):
    old = pltpu.make_async_copy(pages_hbm.at[DEC_SLOTS:], pages.at[DEC_SLOTS:], sems.at[0])
    old.start()
    cached = pltpu.make_async_copy(pages_hbm.at[:DEC_SLOTS], pages.at[:DEC_SLOTS], sems.at[1])
    cached.start()
    core = info[0]; start = info[2]; place = info[3]
    qs[core] = q_own[...]
    qs[1 - core] = packed[0:QROWS, :]
    ks[core] = kv_own[...]
    for b in range(4):
        ks[1 - core, b * 128 : (b + 1) * 128, :] = packed[QROWS:, b * 256 : (b + 1) * 256]
    history = HIST_SLOTS * PAGE_TOKENS
    seen = jnp.where(lax.broadcasted_iota(jnp.int32, (1, history), 1) < start, 0.0, negative_large)
    rows = lax.broadcasted_iota(jnp.int32, (PRE, PRE), 0)
    cols = lax.broadcasted_iota(jnp.int32, (PRE, PRE), 1)
    causal = jnp.where(cols <= rows, 0.0, negative_large)
    causal = jnp.concatenate([causal]*HEADS_AT_ONCE, axis=0)
    c2 = scale*LOG2E
    ones_h = jnp.ones((history, HEAD_SIZE), bf16)
    ones_n = jnp.ones((PRE, HEAD_SIZE), bf16)
    old.wait()
    for s in range(KEY_VALUE_HEADS):
        old_keys = pages[DEC_SLOTS:, :, s * HEAD_SIZE : (s + 1) * HEAD_SIZE].reshape(history, HEAD_SIZE)
        old_values = pages[DEC_SLOTS:, :, (2 + s) * HEAD_SIZE : (3 + s) * HEAD_SIZE].reshape(history, HEAD_SIZE)
        old_values = jnp.concatenate([old_values, ones_h], axis=1)
        new_keys = ks[s, 0:PRE, 0:HEAD_SIZE]
        new_values = jnp.concatenate([ks[s, 0:PRE, HEAD_SIZE:], ones_n], axis=1)
        for h in range(0, GROUP, HEADS_AT_ONCE):
            query = jnp.concatenate([qs[s, 0:PRE, (h+j) * HEAD_SIZE : (h+j + 1) * HEAD_SIZE] for j in range(HEADS_AT_ONCE)], axis=0)
            first = dot_t(query, old_keys) + seen
            second = dot_t(query, new_keys) + causal
            top = jnp.maximum(jnp.max(first, axis=-1, keepdims=True), jnp.max(second, axis=-1, keepdims=True))
            first = jnp.exp2((first - top) * c2)
            second = jnp.exp2((second - top) * c2)
            result = dot(first.astype(bf16), old_values) + dot(second.astype(bf16), new_values)
            done = (result[:, :HEAD_SIZE] / result[:, HEAD_SIZE:]).astype(bf16)
            for j in range(HEADS_AT_ONCE):
                head = s * GROUP + h + j
                out_pre[:, head * HEAD_SIZE : (head + 1) * HEAD_SIZE] = done[j*PRE:(j+1)*PRE]
    private = DEC_SLOTS * PAGE_TOKENS
    R = GROUP*DEC
    row = lax.broadcasted_iota(jnp.int32, (R, GROUP*LINE), 0)
    col = lax.broadcasted_iota(jnp.int32, (R, GROUP*LINE), 1)
    pick = (row >> 2 == col >> 6) & ((col & 63) == place * DEC + (row & 3))
    pick = jnp.where(pick, 1.0, 0.0).astype(bf16)
    cached.wait()
    for s in range(KEY_VALUE_HEADS):
        old_keys = pages[:DEC_SLOTS, :, s * HEAD_SIZE : (s + 1) * HEAD_SIZE].reshape(private, HEAD_SIZE)
        old_values = pages[:DEC_SLOTS, :, (2 + s) * HEAD_SIZE : (3 + s) * HEAD_SIZE].reshape(private, HEAD_SIZE)
        new_keys = ks[s, :, 0:HEAD_SIZE]
        new_values = ks[s, :, HEAD_SIZE:]
        line = jnp.concatenate([qs[s, PRE:QROWS, h * HEAD_SIZE : (h + 1) * HEAD_SIZE] for h in range(GROUP)], axis=0)
        query = dot(pick, line).astype(bf16)
        first = (dot_t(query, old_keys).reshape(R//8, 8, private) + bias_private[...][None]).reshape(R, private)
        second = (dot_t(query, new_keys).reshape(R//8, 8, ROWS) + bias_new[...][None]).reshape(R, ROWS)
        top = jnp.maximum(jnp.max(first, axis=-1, keepdims=True), jnp.max(second, axis=-1, keepdims=True))
        first = jnp.exp2((first - top) * c2)
        second = jnp.exp2((second - top) * c2)
        total = jnp.sum(first, axis=-1, keepdims=True) + jnp.sum(second, axis=-1, keepdims=True)
        result = dot(first.astype(bf16), old_values) + dot(second.astype(bf16), new_values)
        out_dec[s*R:(s+1)*R, :] = result / total
        stat_dec[s*R:(s+1)*R, :] = jnp.broadcast_to(top * scale + jnp.log(total), (R, HEAD_SIZE))

def local_attention(info, q_own, kv_own, packed, bias_private, bias_new, pages):
    return pl.pallas_call(
        local_kernel, name="local",
        out_shape=(jax.ShapeDtypeStruct((PRE, QUERY_HEADS * HEAD_SIZE), bf16), jax.ShapeDtypeStruct((64, HEAD_SIZE), f32), jax.ShapeDtypeStruct((64, HEAD_SIZE), f32)),
        in_specs=[SMEM, VMEM, VMEM, VMEM, VMEM, VMEM, HBM], out_specs=(VMEM, VMEM, VMEM),
        scratch_shapes=[pltpu.VMEM((2, QROWS, HALF), bf16), pltpu.VMEM((2, ROWS, 2 * HEAD_SIZE), bf16), pltpu.VMEM((DEC_SLOTS + HIST_SLOTS, PAGE_TOKENS, 4 * HEAD_SIZE), bf16), pltpu.SemaphoreType.DMA((2,))],
        compiler_params=pltpu.CompilerParams(vmem_limit_bytes=48 << 20),
        cost_estimate=pl.CostEstimate(flops=10**10, bytes_accessed=8 * 10**6, transcendentals=3 * 10**6),
    )(info, q_own, kv_own, packed, bias_private, bias_new, pages)


def finish_kernel(groups, shared, local, local_stat, out):
    row = lax.broadcasted_iota(jnp.int32, (DEC, STAT + 128), 0)
    chosen = jnp.zeros((DEC, STAT + 128), f32)
    for r in range(DEC):
        chosen = jnp.where(row == r, shared[groups[r]], chosen)
    for head in range(QUERY_HEADS):
        rows = slice(head*DEC,(head+1)*DEC)
        at = slice(head * HEAD_SIZE, (head + 1) * HEAD_SIZE)
        far = chosen[:, STAT+head:STAT+head+1]
        near = local_stat[rows, 0:1]
        top = jnp.maximum(far, near)
        far = jnp.exp(far - top); near = jnp.exp(near - top)
        whole = far + near
        out[:, at] = (chosen[:, at] * (far/whole) + local[rows, :] * (near/whole)).astype(bf16)
def finish(groups, shared, local, local_stat):
    return pl.pallas_call(finish_kernel, name="finish", out_shape=jax.ShapeDtypeStruct((DEC, QUERY_HEADS * HEAD_SIZE), bf16),
        in_specs=[SMEM, VMEM, VMEM, VMEM], out_specs=VMEM, compiler_params=pltpu.CompilerParams(vmem_limit_bytes=8 << 20))(groups, shared, local, local_stat)


def small_lookup(entries, indices):
    matches = indices[..., None] == jnp.arange(entries.shape[0], dtype=jnp.int32)
    return jnp.sum(jnp.where(matches, entries, 0), axis=-1)


def rms_scaled(values, gain):
    widened = values.astype(f32)
    factor = lax.rsqrt(jnp.mean(widened * widened, axis=-1, keepdims=True) + epsilon)
    return (widened * factor * gain.astype(f32)).astype(bf16)


def gather_weights(w_query, key_value_weight):
    key_half = key_value_weight.reshape(16, 2, 2, HEAD_SIZE)
    halves = [
        jnp.concatenate([w_query[:, c * HALF : (c + 1) * HALF], key_half[:, 0, c], key_half[:, 1, c]], axis=1)
        for c in range(2)
    ]
    block = jnp.stack(halves, axis=0)
    sent = jnp.broadcast_to(block[None, :, None], (2, 2, 4, 16, WIDE)).reshape(16, 16, WIDE)
    column = lax.all_to_all(sent, ("zh", "c", "zl"), 0, 0, tiled=True)
    whole = lax.all_gather(column.reshape(256, WIDE), ("x", "y"), axis=0, tiled=True)
    return whole.reshape(16, 2, 2, 4, 16, WIDE)


def on_device(
    x_pre, x_dec, rec_hidden, norm_gain, w_query, key_value_weight, cache_pool, shared_kv,
    dec_len, dec_table, dec_group, prefix_len, pre_start, pre_table, rec_req, rec_off,
):
    core = lax.axis_index("c")
    place = lax.axis_index("zl") * 4 + lax.axis_index("y")
    lengths = dec_len[0]
    page_table = dec_table[0]
    groups = dec_group[0]
    prefix_line = prefix_len[0]
    request = rec_req[0]
    within = rec_off[0]

    weights = gather_weights(w_query, key_value_weight)

    dec_pos = small_lookup(prefix_line, groups) + lengths
    parts = jnp.stack([dec_pos // 64, dec_pos % 64], axis=1).astype(bf16)
    extra = jnp.concatenate([x_dec, parts, jnp.zeros((DEC, 126), bf16)], axis=1)
    line = lax.all_to_all(
        jnp.broadcast_to(extra[None], (16, DEC, MODEL + 128)), DP, 0, 0, tiled=True
    ).reshape(LINE, MODEL + 128)
    line_parts = line[:, MODEL : MODEL + 2].astype(jnp.int32)
    line_pos = line_parts[:, 0] * 64 + line_parts[:, 1]

    rows = jnp.concatenate([x_pre, line[:, :MODEL], rec_hidden], axis=0)
    normed = rms_scaled(rows, norm_gain)
    pre_pos = pre_start[0] + jnp.arange(PRE, dtype=jnp.int32)
    rec_pos = small_lookup(prefix_line, small_lookup(groups, request)) + within
    positions = jnp.concatenate([pre_pos, line_pos, rec_pos], axis=0)
    half_dim = HEAD_SIZE // 2
    frequency = theta_base ** (-jnp.arange(half_dim, dtype=f32) * 2.0 / HEAD_SIZE)
    angles = positions.astype(f32)[:, None] * frequency
    cosines = jnp.cos(angles)
    sines = jnp.sin(angles)
    table = jnp.concatenate([cosines, cosines, -sines, sines], axis=1)
    swap = [(0, 1), (1, 0)]
    other = lax.ppermute(normed, "c", swap)
    other_table = lax.ppermute(table, "c", swap)

    counts = (lengths + PAGE_TOKENS - 1) // PAGE_TOKENS
    ends = jnp.cumsum(counts)
    firsts = ends - counts
    slot = jnp.arange(DEC_SLOTS, dtype=jnp.int32)
    slot_request = jnp.sum((slot[:, None] >= ends[None, :]).astype(jnp.int32), axis=1)
    used = slot_request < DEC
    slot_request = jnp.minimum(slot_request, DEC - 1)
    slot_page = jnp.where(used, slot - small_lookup(firsts, slot_request), 0)
    dec_pages = small_lookup(page_table.reshape(-1), slot_request * page_table.shape[1] + slot_page)
    slots = jnp.concatenate([dec_pages, pre_table[0]], axis=0)
    key_pos = slot_page[:, None] * PAGE_TOKENS + jnp.arange(PAGE_TOKENS, dtype=jnp.int32)[None, :]
    valid = used[:, None] & (key_pos < small_lookup(lengths, slot_request)[:, None])
    rec_slot = small_lookup(firsts, request) + within // PAGE_TOKENS
    slot_hot = (rec_slot[None, :] == slot[:, None]).astype(bf16)
    token_hot = (within[:, None] % PAGE_TOKENS == jnp.arange(PAGE_TOKENS, dtype=jnp.int32)[None, :]).astype(bf16)
    replaced = jnp.dot(slot_hot, token_hot, preferred_element_type=f32) > 0.5
    kept = (valid & ~replaced).reshape(-1)
    eight = jnp.arange(8, dtype=jnp.int32) % DEC
    key_request = jnp.repeat(slot_request, PAGE_TOKENS)
    bias_private = jnp.where(kept[None, :] & (key_request[None, :] == eight[:, None]), 0.0, negative_large)
    new_request = jnp.concatenate(
        [jnp.full((PRE,), -1, jnp.int32), jnp.arange(LINE, dtype=jnp.int32) - place * DEC, request], axis=0
    )
    bias_new = jnp.where(new_request[None, :] == eight[:, None], 0.0, negative_large)
    own_prefix = small_lookup(prefix_line, place[None])[0]
    info = jnp.stack([core, own_prefix, pre_start[0], place]).astype(jnp.int32)

    pages = take_pages(slots, cache_pool)
    weights, pages, bias_private, bias_new, info, slots = lax.optimization_barrier(
        (weights, pages, bias_private, bias_new, info, slots)
    )
    q_own, kv_own, packed = project(weights, normed, other, table, other_table)
    packed = lax.ppermute(packed, "c", swap)
    shared_part = shared_attention(info, q_own, packed, shared_kv)
    shared_part = lax.all_to_all(shared_part, DP, 0, 0, tiled=True)
    out_pre, dec_part, dec_stat = local_attention(
        info, q_own, kv_own, packed, bias_private, bias_new, pages
    )
    out_dec = finish(groups, shared_part, dec_part, dec_stat)
    return (out_pre, out_dec)


def solution(mesh):
    split = Mesh(mesh.devices.reshape(2, 4, 2, 4, 4), AXES)
    first = P(AXES, None)
    second = P(AXES, None, None)
    return jax.shard_map(
        on_device,
        mesh=split,
        in_specs=(
            first, first, first, P(), first, first, second, first,
            first, second, first, P(("zh", "x", "c"), None), P(AXES), first, first, first,
        ),
        out_specs=(first, first),
        check_vma=False,
    )
```

```python
import functools

import jax
import jax.numpy as jnp
from jax import lax
from jax.experimental import pallas as pl
from jax.experimental.pallas import tpu as pltpu
from jax.sharding import Mesh
from jax.sharding import PartitionSpec as P

QUERY_HEADS = 16
KEY_VALUE_HEADS = 2
GROUP = QUERY_HEADS // KEY_VALUE_HEADS
HEAD_SIZE = 128
PAGE_TOKENS = 64
PRE = 128
DEC = 4
REC = 320
LINE = 64
ROWS = PRE + LINE + REC
QROWS = PRE + LINE
DEC_SLOTS = 68
HIST_SLOTS = 16
HALF = GROUP * HEAD_SIZE
WIDE = HALF + 2 * HEAD_SIZE
MODEL = 4096
SPAN = 512
STAT = QUERY_HEADS * HEAD_SIZE
SPLIT = 512
HEADS_AT_ONCE = 2
LOG2E = 1.4426950408889634

AXES = ("zh", "x", "c", "zl", "y")
DP = ("zl", "y")

theta_base = 5000000.0
epsilon = 1e-05
negative_large = -1e30
scale = HEAD_SIZE**-0.5

f32 = jnp.float32
bf16 = jnp.bfloat16
ANY = pl.BlockSpec(memory_space=pl.ANY)
VMEM = pl.BlockSpec(memory_space=pltpu.VMEM)
HBM = pl.BlockSpec(memory_space=pltpu.HBM)
SMEM = pl.BlockSpec(memory_space=pltpu.SMEM)


def dot_t(a, b):
    return lax.dot_general(a, b, (((1,), (1,)), ((), ())), preferred_element_type=f32)


def dot(a, b):
    return lax.dot_general(a, b, (((1,), (0,)), ((), ())), preferred_element_type=f32)


def turned(values, tab):
    return values * tab[:, :HEAD_SIZE] + pltpu.roll(values, HEAD_SIZE // 2, 1) * tab[:, HEAD_SIZE:]

def project_kernel(w_hbm, own_hbm, other_hbm, tab_own, tab_oth, q_own, kv_own, packed, w, x, w_sem, x_sem):
    copies = [
        pltpu.make_async_copy(own_hbm.at[0:QROWS], x.at[0:QROWS], x_sem.at[0]),
        pltpu.make_async_copy(other_hbm.at[0:QROWS], x.at[QROWS : 2 * QROWS], x_sem.at[1]),
        pltpu.make_async_copy(own_hbm.at[QROWS:ROWS], x.at[2 * QROWS : 2 * QROWS + REC], x_sem.at[2]),
        pltpu.make_async_copy(other_hbm.at[QROWS:ROWS], x.at[2 * QROWS + REC : 2 * ROWS], x_sem.at[3]),
    ]
    groups = [(0, SPLIT), (SPLIT, WIDE)]
    pieces=[]
    for k,(lo,hi) in enumerate(groups):
        for xi in range(4):
            for yi in range(4):
                pieces.append(pltpu.make_async_copy(w_hbm.at[xi*4+yi, :, :, :, :, lo:hi], w.at[:, xi, :, :, yi, :, lo:hi], w_sem.at[k, xi*4+yi]))
    for copy in copies[:2]: copy.start()
    for copy in pieces: copy.start()
    for copy in copies[2:]: copy.start()
    for copy in copies[:2]: copy.wait()
    wf = w.reshape(MODEL, WIDE)
    for k,(lo,hi) in enumerate(groups):
        for copy in pieces[k*16:(k+1)*16]: copy.wait()
        for c0 in range(lo,hi,256):
            cols=slice(c0,c0+256)
            if c0<HALF:
                acc = dot(x[0:2*QROWS, :], wf[:, cols])
                for h in range(2):
                    at = slice(c0 + h * HEAD_SIZE, c0 + (h + 1) * HEAD_SIZE)
                    part = acc[:, h * HEAD_SIZE : (h + 1) * HEAD_SIZE]
                    q_own[:, at] = turned(part[:QROWS], tab_own[0:QROWS,:]).astype(bf16)
                    packed[0:QROWS, at] = turned(part[QROWS:], tab_oth[0:QROWS,:]).astype(bf16)
            else:
                for copy in copies[2:]: copy.wait()
                acc = dot(x[...], wf[:, cols])
                for own in (True, False):
                    tab = (tab_own if own else tab_oth)[...]
                    first = acc[0:QROWS] if own else acc[QROWS : 2 * QROWS]
                    rest = acc[2 * QROWS : 2 * QROWS + REC] if own else acc[2 * QROWS + REC :]
                    both = jnp.concatenate([first, rest], axis=0)
                    keys = turned(both[:, :HEAD_SIZE], tab).astype(bf16)
                    values = both[:, HEAD_SIZE:].astype(bf16)
                    if own:
                        kv_own[:, :HEAD_SIZE] = keys
                        kv_own[:, HEAD_SIZE:] = values
                    else:
                        for b in range(4):
                            rows = slice(b * 128, (b + 1) * 128)
                            packed[QROWS:, b * 256 : b * 256 + 128] = keys[rows]
                            packed[QROWS:, b * 256 + 128 : (b + 1) * 256] = values[rows]

def project(weights, own, other, tab_own, tab_oth):
    return pl.pallas_call(
        project_kernel, name="project",
        out_shape=(jax.ShapeDtypeStruct((QROWS, HALF), bf16), jax.ShapeDtypeStruct((ROWS, 2 * HEAD_SIZE), bf16), jax.ShapeDtypeStruct((QROWS + 128, HALF), bf16)),
        in_specs=[ANY, ANY, ANY, VMEM, VMEM], out_specs=(VMEM, VMEM, VMEM),
        scratch_shapes=[pltpu.VMEM((2, 4, 2, 4, 4, 16, WIDE), bf16), pltpu.VMEM((2 * ROWS, MODEL), bf16),
            pltpu.SemaphoreType.DMA((2, 16)), pltpu.SemaphoreType.DMA((4,))],
        compiler_params=pltpu.CompilerParams(vmem_limit_bytes=40 << 20),
        cost_estimate=pl.CostEstimate(flops=6 * 10**9, bytes_accessed=20 * 10**6, transcendentals=0),
    )(weights, own, other, tab_own, tab_oth)


def shared_kernel(info, q_own, packed, kv, out, qs):
    core = info[0]
    qs[core] = q_own[PRE:QROWS, :]
    qs[1 - core] = packed[PRE:QROWS, :]
    limit = info[1]
    bias = jnp.where(lax.broadcasted_iota(jnp.int32, (1, SPAN), 1) < limit, 0.0, negative_large)
    lane = lax.broadcasted_iota(jnp.int32, (LINE, HEAD_SIZE), 1)
    stats = jnp.zeros((LINE, HEAD_SIZE), f32)
    ones = jnp.ones((SPAN, HEAD_SIZE), bf16)
    c2 = scale*LOG2E
    for s in range(KEY_VALUE_HEADS):
        keys = kv[:, s * HEAD_SIZE : (s + 1) * HEAD_SIZE]
        values = jnp.concatenate([kv[:, (2 + s) * HEAD_SIZE : (3 + s) * HEAD_SIZE], ones], axis=1)
        query = jnp.concatenate([qs[s, :, h * HEAD_SIZE : (h + 1) * HEAD_SIZE] for h in range(GROUP)], axis=0)
        scores = dot_t(query, keys) + bias
        top = jnp.max(scores, axis=-1, keepdims=True)
        weights = jnp.exp2((scores - top) * c2)
        result = dot(weights.astype(bf16), values)
        total = result[:, HEAD_SIZE:]
        done = result[:, :HEAD_SIZE] / total
        level = top * scale + jnp.log(total)
        for h in range(GROUP):
            head = s * GROUP + h
            out[:, :, head * HEAD_SIZE : (head + 1) * HEAD_SIZE] = done[h*LINE:(h+1)*LINE].reshape(16,4,HEAD_SIZE)
            stats = jnp.where(lane == head, level[h*LINE:(h+1)*LINE], stats)
    out[:, :, STAT:] = stats.reshape(16,4,HEAD_SIZE)
def shared_attention(info, q_own, packed, kv):
    return pl.pallas_call(shared_kernel, name="shared", out_shape=jax.ShapeDtypeStruct((16,4, STAT + 128), f32),
        in_specs=[SMEM, VMEM, VMEM, VMEM], out_specs=VMEM, scratch_shapes=[pltpu.VMEM((2, LINE, HALF), bf16)],
        compiler_params=pltpu.CompilerParams(vmem_limit_bytes=16 << 20),
        cost_estimate=pl.CostEstimate(flops=3 * 10**8, bytes_accessed=10**6, transcendentals=10**6))(info, q_own, packed, kv)


def pages_kernel(slots, pool, pages, held, sems, out_sem):
    copies = [
        pltpu.make_async_copy(pool.at[slots[i]], held.at[i], sems.at[i]) for i in range(DEC_SLOTS + HIST_SLOTS)
    ]
    for copy in copies:
        copy.start()
    for copy in copies:
        copy.wait()
    out = pltpu.make_async_copy(held, pages, out_sem)
    out.start()
    out.wait()


def take_pages(slots, pool):
    shape = (DEC_SLOTS + HIST_SLOTS, PAGE_TOKENS, 4 * HEAD_SIZE)
    return pl.pallas_call(
        pages_kernel,
        name="take_pages",
        out_shape=jax.ShapeDtypeStruct(shape, bf16),
        in_specs=[SMEM, HBM],
        out_specs=HBM,
        scratch_shapes=[
            pltpu.VMEM(shape, bf16),
            pltpu.SemaphoreType.DMA((DEC_SLOTS + HIST_SLOTS,)),
            pltpu.SemaphoreType.DMA,
        ],
        compiler_params=pltpu.CompilerParams(vmem_limit_bytes=12 << 20),
        cost_estimate=pl.CostEstimate(flops=0, bytes_accessed=22 * 10**6, transcendentals=0),
    )(slots, pool)


def local_kernel(info, q_own, kv_own, packed, bias_private, bias_new, pages_hbm, out_pre, out_dec, stat_dec, qs, ks, pages, sems):
    old = pltpu.make_async_copy(pages_hbm.at[DEC_SLOTS:], pages.at[DEC_SLOTS:], sems.at[0])
    old.start()
    cached = pltpu.make_async_copy(pages_hbm.at[:DEC_SLOTS], pages.at[:DEC_SLOTS], sems.at[1])
    cached.start()
    core = info[0]; start = info[2]; place = info[3]
    qs[core] = q_own[...]
    qs[1 - core] = packed[0:QROWS, :]
    ks[core] = kv_own[...]
    for b in range(4):
        ks[1 - core, b * 128 : (b + 1) * 128, :] = packed[QROWS:, b * 256 : (b + 1) * 256]
    history = HIST_SLOTS * PAGE_TOKENS
    seen = jnp.where(lax.broadcasted_iota(jnp.int32, (1, history), 1) < start, 0.0, negative_large)
    rows = lax.broadcasted_iota(jnp.int32, (PRE, PRE), 0)
    cols = lax.broadcasted_iota(jnp.int32, (PRE, PRE), 1)
    causal = jnp.where(cols <= rows, 0.0, negative_large)
    causal = jnp.concatenate([causal]*HEADS_AT_ONCE, axis=0)
    c2 = scale*LOG2E
    ones_h = jnp.ones((history, HEAD_SIZE), bf16)
    ones_n = jnp.ones((PRE, HEAD_SIZE), bf16)
    old.wait()
    for s in range(KEY_VALUE_HEADS):
        old_keys = pages[DEC_SLOTS:, :, s * HEAD_SIZE : (s + 1) * HEAD_SIZE].reshape(history, HEAD_SIZE)
        old_values = pages[DEC_SLOTS:, :, (2 + s) * HEAD_SIZE : (3 + s) * HEAD_SIZE].reshape(history, HEAD_SIZE)
        old_values = jnp.concatenate([old_values, ones_h], axis=1)
        new_keys = ks[s, 0:PRE, 0:HEAD_SIZE]
        new_values = jnp.concatenate([ks[s, 0:PRE, HEAD_SIZE:], ones_n], axis=1)
        for h in range(0, GROUP, HEADS_AT_ONCE):
            query = jnp.concatenate([qs[s, 0:PRE, (h+j) * HEAD_SIZE : (h+j + 1) * HEAD_SIZE] for j in range(HEADS_AT_ONCE)], axis=0)
            first = dot_t(query, old_keys) + seen
            second = dot_t(query, new_keys) + causal
            top = jnp.maximum(jnp.max(first, axis=-1, keepdims=True), jnp.max(second, axis=-1, keepdims=True))
            first = jnp.exp2((first - top) * c2)
            second = jnp.exp2((second - top) * c2)
            result = dot(first.astype(bf16), old_values) + dot(second.astype(bf16), new_values)
            done = (result[:, :HEAD_SIZE] / result[:, HEAD_SIZE:]).astype(bf16)
            for j in range(HEADS_AT_ONCE):
                head = s * GROUP + h + j
                out_pre[:, head * HEAD_SIZE : (head + 1) * HEAD_SIZE] = done[j*PRE:(j+1)*PRE]
    private = DEC_SLOTS * PAGE_TOKENS
    R = GROUP*DEC
    row = lax.broadcasted_iota(jnp.int32, (R, GROUP*LINE), 0)
    col = lax.broadcasted_iota(jnp.int32, (R, GROUP*LINE), 1)
    pick = (row >> 2 == col >> 6) & ((col & 63) == place * DEC + (row & 3))
    pick = jnp.where(pick, 1.0, 0.0).astype(bf16)
    cached.wait()
    for s in range(KEY_VALUE_HEADS):
        old_keys = pages[:DEC_SLOTS, :, s * HEAD_SIZE : (s + 1) * HEAD_SIZE].reshape(private, HEAD_SIZE)
        old_values = pages[:DEC_SLOTS, :, (2 + s) * HEAD_SIZE : (3 + s) * HEAD_SIZE].reshape(private, HEAD_SIZE)
        new_keys = ks[s, :, 0:HEAD_SIZE]
        new_values = ks[s, :, HEAD_SIZE:]
        line = jnp.concatenate([qs[s, PRE:QROWS, h * HEAD_SIZE : (h + 1) * HEAD_SIZE] for h in range(GROUP)], axis=0)
        query = dot(pick, line).astype(bf16)
        first = (dot_t(query, old_keys).reshape(R//8, 8, private) + bias_private[...][None]).reshape(R, private)
        second = (dot_t(query, new_keys).reshape(R//8, 8, ROWS) + bias_new[...][None]).reshape(R, ROWS)
        top = jnp.maximum(jnp.max(first, axis=-1, keepdims=True), jnp.max(second, axis=-1, keepdims=True))
        first = jnp.exp2((first - top) * c2)
        second = jnp.exp2((second - top) * c2)
        total = jnp.sum(first, axis=-1, keepdims=True) + jnp.sum(second, axis=-1, keepdims=True)
        result = dot(first.astype(bf16), old_values) + dot(second.astype(bf16), new_values)
        out_dec[s*R:(s+1)*R, :] = result / total
        stat_dec[s*R:(s+1)*R, :] = jnp.broadcast_to(top * scale + jnp.log(total), (R, HEAD_SIZE))

def local_attention(info, q_own, kv_own, packed, bias_private, bias_new, pages):
    return pl.pallas_call(
        local_kernel, name="local",
        out_shape=(jax.ShapeDtypeStruct((PRE, QUERY_HEADS * HEAD_SIZE), bf16), jax.ShapeDtypeStruct((64, HEAD_SIZE), f32), jax.ShapeDtypeStruct((64, HEAD_SIZE), f32)),
        in_specs=[SMEM, VMEM, VMEM, VMEM, VMEM, VMEM, HBM], out_specs=(VMEM, VMEM, VMEM),
        scratch_shapes=[pltpu.VMEM((2, QROWS, HALF), bf16), pltpu.VMEM((2, ROWS, 2 * HEAD_SIZE), bf16), pltpu.VMEM((DEC_SLOTS + HIST_SLOTS, PAGE_TOKENS, 4 * HEAD_SIZE), bf16), pltpu.SemaphoreType.DMA((2,))],
        compiler_params=pltpu.CompilerParams(vmem_limit_bytes=48 << 20),
        cost_estimate=pl.CostEstimate(flops=10**10, bytes_accessed=8 * 10**6, transcendentals=3 * 10**6),
    )(info, q_own, kv_own, packed, bias_private, bias_new, pages)


def finish_kernel(groups, shared, local, local_stat, out):
    row = lax.broadcasted_iota(jnp.int32, (DEC, STAT + 128), 0)
    chosen = jnp.zeros((DEC, STAT + 128), f32)
    for r in range(DEC):
        chosen = jnp.where(row == r, shared[groups[r]], chosen)
    for head in range(QUERY_HEADS):
        rows = slice(head*DEC,(head+1)*DEC)
        at = slice(head * HEAD_SIZE, (head + 1) * HEAD_SIZE)
        far = chosen[:, STAT+head:STAT+head+1]
        near = local_stat[rows, 0:1]
        top = jnp.maximum(far, near)
        far = jnp.exp(far - top); near = jnp.exp(near - top)
        whole = far + near
        out[:, at] = (chosen[:, at] * (far/whole) + local[rows, :] * (near/whole)).astype(bf16)
def finish(groups, shared, local, local_stat):
    return pl.pallas_call(finish_kernel, name="finish", out_shape=jax.ShapeDtypeStruct((DEC, QUERY_HEADS * HEAD_SIZE), bf16),
        in_specs=[SMEM, VMEM, VMEM, VMEM], out_specs=VMEM, compiler_params=pltpu.CompilerParams(vmem_limit_bytes=8 << 20))(groups, shared, local, local_stat)


def small_lookup(entries, indices):
    matches = indices[..., None] == jnp.arange(entries.shape[0], dtype=jnp.int32)
    return jnp.sum(jnp.where(matches, entries, 0), axis=-1)


def rms_scaled(values, gain):
    widened = values.astype(f32)
    factor = lax.rsqrt(jnp.mean(widened * widened, axis=-1, keepdims=True) + epsilon)
    return (widened * factor * gain.astype(f32)).astype(bf16)


def gather_weights(w_query, key_value_weight):
    key_half = key_value_weight.reshape(16, 2, 2, HEAD_SIZE)
    halves = [
        jnp.concatenate([w_query[:, c * HALF : (c + 1) * HALF], key_half[:, 0, c], key_half[:, 1, c]], axis=1)
        for c in range(2)
    ]
    block = jnp.stack(halves, axis=0)
    sent = jnp.broadcast_to(block[None, :, None], (2, 2, 4, 16, WIDE)).reshape(16, 16, WIDE)
    column = lax.all_to_all(sent, ("zh", "c", "zl"), 0, 0, tiled=True)
    whole = lax.all_gather(column.reshape(256, WIDE), ("x", "y"), axis=0, tiled=True)
    return whole.reshape(16, 2, 2, 4, 16, WIDE)


def on_device(
    x_pre, x_dec, rec_hidden, norm_gain, w_query, key_value_weight, cache_pool, shared_kv,
    dec_len, dec_table, dec_group, prefix_len, pre_start, pre_table, rec_req, rec_off,
):
    core = lax.axis_index("c")
    place = lax.axis_index("zl") * 4 + lax.axis_index("y")
    lengths = dec_len[0]
    page_table = dec_table[0]
    groups = dec_group[0]
    prefix_line = prefix_len[0]
    request = rec_req[0]
    within = rec_off[0]

    weights = gather_weights(w_query, key_value_weight)

    dec_pos = small_lookup(prefix_line, groups) + lengths
    parts = jnp.stack([dec_pos // 64, dec_pos % 64], axis=1).astype(bf16)
    extra = jnp.concatenate([x_dec, parts, jnp.zeros((DEC, 126), bf16)], axis=1)
    line = lax.all_to_all(
        jnp.broadcast_to(extra[None], (16, DEC, MODEL + 128)), DP, 0, 0, tiled=True
    ).reshape(LINE, MODEL + 128)
    line_parts = line[:, MODEL : MODEL + 2].astype(jnp.int32)
    line_pos = line_parts[:, 0] * 64 + line_parts[:, 1]

    rows = jnp.concatenate([x_pre, line[:, :MODEL], rec_hidden], axis=0)
    normed = rms_scaled(rows, norm_gain)
    pre_pos = pre_start[0] + jnp.arange(PRE, dtype=jnp.int32)
    rec_pos = small_lookup(prefix_line, small_lookup(groups, request)) + within
    positions = jnp.concatenate([pre_pos, line_pos, rec_pos], axis=0)
    half_dim = HEAD_SIZE // 2
    frequency = theta_base ** (-jnp.arange(half_dim, dtype=f32) * 2.0 / HEAD_SIZE)
    angles = positions.astype(f32)[:, None] * frequency
    cosines = jnp.cos(angles)
    sines = jnp.sin(angles)
    table = jnp.concatenate([cosines, cosines, -sines, sines], axis=1)
    swap = [(0, 1), (1, 0)]
    other = lax.ppermute(normed, "c", swap)
    other_table = lax.ppermute(table, "c", swap)

    counts = (lengths + PAGE_TOKENS - 1) // PAGE_TOKENS
    ends = jnp.cumsum(counts)
    firsts = ends - counts
    slot = jnp.arange(DEC_SLOTS, dtype=jnp.int32)
    slot_request = jnp.sum((slot[:, None] >= ends[None, :]).astype(jnp.int32), axis=1)
    used = slot_request < DEC
    slot_request = jnp.minimum(slot_request, DEC - 1)
    slot_page = jnp.where(used, slot - small_lookup(firsts, slot_request), 0)
    dec_pages = small_lookup(page_table.reshape(-1), slot_request * page_table.shape[1] + slot_page)
    slots = jnp.concatenate([dec_pages, pre_table[0]], axis=0)
    key_pos = slot_page[:, None] * PAGE_TOKENS + jnp.arange(PAGE_TOKENS, dtype=jnp.int32)[None, :]
    valid = used[:, None] & (key_pos < small_lookup(lengths, slot_request)[:, None])
    rec_slot = small_lookup(firsts, request) + within // PAGE_TOKENS
    slot_hot = (rec_slot[None, :] == slot[:, None]).astype(bf16)
    token_hot = (within[:, None] % PAGE_TOKENS == jnp.arange(PAGE_TOKENS, dtype=jnp.int32)[None, :]).astype(bf16)
    replaced = jnp.dot(slot_hot, token_hot, preferred_element_type=f32) > 0.5
    kept = (valid & ~replaced).reshape(-1)
    eight = jnp.arange(8, dtype=jnp.int32) % DEC
    key_request = jnp.repeat(slot_request, PAGE_TOKENS)
    bias_private = jnp.where(kept[None, :] & (key_request[None, :] == eight[:, None]), 0.0, negative_large)
    new_request = jnp.concatenate(
        [jnp.full((PRE,), -1, jnp.int32), jnp.arange(LINE, dtype=jnp.int32) - place * DEC, request], axis=0
    )
    bias_new = jnp.where(new_request[None, :] == eight[:, None], 0.0, negative_large)
    own_prefix = small_lookup(prefix_line, place[None])[0]
    info = jnp.stack([core, own_prefix, pre_start[0], place]).astype(jnp.int32)

    pages = take_pages(slots, cache_pool)
    weights, pages, bias_private, bias_new, info, slots = lax.optimization_barrier(
        (weights, pages, bias_private, bias_new, info, slots)
    )
    q_own, kv_own, packed = project(weights, normed, other, table, other_table)
    packed = lax.ppermute(packed, "c", swap)
    shared_part = shared_attention(info, q_own, packed, shared_kv)
    shared_part = lax.all_to_all(shared_part, DP, 0, 0, tiled=True)
    out_pre, dec_part, dec_stat = local_attention(
        info, q_own, kv_own, packed, bias_private, bias_new, pages
    )
    out_dec = finish(groups, shared_part, dec_part, dec_stat)
    return (out_pre, out_dec)


def solution(mesh):
    split = Mesh(mesh.devices.reshape(2, 4, 2, 4, 4), AXES)
    first = P(AXES, None)
    second = P(AXES, None, None)
    return jax.shard_map(
        on_device,
        mesh=split,
        in_specs=(
            first, first, first, P(), first, first, second, first,
            first, second, first, P(("zh", "x", "c"), None), P(AXES), first, first, first,
        ),
        out_specs=(first, first),
        check_vma=False,
    )
```

```python
import functools

import jax
import jax.numpy as jnp
from jax import lax
from jax.experimental import pallas as pl
from jax.experimental.pallas import tpu as pltpu
from jax.sharding import Mesh
from jax.sharding import PartitionSpec as P

QUERY_HEADS = 16
KEY_VALUE_HEADS = 2
GROUP = QUERY_HEADS // KEY_VALUE_HEADS
HEAD_SIZE = 128
PAGE_TOKENS = 64
PRE = 128
DEC = 4
REC = 320
LINE = 64
ROWS = PRE + LINE + REC
QROWS = PRE + LINE
DEC_SLOTS = 68
HIST_SLOTS = 16
HALF = GROUP * HEAD_SIZE
WIDE = HALF + 2 * HEAD_SIZE
MODEL = 4096
SPAN = 512
STAT = QUERY_HEADS * HEAD_SIZE
MAIN = 896
SIDE = WIDE - MAIN
HEADS_AT_ONCE = 2
LOG2E = 1.4426950408889634

AXES = ("zh", "x", "c", "zl", "y")
DP = ("zl", "y")

theta_base = 5000000.0
epsilon = 1e-05
negative_large = -1e30
scale = HEAD_SIZE**-0.5

f32 = jnp.float32
bf16 = jnp.bfloat16
ANY = pl.BlockSpec(memory_space=pl.ANY)
VMEM = pl.BlockSpec(memory_space=pltpu.VMEM)
HBM = pl.BlockSpec(memory_space=pltpu.HBM)
SMEM = pl.BlockSpec(memory_space=pltpu.SMEM)


def dot_t(a, b):
    return lax.dot_general(a, b, (((1,), (1,)), ((), ())), preferred_element_type=f32)


def dot(a, b):
    return lax.dot_general(a, b, (((1,), (0,)), ((), ())), preferred_element_type=f32)


def turned(values, tab):
    return values * tab[:, :HEAD_SIZE] + pltpu.roll(values, HEAD_SIZE // 2, 1) * tab[:, HEAD_SIZE:]


def project_kernel(
    info, main_hbm, z0, up1, down1, up2, down2, up3, down3, up4, down4, own_hbm, other_hbm, tab_own, tab_oth,
    q_own, kv_own, packed, main, side, x, main_sem, side_sem, x_sem,
):
    x_copies = [
        pltpu.make_async_copy(own_hbm.at[0:QROWS], x.at[0:QROWS], x_sem.at[0]),
        pltpu.make_async_copy(other_hbm.at[0:QROWS], x.at[QROWS : 2 * QROWS], x_sem.at[1]),
        pltpu.make_async_copy(own_hbm.at[QROWS:ROWS], x.at[2 * QROWS : 2 * QROWS + REC], x_sem.at[2]),
        pltpu.make_async_copy(other_hbm.at[QROWS:ROWS], x.at[2 * QROWS + REC : 2 * ROWS], x_sem.at[3]),
    ]
    here = info[4]
    side_copies = []
    for i, (block, far) in enumerate(zip((z0, up1, down1, up2, down2, up3, down3), (0, -1, 1, -2, 2, -3, 3))):
        z = (here + far) & 7
        side_copies.append(pltpu.make_async_copy(block, side.at[z >> 2, :, :, z & 3], side_sem.at[i]))
    z = (here + 4) & 7
    side_copies.append(pltpu.make_async_copy(up4, side.at[z >> 2, 0:2, :, z & 3], side_sem.at[7]))
    side_copies.append(pltpu.make_async_copy(down4, side.at[z >> 2, 2:4, :, z & 3], side_sem.at[8]))
    groups = [(0, 512), (512, MAIN)]
    main_copies = []
    for k, (lo, hi) in enumerate(groups):
        for xi in range(4):
            for yi in range(4):
                main_copies.append(
                    pltpu.make_async_copy(
                        main_hbm.at[xi * 4 + yi, :, :, :, :, lo:hi],
                        main.at[:, xi, :, :, yi, :, lo:hi],
                        main_sem.at[k, xi * 4 + yi],
                    )
                )
    for copy in x_copies + side_copies + main_copies:
        copy.start()
    for copy in x_copies + side_copies:
        copy.wait()

    def store_queries(acc, first_head):
        for h in range(acc.shape[1] // HEAD_SIZE):
            at = slice((first_head + h) * HEAD_SIZE, (first_head + h + 1) * HEAD_SIZE)
            part = acc[:, h * HEAD_SIZE : (h + 1) * HEAD_SIZE]
            q_own[:, at] = turned(part[:QROWS], tab_own[0:QROWS, :]).astype(bf16)
            packed[0:QROWS, at] = turned(part[QROWS:], tab_oth[0:QROWS, :]).astype(bf16)

    side_flat = side.reshape(MODEL, SIDE)
    acc = dot(x[...], side_flat[:, SIDE - 256 :])
    for own in (True, False):
        tab = (tab_own if own else tab_oth)[...]
        first = acc[0:QROWS] if own else acc[QROWS : 2 * QROWS]
        rest = acc[2 * QROWS : 2 * QROWS + REC] if own else acc[2 * QROWS + REC :]
        both = jnp.concatenate([first, rest], axis=0)
        keys = turned(both[:, :HEAD_SIZE], tab).astype(bf16)
        values = both[:, HEAD_SIZE:].astype(bf16)
        if own:
            kv_own[:, :HEAD_SIZE] = keys
            kv_own[:, HEAD_SIZE:] = values
        else:
            for b in range(4):
                rows = slice(b * 128, (b + 1) * 128)
                packed[QROWS:, b * 256 : b * 256 + 128] = keys[rows]
                packed[QROWS:, b * 256 + 128 : (b + 1) * 256] = values[rows]
    store_queries(dot(x[0 : 2 * QROWS, :], side_flat[:, : SIDE - 256]), MAIN // HEAD_SIZE)
    main_flat = main.reshape(MODEL, MAIN)
    for k, (lo, hi) in enumerate(groups):
        for copy in main_copies[k * 16 : (k + 1) * 16]:
            copy.wait()
        for c0 in range(lo, hi, 256):
            c1 = min(c0 + 256, hi)
            store_queries(dot(x[0 : 2 * QROWS, :], main_flat[:, c0:c1]), c0 // HEAD_SIZE)


def project(info, main, side, own, other, tab_own, tab_oth):
    return pl.pallas_call(
        project_kernel,
        name="project",
        out_shape=(
            jax.ShapeDtypeStruct((QROWS, HALF), bf16),
            jax.ShapeDtypeStruct((ROWS, 2 * HEAD_SIZE), bf16),
            jax.ShapeDtypeStruct((QROWS + 128, HALF), bf16),
        ),
        in_specs=[SMEM] + [ANY] * 12 + [VMEM, VMEM],
        out_specs=(VMEM, VMEM, VMEM),
        scratch_shapes=[
            pltpu.VMEM((2, 4, 2, 4, 4, 16, MAIN), bf16),
            pltpu.VMEM((2, 4, 2, 4, 4, 16, SIDE), bf16),
            pltpu.VMEM((2 * ROWS, MODEL), bf16),
            pltpu.SemaphoreType.DMA((2, 16)),
            pltpu.SemaphoreType.DMA((9,)),
            pltpu.SemaphoreType.DMA((4,)),
        ],
        compiler_params=pltpu.CompilerParams(vmem_limit_bytes=40 << 20),
        cost_estimate=pl.CostEstimate(flops=6 * 10**9, bytes_accessed=20 * 10**6, transcendentals=0),
    )(info, main, *side, own, other, tab_own, tab_oth)


def shared_kernel(info, q_own, packed, kv, out, qs):
    core = info[0]
    qs[core] = q_own[PRE:QROWS, :]
    qs[1 - core] = packed[PRE:QROWS, :]
    limit = info[1]
    bias = jnp.where(lax.broadcasted_iota(jnp.int32, (1, SPAN), 1) < limit, 0.0, negative_large)
    lane = lax.broadcasted_iota(jnp.int32, (LINE, HEAD_SIZE), 1)
    stats = jnp.zeros((LINE, HEAD_SIZE), f32)
    ones = jnp.ones((SPAN, HEAD_SIZE), bf16)
    c2 = scale*LOG2E
    for s in range(KEY_VALUE_HEADS):
        keys = kv[:, s * HEAD_SIZE : (s + 1) * HEAD_SIZE]
        values = jnp.concatenate([kv[:, (2 + s) * HEAD_SIZE : (3 + s) * HEAD_SIZE], ones], axis=1)
        query = jnp.concatenate([qs[s, :, h * HEAD_SIZE : (h + 1) * HEAD_SIZE] for h in range(GROUP)], axis=0)
        scores = dot_t(query, keys) + bias
        top = jnp.max(scores, axis=-1, keepdims=True)
        weights = jnp.exp2((scores - top) * c2)
        result = dot(weights.astype(bf16), values)
        total = result[:, HEAD_SIZE:]
        done = result[:, :HEAD_SIZE] / total
        level = top * scale + jnp.log(total)
        for h in range(GROUP):
            head = s * GROUP + h
            out[:, :, head * HEAD_SIZE : (head + 1) * HEAD_SIZE] = done[h*LINE:(h+1)*LINE].reshape(16,4,HEAD_SIZE).astype(bf16)
            stats = jnp.where(lane == head, level[h*LINE:(h+1)*LINE], stats)
    high = stats.astype(bf16).astype(f32)
    left = stats - high
    middle = left.astype(bf16).astype(f32)
    low = left - middle
    parts = high + pltpu.roll(middle, QUERY_HEADS, 1) + pltpu.roll(low, 2 * QUERY_HEADS, 1)
    out[:, :, STAT:] = parts.reshape(16, 4, HEAD_SIZE).astype(bf16)
def shared_attention(info, q_own, packed, kv):
    return pl.pallas_call(shared_kernel, name="shared", out_shape=jax.ShapeDtypeStruct((16, 4, STAT + 128), bf16),
        in_specs=[SMEM, VMEM, VMEM, VMEM], out_specs=VMEM, scratch_shapes=[pltpu.VMEM((2, LINE, HALF), bf16)],
        compiler_params=pltpu.CompilerParams(vmem_limit_bytes=16 << 20),
        cost_estimate=pl.CostEstimate(flops=3 * 10**8, bytes_accessed=10**6, transcendentals=10**6))(info, q_own, packed, kv)


def pages_kernel(slots, pool, pages, held, sems, out_sem):
    copies = [
        pltpu.make_async_copy(pool.at[slots[i]], held.at[i], sems.at[i]) for i in range(DEC_SLOTS + HIST_SLOTS)
    ]
    for copy in copies:
        copy.start()
    for copy in copies:
        copy.wait()
    out = pltpu.make_async_copy(held, pages, out_sem)
    out.start()
    out.wait()


def take_pages(slots, pool):
    shape = (DEC_SLOTS + HIST_SLOTS, PAGE_TOKENS, 4 * HEAD_SIZE)
    return pl.pallas_call(
        pages_kernel,
        name="take_pages",
        out_shape=jax.ShapeDtypeStruct(shape, bf16),
        in_specs=[SMEM, HBM],
        out_specs=HBM,
        scratch_shapes=[
            pltpu.VMEM(shape, bf16),
            pltpu.SemaphoreType.DMA((DEC_SLOTS + HIST_SLOTS,)),
            pltpu.SemaphoreType.DMA,
        ],
        compiler_params=pltpu.CompilerParams(vmem_limit_bytes=12 << 20),
        cost_estimate=pl.CostEstimate(flops=0, bytes_accessed=22 * 10**6, transcendentals=0),
    )(slots, pool)


def local_kernel(info, q_own, kv_own, packed, bias_private, bias_new, pages_hbm, out_pre, out_dec, stat_dec, qs, ks, pages, sems):
    old = pltpu.make_async_copy(pages_hbm.at[DEC_SLOTS:], pages.at[DEC_SLOTS:], sems.at[0])
    old.start()
    cached = pltpu.make_async_copy(pages_hbm.at[:DEC_SLOTS], pages.at[:DEC_SLOTS], sems.at[1])
    cached.start()
    core = info[0]; start = info[2]; place = info[3]
    qs[core] = q_own[...]
    qs[1 - core] = packed[0:QROWS, :]
    ks[core] = kv_own[...]
    for b in range(4):
        ks[1 - core, b * 128 : (b + 1) * 128, :] = packed[QROWS:, b * 256 : (b + 1) * 256]
    history = HIST_SLOTS * PAGE_TOKENS
    seen = jnp.where(lax.broadcasted_iota(jnp.int32, (1, history), 1) < start, 0.0, negative_large)
    rows = lax.broadcasted_iota(jnp.int32, (PRE, PRE), 0)
    cols = lax.broadcasted_iota(jnp.int32, (PRE, PRE), 1)
    causal = jnp.where(cols <= rows, 0.0, negative_large)
    causal = jnp.concatenate([causal]*HEADS_AT_ONCE, axis=0)
    c2 = scale*LOG2E
    ones_h = jnp.ones((history, HEAD_SIZE), bf16)
    ones_n = jnp.ones((PRE, HEAD_SIZE), bf16)
    old.wait()
    for s in range(KEY_VALUE_HEADS):
        old_keys = pages[DEC_SLOTS:, :, s * HEAD_SIZE : (s + 1) * HEAD_SIZE].reshape(history, HEAD_SIZE)
        old_values = pages[DEC_SLOTS:, :, (2 + s) * HEAD_SIZE : (3 + s) * HEAD_SIZE].reshape(history, HEAD_SIZE)
        old_values = jnp.concatenate([old_values, ones_h], axis=1)
        new_keys = ks[s, 0:PRE, 0:HEAD_SIZE]
        new_values = jnp.concatenate([ks[s, 0:PRE, HEAD_SIZE:], ones_n], axis=1)
        for h in range(0, GROUP, HEADS_AT_ONCE):
            query = jnp.concatenate([qs[s, 0:PRE, (h+j) * HEAD_SIZE : (h+j + 1) * HEAD_SIZE] for j in range(HEADS_AT_ONCE)], axis=0)
            first = dot_t(query, old_keys) + seen
            second = dot_t(query, new_keys) + causal
            top = jnp.maximum(jnp.max(first, axis=-1, keepdims=True), jnp.max(second, axis=-1, keepdims=True))
            first = jnp.exp2((first - top) * c2)
            second = jnp.exp2((second - top) * c2)
            result = dot(first.astype(bf16), old_values) + dot(second.astype(bf16), new_values)
            done = (result[:, :HEAD_SIZE] / result[:, HEAD_SIZE:]).astype(bf16)
            for j in range(HEADS_AT_ONCE):
                head = s * GROUP + h + j
                out_pre[:, head * HEAD_SIZE : (head + 1) * HEAD_SIZE] = done[j*PRE:(j+1)*PRE]
    private = DEC_SLOTS * PAGE_TOKENS
    R = GROUP*DEC
    row = lax.broadcasted_iota(jnp.int32, (R, GROUP*LINE), 0)
    col = lax.broadcasted_iota(jnp.int32, (R, GROUP*LINE), 1)
    pick = (row >> 2 == col >> 6) & ((col & 63) == place * DEC + (row & 3))
    pick = jnp.where(pick, 1.0, 0.0).astype(bf16)
    cached.wait()
    for s in range(KEY_VALUE_HEADS):
        old_keys = pages[:DEC_SLOTS, :, s * HEAD_SIZE : (s + 1) * HEAD_SIZE].reshape(private, HEAD_SIZE)
        old_values = pages[:DEC_SLOTS, :, (2 + s) * HEAD_SIZE : (3 + s) * HEAD_SIZE].reshape(private, HEAD_SIZE)
        new_keys = ks[s, :, 0:HEAD_SIZE]
        new_values = ks[s, :, HEAD_SIZE:]
        line = jnp.concatenate([qs[s, PRE:QROWS, h * HEAD_SIZE : (h + 1) * HEAD_SIZE] for h in range(GROUP)], axis=0)
        query = dot(pick, line).astype(bf16)
        first = (dot_t(query, old_keys).reshape(R//8, 8, private) + bias_private[...][None]).reshape(R, private)
        second = (dot_t(query, new_keys).reshape(R//8, 8, ROWS) + bias_new[...][None]).reshape(R, ROWS)
        top = jnp.maximum(jnp.max(first, axis=-1, keepdims=True), jnp.max(second, axis=-1, keepdims=True))
        first = jnp.exp2((first - top) * c2)
        second = jnp.exp2((second - top) * c2)
        total = jnp.sum(first, axis=-1, keepdims=True) + jnp.sum(second, axis=-1, keepdims=True)
        result = dot(first.astype(bf16), old_values) + dot(second.astype(bf16), new_values)
        out_dec[s*R:(s+1)*R, :] = result / total
        stat_dec[s*R:(s+1)*R, :] = jnp.broadcast_to(top * scale + jnp.log(total), (R, HEAD_SIZE))

def local_attention(info, q_own, kv_own, packed, bias_private, bias_new, pages):
    return pl.pallas_call(
        local_kernel, name="local",
        out_shape=(jax.ShapeDtypeStruct((PRE, QUERY_HEADS * HEAD_SIZE), bf16), jax.ShapeDtypeStruct((64, HEAD_SIZE), f32), jax.ShapeDtypeStruct((64, HEAD_SIZE), f32)),
        in_specs=[SMEM, VMEM, VMEM, VMEM, VMEM, VMEM, HBM], out_specs=(VMEM, VMEM, VMEM),
        scratch_shapes=[pltpu.VMEM((2, QROWS, HALF), bf16), pltpu.VMEM((2, ROWS, 2 * HEAD_SIZE), bf16), pltpu.VMEM((DEC_SLOTS + HIST_SLOTS, PAGE_TOKENS, 4 * HEAD_SIZE), bf16), pltpu.SemaphoreType.DMA((2,))],
        compiler_params=pltpu.CompilerParams(vmem_limit_bytes=48 << 20),
        cost_estimate=pl.CostEstimate(flops=10**10, bytes_accessed=8 * 10**6, transcendentals=3 * 10**6),
    )(info, q_own, kv_own, packed, bias_private, bias_new, pages)


def finish_kernel(groups, shared, local, local_stat, out):
    row = lax.broadcasted_iota(jnp.int32, (DEC, STAT + 128), 0)
    chosen = jnp.zeros((DEC, STAT + 128), f32)
    for r in range(DEC):
        chosen = jnp.where(row == r, shared[groups[r]].astype(f32), chosen)
    for head in range(QUERY_HEADS):
        rows = slice(head*DEC,(head+1)*DEC)
        at = slice(head * HEAD_SIZE, (head + 1) * HEAD_SIZE)
        at_stat = STAT + head
        far = (
            chosen[:, at_stat : at_stat + 1]
            + chosen[:, at_stat + QUERY_HEADS : at_stat + QUERY_HEADS + 1]
            + chosen[:, at_stat + 2 * QUERY_HEADS : at_stat + 2 * QUERY_HEADS + 1]
        )
        near = local_stat[rows, 0:1]
        top = jnp.maximum(far, near)
        far = jnp.exp(far - top); near = jnp.exp(near - top)
        whole = far + near
        out[:, at] = (chosen[:, at] * (far/whole) + local[rows, :] * (near/whole)).astype(bf16)
def finish(groups, shared, local, local_stat):
    return pl.pallas_call(finish_kernel, name="finish", out_shape=jax.ShapeDtypeStruct((DEC, QUERY_HEADS * HEAD_SIZE), bf16),
        in_specs=[SMEM, VMEM, VMEM, VMEM], out_specs=VMEM, compiler_params=pltpu.CompilerParams(vmem_limit_bytes=8 << 20))(groups, shared, local, local_stat)


def small_lookup(entries, indices):
    matches = indices[..., None] == jnp.arange(entries.shape[0], dtype=jnp.int32)
    return jnp.sum(jnp.where(matches, entries, 0), axis=-1)


def rms_scaled(values, gain):
    widened = values.astype(f32)
    factor = lax.rsqrt(jnp.mean(widened * widened, axis=-1, keepdims=True) + epsilon)
    return (widened * factor * gain.astype(f32)).astype(bf16)


def along_z(step):
    pairs = []
    for i in range(256):
        z = (i // 128) * 4 + (i // 4) % 4
        to = (z + step) % 8
        pairs.append((i, i % 128 - (i // 4) % 4 * 4 + (to // 4) * 128 + (to % 4) * 4))
    return pairs


def start_weights(w_query, key_value_weight):
    key_half = key_value_weight.reshape(16, 2, 2, HEAD_SIZE)
    halves = [
        jnp.concatenate([w_query[:, c * HALF : (c + 1) * HALF], key_half[:, 0, c], key_half[:, 1, c]], axis=1)
        for c in range(2)
    ]
    block = jnp.stack(halves, axis=0)
    sent = jnp.broadcast_to(block[None, :, None, :, :MAIN], (2, 2, 4, 16, MAIN)).reshape(16, 16, MAIN)
    column = lax.all_to_all(sent, ("zh", "c", "zl"), 0, 0, tiled=True)
    rest, column = lax.optimization_barrier((block[:, :, MAIN:], column))
    main = lax.all_gather(column.reshape(256, MAIN), ("x", "y"), axis=0, tiled=True)
    main = main.reshape(16, 2, 2, 4, 16, MAIN)
    sent = jnp.broadcast_to(rest[None, :, None], (4, 2, 4, 16, SIDE)).reshape(32, 16, SIDE)
    plane = lax.all_to_all(sent, ("x", "c", "y"), 0, 0, tiled=True).reshape(4, 2, 4, 16, SIDE)
    return main, plane


def ring_along_z(plane):
    side = [plane]
    up = down = plane
    for _ in range(3):
        up = lax.ppermute(up, AXES, along_z(1))
        down = lax.ppermute(down, AXES, along_z(-1))
        side += [up, down]
    side += [lax.ppermute(up[:2], AXES, along_z(1)), lax.ppermute(down[2:], AXES, along_z(-1))]
    return side


def on_device(
    x_pre, x_dec, rec_hidden, norm_gain, w_query, key_value_weight, cache_pool, shared_kv,
    dec_len, dec_table, dec_group, prefix_len, pre_start, pre_table, rec_req, rec_off,
):
    core = lax.axis_index("c")
    place = lax.axis_index("zl") * 4 + lax.axis_index("y")
    lengths = dec_len[0]
    page_table = dec_table[0]
    groups = dec_group[0]
    prefix_line = prefix_len[0]
    request = rec_req[0]
    within = rec_off[0]

    main, plane = start_weights(w_query, key_value_weight)

    dec_pos = small_lookup(prefix_line, groups) + lengths
    parts = jnp.stack([dec_pos // 64, dec_pos % 64], axis=1).astype(bf16)
    extra = jnp.concatenate([x_dec, parts, jnp.zeros((DEC, 126), bf16)], axis=1)
    plane, extra = lax.optimization_barrier((plane, extra))
    side = ring_along_z(plane)
    line = lax.all_to_all(
        jnp.broadcast_to(extra[None], (16, DEC, MODEL + 128)), DP, 0, 0, tiled=True
    ).reshape(LINE, MODEL + 128)
    line_parts = line[:, MODEL : MODEL + 2].astype(jnp.int32)
    line_pos = line_parts[:, 0] * 64 + line_parts[:, 1]

    rows = jnp.concatenate([x_pre, line[:, :MODEL], rec_hidden], axis=0)
    normed = rms_scaled(rows, norm_gain)
    pre_pos = pre_start[0] + jnp.arange(PRE, dtype=jnp.int32)
    rec_pos = small_lookup(prefix_line, small_lookup(groups, request)) + within
    positions = jnp.concatenate([pre_pos, line_pos, rec_pos], axis=0)
    half_dim = HEAD_SIZE // 2
    frequency = theta_base ** (-jnp.arange(half_dim, dtype=f32) * 2.0 / HEAD_SIZE)
    angles = positions.astype(f32)[:, None] * frequency
    cosines = jnp.cos(angles)
    sines = jnp.sin(angles)
    table = jnp.concatenate([cosines, cosines, -sines, sines], axis=1)
    swap = [(0, 1), (1, 0)]
    other = lax.ppermute(normed, "c", swap)
    other_table = lax.ppermute(table, "c", swap)

    counts = (lengths + PAGE_TOKENS - 1) // PAGE_TOKENS
    ends = jnp.cumsum(counts)
    firsts = ends - counts
    slot = jnp.arange(DEC_SLOTS, dtype=jnp.int32)
    slot_request = jnp.sum((slot[:, None] >= ends[None, :]).astype(jnp.int32), axis=1)
    used = slot_request < DEC
    slot_request = jnp.minimum(slot_request, DEC - 1)
    slot_page = jnp.where(used, slot - small_lookup(firsts, slot_request), 0)
    dec_pages = small_lookup(page_table.reshape(-1), slot_request * page_table.shape[1] + slot_page)
    slots = jnp.concatenate([dec_pages, pre_table[0]], axis=0)
    key_pos = slot_page[:, None] * PAGE_TOKENS + jnp.arange(PAGE_TOKENS, dtype=jnp.int32)[None, :]
    valid = used[:, None] & (key_pos < small_lookup(lengths, slot_request)[:, None])
    rec_slot = small_lookup(firsts, request) + within // PAGE_TOKENS
    slot_hot = (rec_slot[None, :] == slot[:, None]).astype(bf16)
    token_hot = (within[:, None] % PAGE_TOKENS == jnp.arange(PAGE_TOKENS, dtype=jnp.int32)[None, :]).astype(bf16)
    replaced = jnp.dot(slot_hot, token_hot, preferred_element_type=f32) > 0.5
    kept = (valid & ~replaced).reshape(-1)
    eight = jnp.arange(8, dtype=jnp.int32) % DEC
    key_request = jnp.repeat(slot_request, PAGE_TOKENS)
    bias_private = jnp.where(kept[None, :] & (key_request[None, :] == eight[:, None]), 0.0, negative_large)
    new_request = jnp.concatenate(
        [jnp.full((PRE,), -1, jnp.int32), jnp.arange(LINE, dtype=jnp.int32) - place * DEC, request], axis=0
    )
    bias_new = jnp.where(new_request[None, :] == eight[:, None], 0.0, negative_large)
    own_prefix = small_lookup(prefix_line, place[None])[0]
    depth = lax.axis_index("zh") * 4 + lax.axis_index("zl")
    info = jnp.stack([core, own_prefix, pre_start[0], place, depth]).astype(jnp.int32)

    pages = take_pages(slots, cache_pool)
    main, pages, bias_private, bias_new, info = lax.optimization_barrier(
        (main, pages, bias_private, bias_new, info)
    )
    q_own, kv_own, packed = project(info, main, side, normed, other, table, other_table)
    packed = lax.ppermute(packed, "c", swap)
    shared_part = shared_attention(info, q_own, packed, shared_kv)
    shared_part = lax.all_to_all(shared_part, DP, 0, 0, tiled=True)
    out_pre, dec_part, dec_stat = local_attention(
        info, q_own, kv_own, packed, bias_private, bias_new, pages
    )
    out_dec = finish(groups, shared_part, dec_part, dec_stat)
    return (out_pre, out_dec)


def solution(mesh):
    split = Mesh(mesh.devices.reshape(2, 4, 2, 4, 4), AXES)
    first = P(AXES, None)
    second = P(AXES, None, None)
    return jax.shard_map(
        on_device,
        mesh=split,
        in_specs=(
            first, first, first, P(), first, first, second, first,
            first, second, first, P(("zh", "x", "c"), None), P(AXES), first, first, first,
        ),
        out_specs=(first, first),
        check_vma=False,
    )
```

```python
import functools

import jax
import jax.numpy as jnp
from jax import lax
from jax.experimental import pallas as pl
from jax.experimental.pallas import tpu as pltpu
from jax.sharding import Mesh
from jax.sharding import PartitionSpec as P

QUERY_HEADS = 16
KEY_VALUE_HEADS = 2
GROUP = QUERY_HEADS // KEY_VALUE_HEADS
HEAD_SIZE = 128
PAGE_TOKENS = 64
PRE = 128
DEC = 4
REC = 320
LINE = 64
ROWS = PRE + LINE + REC
QROWS = PRE + LINE
DEC_SLOTS = 68
HIST_SLOTS = 16
HALF = GROUP * HEAD_SIZE
WIDE = HALF + 2 * HEAD_SIZE
MODEL = 4096
SPAN = 512
STAT = QUERY_HEADS * HEAD_SIZE
MAIN = 896
SIDE = WIDE - MAIN
HEADS_AT_ONCE = 2
LOG2E = 1.4426950408889634

AXES = ("zh", "x", "c", "zl", "y")
DP = ("zl", "y")

theta_base = 5000000.0
epsilon = 1e-05
negative_large = -1e30
scale = HEAD_SIZE**-0.5

f32 = jnp.float32
bf16 = jnp.bfloat16
ANY = pl.BlockSpec(memory_space=pl.ANY)
VMEM = pl.BlockSpec(memory_space=pltpu.VMEM)
HBM = pl.BlockSpec(memory_space=pltpu.HBM)
SMEM = pl.BlockSpec(memory_space=pltpu.SMEM)


def dot_t(a, b):
    return lax.dot_general(a, b, (((1,), (1,)), ((), ())), preferred_element_type=f32)


def dot(a, b):
    return lax.dot_general(a, b, (((1,), (0,)), ((), ())), preferred_element_type=f32)


def turned(values, tab):
    return values * tab[:, :HEAD_SIZE] + pltpu.roll(values, HEAD_SIZE // 2, 1) * tab[:, HEAD_SIZE:]


def project_kernel(
    info, main_hbm, z0, up1, down1, up2, down2, up3, down3, up4, down4, x, tab_own, tab_oth,
    q_own, kv_own, packed, main, side, main_sem, side_sem,
):
    here = info[4]
    side_copies = []
    for i, (block, far) in enumerate(zip((z0, up1, down1, up2, down2, up3, down3), (0, -1, 1, -2, 2, -3, 3))):
        z = (here + far) & 7
        side_copies.append(pltpu.make_async_copy(block, side.at[z >> 2, :, :, z & 3], side_sem.at[i]))
    z = (here + 4) & 7
    side_copies.append(pltpu.make_async_copy(up4, side.at[z >> 2, 0:2, :, z & 3], side_sem.at[7]))
    side_copies.append(pltpu.make_async_copy(down4, side.at[z >> 2, 2:4, :, z & 3], side_sem.at[8]))
    groups = [(0, 512), (512, MAIN)]
    main_copies = []
    for k, (lo, hi) in enumerate(groups):
        for xi in range(4):
            for yi in range(4):
                main_copies.append(
                    pltpu.make_async_copy(
                        main_hbm.at[xi * 4 + yi, :, :, :, :, lo:hi],
                        main.at[:, xi, :, :, yi, :, lo:hi],
                        main_sem.at[k, xi * 4 + yi],
                    )
                )
    for copy in side_copies + main_copies:
        copy.start()
    for copy in side_copies:
        copy.wait()

    def store_queries(acc, first_head):
        for h in range(acc.shape[1] // HEAD_SIZE):
            at = slice((first_head + h) * HEAD_SIZE, (first_head + h + 1) * HEAD_SIZE)
            part = acc[:, h * HEAD_SIZE : (h + 1) * HEAD_SIZE]
            q_own[:, at] = turned(part[:QROWS], tab_own[0:QROWS, :]).astype(bf16)
            packed[0:QROWS, at] = turned(part[QROWS:], tab_oth[0:QROWS, :]).astype(bf16)

    side_flat = side.reshape(MODEL, SIDE)
    acc = dot(x[...], side_flat[:, SIDE - 256 :])
    for own in (True, False):
        tab = (tab_own if own else tab_oth)[...]
        first = acc[0:QROWS] if own else acc[QROWS : 2 * QROWS]
        rest = acc[2 * QROWS : 2 * QROWS + REC] if own else acc[2 * QROWS + REC :]
        both = jnp.concatenate([first, rest], axis=0)
        keys = turned(both[:, :HEAD_SIZE], tab).astype(bf16)
        values = both[:, HEAD_SIZE:].astype(bf16)
        if own:
            kv_own[:, :HEAD_SIZE] = keys
            kv_own[:, HEAD_SIZE:] = values
        else:
            for b in range(4):
                rows = slice(b * 128, (b + 1) * 128)
                packed[QROWS:, b * 256 : b * 256 + 128] = keys[rows]
                packed[QROWS:, b * 256 + 128 : (b + 1) * 256] = values[rows]
    store_queries(dot(x[0 : 2 * QROWS, :], side_flat[:, : SIDE - 256]), MAIN // HEAD_SIZE)
    main_flat = main.reshape(MODEL, MAIN)
    for k, (lo, hi) in enumerate(groups):
        for copy in main_copies[k * 16 : (k + 1) * 16]:
            copy.wait()
        for c0 in range(lo, hi, 256):
            c1 = min(c0 + 256, hi)
            store_queries(dot(x[0 : 2 * QROWS, :], main_flat[:, c0:c1]), c0 // HEAD_SIZE)


def project(info, main, side, rows, tab_own, tab_oth):
    return pl.pallas_call(
        project_kernel,
        name="project",
        out_shape=(
            jax.ShapeDtypeStruct((QROWS, HALF), bf16),
            jax.ShapeDtypeStruct((ROWS, 2 * HEAD_SIZE), bf16),
            jax.ShapeDtypeStruct((QROWS + 128, HALF), bf16),
        ),
        in_specs=[SMEM] + [ANY] * 10 + [VMEM] * 3,
        out_specs=(VMEM, VMEM, VMEM),
        scratch_shapes=[
            pltpu.VMEM((2, 4, 2, 4, 4, 16, MAIN), bf16),
            pltpu.VMEM((2, 4, 2, 4, 4, 16, SIDE), bf16),
            pltpu.SemaphoreType.DMA((2, 16)),
            pltpu.SemaphoreType.DMA((9,)),
        ],
        compiler_params=pltpu.CompilerParams(vmem_limit_bytes=46 << 20),
        cost_estimate=pl.CostEstimate(flops=6 * 10**9, bytes_accessed=20 * 10**6, transcendentals=0),
    )(info, main, *side, rows, tab_own, tab_oth)


def shared_kernel(info, q_own, packed, kv, out, qs):
    core = info[0]
    qs[core] = q_own[PRE:QROWS, :]
    qs[1 - core] = packed[PRE:QROWS, :]
    limit = info[1]
    bias = jnp.where(lax.broadcasted_iota(jnp.int32, (1, SPAN), 1) < limit, 0.0, negative_large)
    lane = lax.broadcasted_iota(jnp.int32, (LINE, HEAD_SIZE), 1)
    stats = jnp.zeros((LINE, HEAD_SIZE), f32)
    ones = jnp.ones((SPAN, HEAD_SIZE), bf16)
    c2 = scale*LOG2E
    for s in range(KEY_VALUE_HEADS):
        keys = kv[:, s * HEAD_SIZE : (s + 1) * HEAD_SIZE]
        values = jnp.concatenate([kv[:, (2 + s) * HEAD_SIZE : (3 + s) * HEAD_SIZE], ones], axis=1)
        query = jnp.concatenate([qs[s, :, h * HEAD_SIZE : (h + 1) * HEAD_SIZE] for h in range(GROUP)], axis=0)
        scores = dot_t(query, keys) + bias
        top = jnp.max(scores, axis=-1, keepdims=True)
        weights = jnp.exp2((scores - top) * c2)
        result = dot(weights.astype(bf16), values)
        total = result[:, HEAD_SIZE:]
        done = result[:, :HEAD_SIZE] / total
        level = top * scale + jnp.log(total)
        for h in range(GROUP):
            head = s * GROUP + h
            out[:, :, head * HEAD_SIZE : (head + 1) * HEAD_SIZE] = done[h*LINE:(h+1)*LINE].reshape(16,4,HEAD_SIZE).astype(bf16)
            stats = jnp.where(lane == head, level[h*LINE:(h+1)*LINE], stats)
    high = stats.astype(bf16).astype(f32)
    left = stats - high
    middle = left.astype(bf16).astype(f32)
    low = left - middle
    parts = high + pltpu.roll(middle, QUERY_HEADS, 1) + pltpu.roll(low, 2 * QUERY_HEADS, 1)
    out[:, :, STAT:] = parts.reshape(16, 4, HEAD_SIZE).astype(bf16)
def shared_attention(info, q_own, packed, kv):
    return pl.pallas_call(shared_kernel, name="shared", out_shape=jax.ShapeDtypeStruct((16, 4, STAT + 128), bf16),
        in_specs=[SMEM, VMEM, VMEM, VMEM], out_specs=VMEM, scratch_shapes=[pltpu.VMEM((2, LINE, HALF), bf16)],
        compiler_params=pltpu.CompilerParams(vmem_limit_bytes=16 << 20),
        cost_estimate=pl.CostEstimate(flops=3 * 10**8, bytes_accessed=10**6, transcendentals=10**6))(info, q_own, packed, kv)


def pages_kernel(slots, pool, pages, held, sems, out_sem):
    copies = [
        pltpu.make_async_copy(pool.at[slots[i]], held.at[i], sems.at[i]) for i in range(DEC_SLOTS + HIST_SLOTS)
    ]
    for copy in copies:
        copy.start()
    for copy in copies:
        copy.wait()
    out = pltpu.make_async_copy(held, pages, out_sem)
    out.start()
    out.wait()


def take_pages(slots, pool):
    shape = (DEC_SLOTS + HIST_SLOTS, PAGE_TOKENS, 4 * HEAD_SIZE)
    return pl.pallas_call(
        pages_kernel,
        name="take_pages",
        out_shape=jax.ShapeDtypeStruct(shape, bf16),
        in_specs=[SMEM, HBM],
        out_specs=HBM,
        scratch_shapes=[
            pltpu.VMEM(shape, bf16),
            pltpu.SemaphoreType.DMA((DEC_SLOTS + HIST_SLOTS,)),
            pltpu.SemaphoreType.DMA,
        ],
        compiler_params=pltpu.CompilerParams(vmem_limit_bytes=12 << 20),
        cost_estimate=pl.CostEstimate(flops=0, bytes_accessed=22 * 10**6, transcendentals=0),
    )(slots, pool)


def local_kernel(info, q_own, kv_own, packed, bias_private, bias_new, pages_hbm, out_pre, out_dec, stat_dec, qs, ks, pages, sems):
    old = pltpu.make_async_copy(pages_hbm.at[DEC_SLOTS:], pages.at[DEC_SLOTS:], sems.at[0])
    old.start()
    cached = pltpu.make_async_copy(pages_hbm.at[:DEC_SLOTS], pages.at[:DEC_SLOTS], sems.at[1])
    cached.start()
    core = info[0]; start = info[2]; place = info[3]
    q_copy = pltpu.make_async_copy(q_own, qs.at[core], sems.at[2])
    q_copy.start()
    kv_copy = pltpu.make_async_copy(kv_own, ks.at[core], sems.at[3])
    kv_copy.start()
    qs[1 - core] = packed[0:QROWS, :]
    for b in range(4):
        ks[1 - core, b * 128 : (b + 1) * 128, :] = packed[QROWS:, b * 256 : (b + 1) * 256]
    history = HIST_SLOTS * PAGE_TOKENS
    seen = jnp.where(lax.broadcasted_iota(jnp.int32, (1, history), 1) < start, 0.0, negative_large)
    rows = lax.broadcasted_iota(jnp.int32, (PRE, PRE), 0)
    cols = lax.broadcasted_iota(jnp.int32, (PRE, PRE), 1)
    causal = jnp.where(cols <= rows, 0.0, negative_large)
    causal = jnp.concatenate([causal]*HEADS_AT_ONCE, axis=0)
    c2 = scale*LOG2E
    ones_h = jnp.ones((history, HEAD_SIZE), bf16)
    ones_n = jnp.ones((PRE, HEAD_SIZE), bf16)
    q_copy.wait()
    kv_copy.wait()
    old.wait()
    for s in range(KEY_VALUE_HEADS):
        old_keys = pages[DEC_SLOTS:, :, s * HEAD_SIZE : (s + 1) * HEAD_SIZE].reshape(history, HEAD_SIZE)
        old_values = pages[DEC_SLOTS:, :, (2 + s) * HEAD_SIZE : (3 + s) * HEAD_SIZE].reshape(history, HEAD_SIZE)
        old_values = jnp.concatenate([old_values, ones_h], axis=1)
        new_keys = ks[s, 0:PRE, 0:HEAD_SIZE]
        new_values = jnp.concatenate([ks[s, 0:PRE, HEAD_SIZE:], ones_n], axis=1)
        for h in range(0, GROUP, HEADS_AT_ONCE):
            query = jnp.concatenate([qs[s, 0:PRE, (h+j) * HEAD_SIZE : (h+j + 1) * HEAD_SIZE] for j in range(HEADS_AT_ONCE)], axis=0)
            first = dot_t(query, old_keys) + seen
            second = dot_t(query, new_keys) + causal
            top = jnp.maximum(jnp.max(first, axis=-1, keepdims=True), jnp.max(second, axis=-1, keepdims=True))
            first = jnp.exp2((first - top) * c2)
            second = jnp.exp2((second - top) * c2)
            result = dot(first.astype(bf16), old_values) + dot(second.astype(bf16), new_values)
            done = (result[:, :HEAD_SIZE] / result[:, HEAD_SIZE:]).astype(bf16)
            for j in range(HEADS_AT_ONCE):
                head = s * GROUP + h + j
                out_pre[:, head * HEAD_SIZE : (head + 1) * HEAD_SIZE] = done[j*PRE:(j+1)*PRE]
    private = DEC_SLOTS * PAGE_TOKENS
    R = GROUP*DEC
    row = lax.broadcasted_iota(jnp.int32, (R, GROUP*LINE), 0)
    col = lax.broadcasted_iota(jnp.int32, (R, GROUP*LINE), 1)
    pick = (row >> 2 == col >> 6) & ((col & 63) == place * DEC + (row & 3))
    pick = jnp.where(pick, 1.0, 0.0).astype(bf16)
    cached.wait()
    for s in range(KEY_VALUE_HEADS):
        old_keys = pages[:DEC_SLOTS, :, s * HEAD_SIZE : (s + 1) * HEAD_SIZE].reshape(private, HEAD_SIZE)
        old_values = pages[:DEC_SLOTS, :, (2 + s) * HEAD_SIZE : (3 + s) * HEAD_SIZE].reshape(private, HEAD_SIZE)
        new_keys = ks[s, :, 0:HEAD_SIZE]
        new_values = ks[s, :, HEAD_SIZE:]
        line = jnp.concatenate([qs[s, PRE:QROWS, h * HEAD_SIZE : (h + 1) * HEAD_SIZE] for h in range(GROUP)], axis=0)
        query = dot(pick, line).astype(bf16)
        first = (dot_t(query, old_keys).reshape(R//8, 8, private) + bias_private[...][None]).reshape(R, private)
        second = (dot_t(query, new_keys).reshape(R//8, 8, ROWS) + bias_new[...][None]).reshape(R, ROWS)
        top = jnp.maximum(jnp.max(first, axis=-1, keepdims=True), jnp.max(second, axis=-1, keepdims=True))
        first = jnp.exp2((first - top) * c2)
        second = jnp.exp2((second - top) * c2)
        total = jnp.sum(first, axis=-1, keepdims=True) + jnp.sum(second, axis=-1, keepdims=True)
        result = dot(first.astype(bf16), old_values) + dot(second.astype(bf16), new_values)
        out_dec[s*R:(s+1)*R, :] = result / total
        stat_dec[s*R:(s+1)*R, :] = jnp.broadcast_to(top * scale + jnp.log(total), (R, HEAD_SIZE))

def local_attention(info, q_own, kv_own, packed, bias_private, bias_new, pages):
    return pl.pallas_call(
        local_kernel, name="local",
        out_shape=(jax.ShapeDtypeStruct((PRE, QUERY_HEADS * HEAD_SIZE), bf16), jax.ShapeDtypeStruct((64, HEAD_SIZE), f32), jax.ShapeDtypeStruct((64, HEAD_SIZE), f32)),
        in_specs=[SMEM, ANY, ANY, VMEM, VMEM, VMEM, HBM], out_specs=(VMEM, VMEM, VMEM),
        scratch_shapes=[pltpu.VMEM((2, QROWS, HALF), bf16), pltpu.VMEM((2, ROWS, 2 * HEAD_SIZE), bf16), pltpu.VMEM((DEC_SLOTS + HIST_SLOTS, PAGE_TOKENS, 4 * HEAD_SIZE), bf16), pltpu.SemaphoreType.DMA((4,))],
        compiler_params=pltpu.CompilerParams(vmem_limit_bytes=48 << 20),
        cost_estimate=pl.CostEstimate(flops=10**10, bytes_accessed=8 * 10**6, transcendentals=3 * 10**6),
    )(info, q_own, kv_own, packed, bias_private, bias_new, pages)


def finish_kernel(groups, shared, local, local_stat, out):
    row = lax.broadcasted_iota(jnp.int32, (DEC, STAT + 128), 0)
    chosen = jnp.zeros((DEC, STAT + 128), f32)
    for r in range(DEC):
        chosen = jnp.where(row == r, shared[groups[r]].astype(f32), chosen)
    for head in range(QUERY_HEADS):
        rows = slice(head*DEC,(head+1)*DEC)
        at = slice(head * HEAD_SIZE, (head + 1) * HEAD_SIZE)
        at_stat = STAT + head
        far = (
            chosen[:, at_stat : at_stat + 1]
            + chosen[:, at_stat + QUERY_HEADS : at_stat + QUERY_HEADS + 1]
            + chosen[:, at_stat + 2 * QUERY_HEADS : at_stat + 2 * QUERY_HEADS + 1]
        )
        near = local_stat[rows, 0:1]
        top = jnp.maximum(far, near)
        far = jnp.exp(far - top); near = jnp.exp(near - top)
        whole = far + near
        out[:, at] = (chosen[:, at] * (far/whole) + local[rows, :] * (near/whole)).astype(bf16)
def finish(groups, shared, local, local_stat):
    return pl.pallas_call(finish_kernel, name="finish", out_shape=jax.ShapeDtypeStruct((DEC, QUERY_HEADS * HEAD_SIZE), bf16),
        in_specs=[SMEM, VMEM, VMEM, VMEM], out_specs=VMEM, compiler_params=pltpu.CompilerParams(vmem_limit_bytes=8 << 20))(groups, shared, local, local_stat)


def small_lookup(entries, indices):
    matches = indices[..., None] == jnp.arange(entries.shape[0], dtype=jnp.int32)
    return jnp.sum(jnp.where(matches, entries, 0), axis=-1)


def rms_scaled(values, gain):
    widened = values.astype(f32)
    factor = lax.rsqrt(jnp.mean(widened * widened, axis=-1, keepdims=True) + epsilon)
    return (widened * factor * gain.astype(f32)).astype(bf16)


def along_z(step):
    pairs = []
    for i in range(256):
        z = (i // 128) * 4 + (i // 4) % 4
        to = (z + step) % 8
        pairs.append((i, i % 128 - (i // 4) % 4 * 4 + (to // 4) * 128 + (to % 4) * 4))
    return pairs


def weight_block(w_query, key_value_weight):
    key_half = key_value_weight.reshape(16, 2, 2, HEAD_SIZE)
    halves = [
        jnp.concatenate([w_query[:, c * HALF : (c + 1) * HALF], key_half[:, 0, c], key_half[:, 1, c]], axis=1)
        for c in range(2)
    ]
    return jnp.stack(halves, axis=0)


def main_column(block):
    sent = jnp.broadcast_to(block[None, :, None], (2, 2, 4, 16, MAIN)).reshape(16, 16, MAIN)
    return lax.all_to_all(sent, ("zh", "c", "zl"), 0, 0, tiled=True)


def side_plane(block):
    sent = jnp.broadcast_to(block[None, :, None], (4, 2, 4, 16, SIDE)).reshape(32, 16, SIDE)
    return lax.all_to_all(sent, ("x", "c", "y"), 0, 0, tiled=True).reshape(4, 2, 4, 16, SIDE)


def ring_step(up, down):
    return lax.ppermute(up, AXES, along_z(1)), lax.ppermute(down, AXES, along_z(-1))


def on_device(
    x_pre, x_dec, rec_hidden, norm_gain, w_query, key_value_weight, cache_pool, shared_kv,
    dec_len, dec_table, dec_group, prefix_len, pre_start, pre_table, rec_req, rec_off,
):
    core = lax.axis_index("c")
    place = lax.axis_index("zl") * 4 + lax.axis_index("y")
    lengths = dec_len[0]
    page_table = dec_table[0]
    groups = dec_group[0]
    prefix_line = prefix_len[0]
    request = rec_req[0]
    within = rec_off[0]

    block = weight_block(w_query, key_value_weight)
    column = main_column(block[:, :, :MAIN])
    rest, column = lax.optimization_barrier((block[:, :, MAIN:], column))
    main = lax.all_gather(column.reshape(256, MAIN), ("x", "y"), axis=0, tiled=True)
    main = main.reshape(16, 2, 2, 4, 16, MAIN)

    dec_pos = small_lookup(prefix_line, groups) + lengths
    parts = jnp.stack([dec_pos // 64, dec_pos % 64], axis=1).astype(bf16)
    extra = jnp.concatenate([x_dec, parts, jnp.zeros((DEC, 126), bf16)], axis=1)
    normed_pre = rms_scaled(x_pre, norm_gain)
    normed_rec = rms_scaled(rec_hidden, norm_gain)

    counts = (lengths + PAGE_TOKENS - 1) // PAGE_TOKENS
    ends = jnp.cumsum(counts)
    firsts = ends - counts
    slot = jnp.arange(DEC_SLOTS, dtype=jnp.int32)
    slot_request = jnp.sum((slot[:, None] >= ends[None, :]).astype(jnp.int32), axis=1)
    used = slot_request < DEC
    slot_request = jnp.minimum(slot_request, DEC - 1)
    slot_page = jnp.where(used, slot - small_lookup(firsts, slot_request), 0)
    dec_pages = small_lookup(page_table.reshape(-1), slot_request * page_table.shape[1] + slot_page)
    slots = jnp.concatenate([dec_pages, pre_table[0]], axis=0)

    rest, normed_pre, slots = lax.optimization_barrier((rest, normed_pre, slots))
    plane = side_plane(rest)
    pages = take_pages(slots, cache_pool)
    plane, pages = lax.optimization_barrier((plane, pages))
    up1, down1 = ring_step(plane, plane)
    up1, down1, extra = lax.optimization_barrier((up1, down1, extra))
    line = lax.all_to_all(
        jnp.broadcast_to(extra[None], (16, DEC, MODEL + 128)), DP, 0, 0, tiled=True
    ).reshape(LINE, MODEL + 128)
    up2, down2 = ring_step(up1, down1)
    up2, down2, line = lax.optimization_barrier((up2, down2, line))
    line_parts = line[:, MODEL : MODEL + 2].astype(jnp.int32)
    line_pos = line_parts[:, 0] * 64 + line_parts[:, 1]
    normed_line = rms_scaled(line[:, :MODEL], norm_gain)
    up3, down3 = ring_step(up2, down2)
    up3, down3, normed_line = lax.optimization_barrier((up3, down3, normed_line))
    up4, down4 = ring_step(up3[:2], down3[2:])
    side = (plane, up1, down1, up2, down2, up3, down3, up4, down4)

    pre_pos = pre_start[0] + jnp.arange(PRE, dtype=jnp.int32)
    rec_pos = small_lookup(prefix_line, small_lookup(groups, request)) + within
    positions = jnp.concatenate([pre_pos, line_pos, rec_pos], axis=0)
    half_dim = HEAD_SIZE // 2
    frequency = theta_base ** (-jnp.arange(half_dim, dtype=f32) * 2.0 / HEAD_SIZE)
    angles = positions.astype(f32)[:, None] * frequency
    cosines = jnp.cos(angles)
    sines = jnp.sin(angles)
    table = jnp.concatenate([cosines, cosines, -sines, sines], axis=1)
    swap = [(0, 1), (1, 0)]
    own = (normed_pre, normed_line, normed_rec)
    other = [lax.ppermute(v, "c", swap) for v in own]
    other_table = lax.ppermute(table, "c", swap)
    rows = jnp.concatenate([own[0], own[1], other[0], other[1], own[2], other[2]], axis=0)

    key_pos = slot_page[:, None] * PAGE_TOKENS + jnp.arange(PAGE_TOKENS, dtype=jnp.int32)[None, :]
    valid = used[:, None] & (key_pos < small_lookup(lengths, slot_request)[:, None])
    rec_slot = small_lookup(firsts, request) + within // PAGE_TOKENS
    slot_hot = (rec_slot[None, :] == slot[:, None]).astype(bf16)
    token_hot = (within[:, None] % PAGE_TOKENS == jnp.arange(PAGE_TOKENS, dtype=jnp.int32)[None, :]).astype(bf16)
    replaced = jnp.dot(slot_hot, token_hot, preferred_element_type=f32) > 0.5
    kept = (valid & ~replaced).reshape(-1)
    eight = jnp.arange(8, dtype=jnp.int32) % DEC
    key_request = jnp.repeat(slot_request, PAGE_TOKENS)
    bias_private = jnp.where(kept[None, :] & (key_request[None, :] == eight[:, None]), 0.0, negative_large)
    new_request = jnp.concatenate(
        [jnp.full((PRE,), -1, jnp.int32), jnp.arange(LINE, dtype=jnp.int32) - place * DEC, request], axis=0
    )
    bias_new = jnp.where(new_request[None, :] == eight[:, None], 0.0, negative_large)
    own_prefix = small_lookup(prefix_line, place[None])[0]
    depth = lax.axis_index("zh") * 4 + lax.axis_index("zl")
    info = jnp.stack([core, own_prefix, pre_start[0], place, depth]).astype(jnp.int32)

    main, rows, table, other_table, bias_private, bias_new, info = lax.optimization_barrier(
        (main, rows, table, other_table, bias_private, bias_new, info)
    )
    q_own, kv_own, packed = project(info, main, side, rows, table, other_table)
    packed = lax.ppermute(packed, "c", swap)
    shared_part = shared_attention(info, q_own, packed, shared_kv)
    shared_part = lax.all_to_all(shared_part, DP, 0, 0, tiled=True)
    out_pre, dec_part, dec_stat = local_attention(
        info, q_own, kv_own, packed, bias_private, bias_new, pages
    )
    out_dec = finish(groups, shared_part, dec_part, dec_stat)
    return (out_pre, out_dec)


def solution(mesh):
    split = Mesh(mesh.devices.reshape(2, 4, 2, 4, 4), AXES)
    first = P(AXES, None)
    second = P(AXES, None, None)
    return jax.shard_map(
        on_device,
        mesh=split,
        in_specs=(
            first, first, first, P(), first, first, second, first,
            first, second, first, P(("zh", "x", "c"), None), P(AXES), first, first, first,
        ),
        out_specs=(first, first),
        check_vma=False,
    )
```

```python
import functools

import jax
import jax.numpy as jnp
from jax import lax
from jax.experimental import pallas as pl
from jax.experimental.pallas import tpu as pltpu
from jax.sharding import Mesh
from jax.sharding import PartitionSpec as P

QUERY_HEADS = 16
KEY_VALUE_HEADS = 2
GROUP = QUERY_HEADS // KEY_VALUE_HEADS
HEAD_SIZE = 128
PAGE_TOKENS = 64
PRE = 128
DEC = 4
REC = 320
LINE = 64
ROWS = PRE + LINE + REC
QROWS = PRE + LINE
DEC_SLOTS = 68
HIST_SLOTS = 16
HALF = GROUP * HEAD_SIZE
WIDE = HALF + 2 * HEAD_SIZE
MODEL = 4096
SPAN = 512
STAT = QUERY_HEADS * HEAD_SIZE
SPLIT = 512
HEADS_AT_ONCE = 2
LOG2E = 1.4426950408889634

AXES = ("zh", "x", "c", "zl", "y")
DP = ("zl", "y")

theta_base = 5000000.0
epsilon = 1e-05
negative_large = -1e30
scale = HEAD_SIZE**-0.5

f32 = jnp.float32
bf16 = jnp.bfloat16
ANY = pl.BlockSpec(memory_space=pl.ANY)
VMEM = pl.BlockSpec(memory_space=pltpu.VMEM)
HBM = pl.BlockSpec(memory_space=pltpu.HBM)
SMEM = pl.BlockSpec(memory_space=pltpu.SMEM)


def dot_t(a, b):
    return lax.dot_general(a, b, (((1,), (1,)), ((), ())), preferred_element_type=f32)


def dot(a, b):
    return lax.dot_general(a, b, (((1,), (0,)), ((), ())), preferred_element_type=f32)


def turned(values, tab):
    return values * tab[:, :HEAD_SIZE] + pltpu.roll(values, HEAD_SIZE // 2, 1) * tab[:, HEAD_SIZE:]

def project_kernel(w_hbm, x, tab_own, tab_oth, q_own, kv_own, packed, w, w_sem):
    groups = [(0, SPLIT), (SPLIT, WIDE)]
    pieces=[]
    for k,(lo,hi) in enumerate(groups):
        for xi in range(4):
            for yi in range(4):
                pieces.append(pltpu.make_async_copy(w_hbm.at[xi*4+yi, :, :, :, :, lo:hi], w.at[:, xi, :, :, yi, :, lo:hi], w_sem.at[k, xi*4+yi]))
    for copy in pieces: copy.start()
    wf = w.reshape(MODEL, WIDE)
    for k,(lo,hi) in enumerate(groups):
        for copy in pieces[k*16:(k+1)*16]: copy.wait()
        for c0 in range(lo,hi,256):
            cols=slice(c0,c0+256)
            if c0<HALF:
                acc = dot(x[0:2*QROWS, :], wf[:, cols])
                for h in range(2):
                    at = slice(c0 + h * HEAD_SIZE, c0 + (h + 1) * HEAD_SIZE)
                    part = acc[:, h * HEAD_SIZE : (h + 1) * HEAD_SIZE]
                    q_own[:, at] = turned(part[:QROWS], tab_own[0:QROWS,:]).astype(bf16)
                    packed[0:QROWS, at] = turned(part[QROWS:], tab_oth[0:QROWS,:]).astype(bf16)
            else:
                acc = dot(x[...], wf[:, cols])
                for own in (True, False):
                    tab = (tab_own if own else tab_oth)[...]
                    first = acc[0:QROWS] if own else acc[QROWS : 2 * QROWS]
                    rest = acc[2 * QROWS : 2 * QROWS + REC] if own else acc[2 * QROWS + REC :]
                    both = jnp.concatenate([first, rest], axis=0)
                    keys = turned(both[:, :HEAD_SIZE], tab).astype(bf16)
                    values = both[:, HEAD_SIZE:].astype(bf16)
                    if own:
                        kv_own[:, :HEAD_SIZE] = keys
                        kv_own[:, HEAD_SIZE:] = values
                    else:
                        for b in range(4):
                            rows = slice(b * 128, (b + 1) * 128)
                            packed[QROWS:, b * 256 : b * 256 + 128] = keys[rows]
                            packed[QROWS:, b * 256 + 128 : (b + 1) * 256] = values[rows]

def project(weights, rows, tab_own, tab_oth):
    return pl.pallas_call(
        project_kernel, name="project",
        out_shape=(jax.ShapeDtypeStruct((QROWS, HALF), bf16), jax.ShapeDtypeStruct((ROWS, 2 * HEAD_SIZE), bf16), jax.ShapeDtypeStruct((QROWS + 128, HALF), bf16)),
        in_specs=[ANY, VMEM, VMEM, VMEM], out_specs=(VMEM, VMEM, VMEM),
        scratch_shapes=[pltpu.VMEM((2, 4, 2, 4, 4, 16, WIDE), bf16),
            pltpu.SemaphoreType.DMA((2, 16))],
        compiler_params=pltpu.CompilerParams(vmem_limit_bytes=44 << 20),
        cost_estimate=pl.CostEstimate(flops=6 * 10**9, bytes_accessed=20 * 10**6, transcendentals=0),
    )(weights, rows, tab_own, tab_oth)


def shared_kernel(info, q_own, packed, kv, out, qs):
    core = info[0]
    qs[core] = q_own[PRE:QROWS, :]
    qs[1 - core] = packed[PRE:QROWS, :]
    limit = info[1]
    bias = jnp.where(lax.broadcasted_iota(jnp.int32, (1, SPAN), 1) < limit, 0.0, negative_large)
    lane = lax.broadcasted_iota(jnp.int32, (LINE, HEAD_SIZE), 1)
    stats = jnp.zeros((LINE, HEAD_SIZE), f32)
    ones = jnp.ones((SPAN, HEAD_SIZE), bf16)
    c2 = scale*LOG2E
    for s in range(KEY_VALUE_HEADS):
        keys = kv[:, s * HEAD_SIZE : (s + 1) * HEAD_SIZE]
        values = jnp.concatenate([kv[:, (2 + s) * HEAD_SIZE : (3 + s) * HEAD_SIZE], ones], axis=1)
        query = jnp.concatenate([qs[s, :, h * HEAD_SIZE : (h + 1) * HEAD_SIZE] for h in range(GROUP)], axis=0)
        scores = dot_t(query, keys) + bias
        top = jnp.max(scores, axis=-1, keepdims=True)
        weights = jnp.exp2((scores - top) * c2)
        result = dot(weights.astype(bf16), values)
        total = result[:, HEAD_SIZE:]
        done = result[:, :HEAD_SIZE] / total
        level = top * scale + jnp.log(total)
        for h in range(GROUP):
            head = s * GROUP + h
            out[:, :, head * HEAD_SIZE : (head + 1) * HEAD_SIZE] = done[h*LINE:(h+1)*LINE].reshape(16,4,HEAD_SIZE).astype(bf16)
            stats = jnp.where(lane == head, level[h*LINE:(h+1)*LINE], stats)
    high = stats.astype(bf16).astype(f32)
    left = stats - high
    middle = left.astype(bf16).astype(f32)
    low = left - middle
    parts = high + pltpu.roll(middle, QUERY_HEADS, 1) + pltpu.roll(low, 2 * QUERY_HEADS, 1)
    out[:, :, STAT:] = parts.reshape(16, 4, HEAD_SIZE).astype(bf16)
def shared_attention(info, q_own, packed, kv):
    return pl.pallas_call(shared_kernel, name="shared", out_shape=jax.ShapeDtypeStruct((16, 4, STAT + 128), bf16),
        in_specs=[SMEM, VMEM, VMEM, VMEM], out_specs=VMEM, scratch_shapes=[pltpu.VMEM((2, LINE, HALF), bf16)],
        compiler_params=pltpu.CompilerParams(vmem_limit_bytes=16 << 20),
        cost_estimate=pl.CostEstimate(flops=3 * 10**8, bytes_accessed=10**6, transcendentals=10**6))(info, q_own, packed, kv)


def pages_kernel(slots, pool, pages, held, sems, out_sem):
    copies = [
        pltpu.make_async_copy(pool.at[slots[i]], held.at[i], sems.at[i]) for i in range(DEC_SLOTS + HIST_SLOTS)
    ]
    for copy in copies:
        copy.start()
    for copy in copies:
        copy.wait()
    out = pltpu.make_async_copy(held, pages, out_sem)
    out.start()
    out.wait()


def take_pages(slots, pool):
    shape = (DEC_SLOTS + HIST_SLOTS, PAGE_TOKENS, 4 * HEAD_SIZE)
    return pl.pallas_call(
        pages_kernel,
        name="take_pages",
        out_shape=jax.ShapeDtypeStruct(shape, bf16),
        in_specs=[SMEM, HBM],
        out_specs=HBM,
        scratch_shapes=[
            pltpu.VMEM(shape, bf16),
            pltpu.SemaphoreType.DMA((DEC_SLOTS + HIST_SLOTS,)),
            pltpu.SemaphoreType.DMA,
        ],
        compiler_params=pltpu.CompilerParams(vmem_limit_bytes=12 << 20),
        cost_estimate=pl.CostEstimate(flops=0, bytes_accessed=22 * 10**6, transcendentals=0),
    )(slots, pool)


def local_kernel(info, q_own, kv_own, packed, bias_private, bias_new, pages_hbm, out_pre, out_dec, stat_dec, qs, ks, pages, sems):
    old = pltpu.make_async_copy(pages_hbm.at[DEC_SLOTS:], pages.at[DEC_SLOTS:], sems.at[0])
    old.start()
    cached = pltpu.make_async_copy(pages_hbm.at[:DEC_SLOTS], pages.at[:DEC_SLOTS], sems.at[1])
    cached.start()
    core = info[0]; start = info[2]; place = info[3]
    q_copy = pltpu.make_async_copy(q_own, qs.at[core], sems.at[2])
    q_copy.start()
    kv_copy = pltpu.make_async_copy(kv_own, ks.at[core], sems.at[3])
    kv_copy.start()
    qs[1 - core] = packed[0:QROWS, :]
    for b in range(4):
        ks[1 - core, b * 128 : (b + 1) * 128, :] = packed[QROWS:, b * 256 : (b + 1) * 256]
    history = HIST_SLOTS * PAGE_TOKENS
    seen = jnp.where(lax.broadcasted_iota(jnp.int32, (1, history), 1) < start, 0.0, negative_large)
    rows = lax.broadcasted_iota(jnp.int32, (PRE, PRE), 0)
    cols = lax.broadcasted_iota(jnp.int32, (PRE, PRE), 1)
    causal = jnp.where(cols <= rows, 0.0, negative_large)
    causal = jnp.concatenate([causal]*HEADS_AT_ONCE, axis=0)
    c2 = scale*LOG2E
    ones_h = jnp.ones((history, HEAD_SIZE), bf16)
    ones_n = jnp.ones((PRE, HEAD_SIZE), bf16)
    q_copy.wait()
    kv_copy.wait()
    old.wait()
    for s in range(KEY_VALUE_HEADS):
        old_keys = pages[DEC_SLOTS:, :, s * HEAD_SIZE : (s + 1) * HEAD_SIZE].reshape(history, HEAD_SIZE)
        old_values = pages[DEC_SLOTS:, :, (2 + s) * HEAD_SIZE : (3 + s) * HEAD_SIZE].reshape(history, HEAD_SIZE)
        old_values = jnp.concatenate([old_values, ones_h], axis=1)
        new_keys = ks[s, 0:PRE, 0:HEAD_SIZE]
        new_values = jnp.concatenate([ks[s, 0:PRE, HEAD_SIZE:], ones_n], axis=1)
        for h in range(0, GROUP, HEADS_AT_ONCE):
            query = jnp.concatenate([qs[s, 0:PRE, (h+j) * HEAD_SIZE : (h+j + 1) * HEAD_SIZE] for j in range(HEADS_AT_ONCE)], axis=0)
            first = dot_t(query, old_keys) + seen
            second = dot_t(query, new_keys) + causal
            top = jnp.maximum(jnp.max(first, axis=-1, keepdims=True), jnp.max(second, axis=-1, keepdims=True))
            first = jnp.exp2((first - top) * c2)
            second = jnp.exp2((second - top) * c2)
            result = dot(first.astype(bf16), old_values) + dot(second.astype(bf16), new_values)
            done = (result[:, :HEAD_SIZE] / result[:, HEAD_SIZE:]).astype(bf16)
            for j in range(HEADS_AT_ONCE):
                head = s * GROUP + h + j
                out_pre[:, head * HEAD_SIZE : (head + 1) * HEAD_SIZE] = done[j*PRE:(j+1)*PRE]
    private = DEC_SLOTS * PAGE_TOKENS
    R = GROUP*DEC
    row = lax.broadcasted_iota(jnp.int32, (R, GROUP*LINE), 0)
    col = lax.broadcasted_iota(jnp.int32, (R, GROUP*LINE), 1)
    pick = (row >> 2 == col >> 6) & ((col & 63) == place * DEC + (row & 3))
    pick = jnp.where(pick, 1.0, 0.0).astype(bf16)
    cached.wait()
    for s in range(KEY_VALUE_HEADS):
        old_keys = pages[:DEC_SLOTS, :, s * HEAD_SIZE : (s + 1) * HEAD_SIZE].reshape(private, HEAD_SIZE)
        old_values = pages[:DEC_SLOTS, :, (2 + s) * HEAD_SIZE : (3 + s) * HEAD_SIZE].reshape(private, HEAD_SIZE)
        new_keys = ks[s, :, 0:HEAD_SIZE]
        new_values = ks[s, :, HEAD_SIZE:]
        line = jnp.concatenate([qs[s, PRE:QROWS, h * HEAD_SIZE : (h + 1) * HEAD_SIZE] for h in range(GROUP)], axis=0)
        query = dot(pick, line).astype(bf16)
        first = (dot_t(query, old_keys).reshape(R//8, 8, private) + bias_private[...][None]).reshape(R, private)
        second = (dot_t(query, new_keys).reshape(R//8, 8, ROWS) + bias_new[...][None]).reshape(R, ROWS)
        top = jnp.maximum(jnp.max(first, axis=-1, keepdims=True), jnp.max(second, axis=-1, keepdims=True))
        first = jnp.exp2((first - top) * c2)
        second = jnp.exp2((second - top) * c2)
        total = jnp.sum(first, axis=-1, keepdims=True) + jnp.sum(second, axis=-1, keepdims=True)
        result = dot(first.astype(bf16), old_values) + dot(second.astype(bf16), new_values)
        out_dec[s*R:(s+1)*R, :] = result / total
        stat_dec[s*R:(s+1)*R, :] = jnp.broadcast_to(top * scale + jnp.log(total), (R, HEAD_SIZE))

def local_attention(info, q_own, kv_own, packed, bias_private, bias_new, pages):
    return pl.pallas_call(
        local_kernel, name="local",
        out_shape=(jax.ShapeDtypeStruct((PRE, QUERY_HEADS * HEAD_SIZE), bf16), jax.ShapeDtypeStruct((64, HEAD_SIZE), f32), jax.ShapeDtypeStruct((64, HEAD_SIZE), f32)),
        in_specs=[SMEM, ANY, ANY, VMEM, VMEM, VMEM, HBM], out_specs=(VMEM, VMEM, VMEM),
        scratch_shapes=[pltpu.VMEM((2, QROWS, HALF), bf16), pltpu.VMEM((2, ROWS, 2 * HEAD_SIZE), bf16), pltpu.VMEM((DEC_SLOTS + HIST_SLOTS, PAGE_TOKENS, 4 * HEAD_SIZE), bf16), pltpu.SemaphoreType.DMA((4,))],
        compiler_params=pltpu.CompilerParams(vmem_limit_bytes=48 << 20),
        cost_estimate=pl.CostEstimate(flops=10**10, bytes_accessed=8 * 10**6, transcendentals=3 * 10**6),
    )(info, q_own, kv_own, packed, bias_private, bias_new, pages)


def finish_kernel(groups, shared, local, local_stat, out):
    row = lax.broadcasted_iota(jnp.int32, (DEC, STAT + 128), 0)
    chosen = jnp.zeros((DEC, STAT + 128), f32)
    for r in range(DEC):
        chosen = jnp.where(row == r, shared[groups[r]].astype(f32), chosen)
    for head in range(QUERY_HEADS):
        rows = slice(head*DEC,(head+1)*DEC)
        at = slice(head * HEAD_SIZE, (head + 1) * HEAD_SIZE)
        at_stat = STAT + head
        far = (
            chosen[:, at_stat : at_stat + 1]
            + chosen[:, at_stat + QUERY_HEADS : at_stat + QUERY_HEADS + 1]
            + chosen[:, at_stat + 2 * QUERY_HEADS : at_stat + 2 * QUERY_HEADS + 1]
        )
        near = local_stat[rows, 0:1]
        top = jnp.maximum(far, near)
        far = jnp.exp(far - top); near = jnp.exp(near - top)
        whole = far + near
        out[:, at] = (chosen[:, at] * (far/whole) + local[rows, :] * (near/whole)).astype(bf16)
def finish(groups, shared, local, local_stat):
    return pl.pallas_call(finish_kernel, name="finish", out_shape=jax.ShapeDtypeStruct((DEC, QUERY_HEADS * HEAD_SIZE), bf16),
        in_specs=[SMEM, VMEM, VMEM, VMEM], out_specs=VMEM, compiler_params=pltpu.CompilerParams(vmem_limit_bytes=8 << 20))(groups, shared, local, local_stat)


def small_lookup(entries, indices):
    matches = indices[..., None] == jnp.arange(entries.shape[0], dtype=jnp.int32)
    return jnp.sum(jnp.where(matches, entries, 0), axis=-1)


def rms_scaled(values, gain):
    widened = values.astype(f32)
    factor = lax.rsqrt(jnp.mean(widened * widened, axis=-1, keepdims=True) + epsilon)
    return (widened * factor * gain.astype(f32)).astype(bf16)


def weight_block(w_query, key_value_weight):
    key_half = key_value_weight.reshape(16, 2, 2, HEAD_SIZE)
    halves = [
        jnp.concatenate([w_query[:, c * HALF : (c + 1) * HALF], key_half[:, 0, c], key_half[:, 1, c]], axis=1)
        for c in range(2)
    ]
    return jnp.stack(halves, axis=0)


def main_column(block):
    sent = jnp.broadcast_to(block[None, :, None], (2, 2, 4, 16, WIDE)).reshape(16, 16, WIDE)
    return lax.all_to_all(sent, ("zh", "c", "zl"), 0, 0, tiled=True)


def on_device(
    x_pre, x_dec, rec_hidden, norm_gain, w_query, key_value_weight, cache_pool, shared_kv,
    dec_len, dec_table, dec_group, prefix_len, pre_start, pre_table, rec_req, rec_off,
):
    core = lax.axis_index("c")
    place = lax.axis_index("zl") * 4 + lax.axis_index("y")
    lengths = dec_len[0]
    page_table = dec_table[0]
    groups = dec_group[0]
    prefix_line = prefix_len[0]
    request = rec_req[0]
    within = rec_off[0]

    column = main_column(weight_block(w_query, key_value_weight))
    weights = lax.all_gather(column.reshape(256, WIDE), ("x", "y"), axis=0, tiled=True)
    weights = weights.reshape(16, 2, 2, 4, 16, WIDE)

    dec_pos = small_lookup(prefix_line, groups) + lengths
    parts = jnp.stack([dec_pos // 64, dec_pos % 64], axis=1).astype(bf16)
    extra = jnp.concatenate([x_dec, parts, jnp.zeros((DEC, 126), bf16)], axis=1)
    normed_pre = rms_scaled(x_pre, norm_gain)
    normed_rec = rms_scaled(rec_hidden, norm_gain)

    counts = (lengths + PAGE_TOKENS - 1) // PAGE_TOKENS
    ends = jnp.cumsum(counts)
    firsts = ends - counts
    slot = jnp.arange(DEC_SLOTS, dtype=jnp.int32)
    slot_request = jnp.sum((slot[:, None] >= ends[None, :]).astype(jnp.int32), axis=1)
    used = slot_request < DEC
    slot_request = jnp.minimum(slot_request, DEC - 1)
    slot_page = jnp.where(used, slot - small_lookup(firsts, slot_request), 0)
    dec_pages = small_lookup(page_table.reshape(-1), slot_request * page_table.shape[1] + slot_page)
    slots = jnp.concatenate([dec_pages, pre_table[0]], axis=0)

    pages = take_pages(slots, cache_pool)

    line = lax.all_to_all(
        jnp.broadcast_to(extra[None], (16, DEC, MODEL + 128)), DP, 0, 0, tiled=True
    ).reshape(LINE, MODEL + 128)
    line_parts = line[:, MODEL : MODEL + 2].astype(jnp.int32)
    line_pos = line_parts[:, 0] * 64 + line_parts[:, 1]
    normed_line = rms_scaled(line[:, :MODEL], norm_gain)
    pre_pos = pre_start[0] + jnp.arange(PRE, dtype=jnp.int32)
    rec_pos = small_lookup(prefix_line, small_lookup(groups, request)) + within
    positions = jnp.concatenate([pre_pos, line_pos, rec_pos], axis=0)
    half_dim = HEAD_SIZE // 2
    frequency = theta_base ** (-jnp.arange(half_dim, dtype=f32) * 2.0 / HEAD_SIZE)
    angles = positions.astype(f32)[:, None] * frequency
    cosines = jnp.cos(angles)
    sines = jnp.sin(angles)
    table = jnp.concatenate([cosines, cosines, -sines, sines], axis=1)
    swap = [(0, 1), (1, 0)]
    own = (normed_pre, normed_line, normed_rec)
    other = [lax.ppermute(v, "c", swap) for v in own]
    other_table = lax.ppermute(table, "c", swap)
    rows = jnp.concatenate([own[0], own[1], other[0], other[1], own[2], other[2]], axis=0)

    key_pos = slot_page[:, None] * PAGE_TOKENS + jnp.arange(PAGE_TOKENS, dtype=jnp.int32)[None, :]
    valid = used[:, None] & (key_pos < small_lookup(lengths, slot_request)[:, None])
    rec_slot = small_lookup(firsts, request) + within // PAGE_TOKENS
    slot_hot = (rec_slot[None, :] == slot[:, None]).astype(bf16)
    token_hot = (within[:, None] % PAGE_TOKENS == jnp.arange(PAGE_TOKENS, dtype=jnp.int32)[None, :]).astype(bf16)
    replaced = jnp.dot(slot_hot, token_hot, preferred_element_type=f32) > 0.5
    kept = (valid & ~replaced).reshape(-1)
    eight = jnp.arange(8, dtype=jnp.int32) % DEC
    key_request = jnp.repeat(slot_request, PAGE_TOKENS)
    bias_private = jnp.where(kept[None, :] & (key_request[None, :] == eight[:, None]), 0.0, negative_large)
    new_request = jnp.concatenate(
        [jnp.full((PRE,), -1, jnp.int32), jnp.arange(LINE, dtype=jnp.int32) - place * DEC, request], axis=0
    )
    bias_new = jnp.where(new_request[None, :] == eight[:, None], 0.0, negative_large)
    own_prefix = small_lookup(prefix_line, place[None])[0]
    info = jnp.stack([core, own_prefix, pre_start[0], place]).astype(jnp.int32)

    weights, rows, table, other_table, pages, bias_private, bias_new, info = lax.optimization_barrier(
        (weights, rows, table, other_table, pages, bias_private, bias_new, info)
    )
    q_own, kv_own, packed = project(weights, rows, table, other_table)
    packed = lax.ppermute(packed, "c", swap)
    shared_part = shared_attention(info, q_own, packed, shared_kv)
    shared_part = lax.all_to_all(shared_part, DP, 0, 0, tiled=True)
    out_pre, dec_part, dec_stat = local_attention(
        info, q_own, kv_own, packed, bias_private, bias_new, pages
    )
    out_dec = finish(groups, shared_part, dec_part, dec_stat)
    return (out_pre, out_dec)


def solution(mesh):
    split = Mesh(mesh.devices.reshape(2, 4, 2, 4, 4), AXES)
    first = P(AXES, None)
    second = P(AXES, None, None)
    return jax.shard_map(
        on_device,
        mesh=split,
        in_specs=(
            first, first, first, P(), first, first, second, first,
            first, second, first, P(("zh", "x", "c"), None), P(AXES), first, first, first,
        ),
        out_specs=(first, first),
        check_vma=False,
    )
```

```python
import functools

import jax
import jax.numpy as jnp
from jax import lax
from jax.experimental import pallas as pl
from jax.experimental.pallas import tpu as pltpu
from jax.sharding import Mesh
from jax.sharding import PartitionSpec as P

QUERY_HEADS = 16
KEY_VALUE_HEADS = 2
GROUP = QUERY_HEADS // KEY_VALUE_HEADS
HEAD_SIZE = 128
PAGE_TOKENS = 64
PRE = 128
DEC = 4
REC = 320
LINE = 64
ROWS = PRE + LINE + REC
QROWS = PRE + LINE
DEC_SLOTS = 68
HIST_SLOTS = 16
HALF = GROUP * HEAD_SIZE
WIDE = HALF + 2 * HEAD_SIZE
MODEL = 4096
SPAN = 512
STAT = QUERY_HEADS * HEAD_SIZE
SPLIT = 512
HEADS_AT_ONCE = 2
LOG2E = 1.4426950408889634

AXES = ("zh", "x", "c", "zl", "y")
DP = ("zl", "y")

theta_base = 5000000.0
epsilon = 1e-05
negative_large = -1e30
scale = HEAD_SIZE**-0.5

f32 = jnp.float32
bf16 = jnp.bfloat16
ANY = pl.BlockSpec(memory_space=pl.ANY)
VMEM = pl.BlockSpec(memory_space=pltpu.VMEM)
HBM = pl.BlockSpec(memory_space=pltpu.HBM)
SMEM = pl.BlockSpec(memory_space=pltpu.SMEM)


def dot_t(a, b):
    return lax.dot_general(a, b, (((1,), (1,)), ((), ())), preferred_element_type=f32)


def dot(a, b):
    return lax.dot_general(a, b, (((1,), (0,)), ((), ())), preferred_element_type=f32)


def turned(values, tab):
    return values * tab[:, :HEAD_SIZE] + pltpu.roll(values, HEAD_SIZE // 2, 1) * tab[:, HEAD_SIZE:]

def project_kernel(w_hbm, own_pre, own_line, own_rec, other_pre, other_line, other_rec, tab_own, tab_oth, q_own, kv_own, packed, w, x, w_sem, x_sem):
    copies = []
    at = 0
    for part in (own_pre, own_line, other_pre, other_line, own_rec, other_rec):
        copies.append(pltpu.make_async_copy(part, x.at[at : at + part.shape[0]], x_sem.at[len(copies)]))
        at += part.shape[0]
    groups = [(0, SPLIT), (SPLIT, WIDE)]
    pieces=[]
    for k,(lo,hi) in enumerate(groups):
        for xi in range(4):
            for yi in range(4):
                pieces.append(pltpu.make_async_copy(w_hbm.at[xi*4+yi, :, :, :, :, lo:hi], w.at[:, xi, :, :, yi, :, lo:hi], w_sem.at[k, xi*4+yi]))
    for copy in copies[:4]: copy.start()
    for copy in pieces: copy.start()
    for copy in copies[4:]: copy.start()
    for copy in copies[:4]: copy.wait()
    wf = w.reshape(MODEL, WIDE)
    for k,(lo,hi) in enumerate(groups):
        for copy in pieces[k*16:(k+1)*16]: copy.wait()
        for c0 in range(lo,hi,256):
            cols=slice(c0,c0+256)
            if c0<HALF:
                acc = dot(x[0:2*QROWS, :], wf[:, cols])
                for h in range(2):
                    at = slice(c0 + h * HEAD_SIZE, c0 + (h + 1) * HEAD_SIZE)
                    part = acc[:, h * HEAD_SIZE : (h + 1) * HEAD_SIZE]
                    q_own[:, at] = turned(part[:QROWS], tab_own[0:QROWS,:]).astype(bf16)
                    packed[0:QROWS, at] = turned(part[QROWS:], tab_oth[0:QROWS,:]).astype(bf16)
            else:
                for copy in copies[4:]: copy.wait()
                acc = dot(x[...], wf[:, cols])
                for own in (True, False):
                    tab = (tab_own if own else tab_oth)[...]
                    first = acc[0:QROWS] if own else acc[QROWS : 2 * QROWS]
                    rest = acc[2 * QROWS : 2 * QROWS + REC] if own else acc[2 * QROWS + REC :]
                    both = jnp.concatenate([first, rest], axis=0)
                    keys = turned(both[:, :HEAD_SIZE], tab).astype(bf16)
                    values = both[:, HEAD_SIZE:].astype(bf16)
                    if own:
                        kv_own[:, :HEAD_SIZE] = keys
                        kv_own[:, HEAD_SIZE:] = values
                    else:
                        for b in range(4):
                            rows = slice(b * 128, (b + 1) * 128)
                            packed[QROWS:, b * 256 : b * 256 + 128] = keys[rows]
                            packed[QROWS:, b * 256 + 128 : (b + 1) * 256] = values[rows]

def project(weights, own, other, tab_own, tab_oth):
    return pl.pallas_call(
        project_kernel, name="project",
        out_shape=(jax.ShapeDtypeStruct((QROWS, HALF), bf16), jax.ShapeDtypeStruct((ROWS, 2 * HEAD_SIZE), bf16), jax.ShapeDtypeStruct((QROWS + 128, HALF), bf16)),
        in_specs=[ANY] * 7 + [VMEM, VMEM], out_specs=(VMEM, VMEM, VMEM),
        scratch_shapes=[pltpu.VMEM((2, 4, 2, 4, 4, 16, WIDE), bf16), pltpu.VMEM((2 * ROWS, MODEL), bf16),
            pltpu.SemaphoreType.DMA((2, 16)), pltpu.SemaphoreType.DMA((6,))],
        compiler_params=pltpu.CompilerParams(vmem_limit_bytes=50 << 20),
        cost_estimate=pl.CostEstimate(flops=6 * 10**9, bytes_accessed=20 * 10**6, transcendentals=0),
    )(weights, *own, *other, tab_own, tab_oth)


def shared_kernel(info, q_own, packed, kv, out, qs):
    core = info[0]
    qs[core] = q_own[PRE:QROWS, :]
    qs[1 - core] = packed[PRE:QROWS, :]
    limit = info[1]
    bias = jnp.where(lax.broadcasted_iota(jnp.int32, (1, SPAN), 1) < limit, 0.0, negative_large)
    lane = lax.broadcasted_iota(jnp.int32, (LINE, HEAD_SIZE), 1)
    stats = jnp.zeros((LINE, HEAD_SIZE), f32)
    ones = jnp.ones((SPAN, HEAD_SIZE), bf16)
    c2 = scale*LOG2E
    for s in range(KEY_VALUE_HEADS):
        keys = kv[:, s * HEAD_SIZE : (s + 1) * HEAD_SIZE]
        values = jnp.concatenate([kv[:, (2 + s) * HEAD_SIZE : (3 + s) * HEAD_SIZE], ones], axis=1)
        query = jnp.concatenate([qs[s, :, h * HEAD_SIZE : (h + 1) * HEAD_SIZE] for h in range(GROUP)], axis=0)
        scores = dot_t(query, keys) + bias
        top = jnp.max(scores, axis=-1, keepdims=True)
        weights = jnp.exp2((scores - top) * c2)
        result = dot(weights.astype(bf16), values)
        total = result[:, HEAD_SIZE:]
        done = result[:, :HEAD_SIZE] / total
        level = top * scale + jnp.log(total)
        for h in range(GROUP):
            head = s * GROUP + h
            out[:, :, head * HEAD_SIZE : (head + 1) * HEAD_SIZE] = done[h*LINE:(h+1)*LINE].reshape(16,4,HEAD_SIZE).astype(bf16)
            stats = jnp.where(lane == head, level[h*LINE:(h+1)*LINE], stats)
    high = stats.astype(bf16).astype(f32)
    left = stats - high
    middle = left.astype(bf16).astype(f32)
    low = left - middle
    parts = high + pltpu.roll(middle, QUERY_HEADS, 1) + pltpu.roll(low, 2 * QUERY_HEADS, 1)
    out[:, :, STAT:] = parts.reshape(16, 4, HEAD_SIZE).astype(bf16)
def shared_attention(info, q_own, packed, kv):
    return pl.pallas_call(shared_kernel, name="shared", out_shape=jax.ShapeDtypeStruct((16, 4, STAT + 128), bf16),
        in_specs=[SMEM, VMEM, VMEM, VMEM], out_specs=VMEM, scratch_shapes=[pltpu.VMEM((2, LINE, HALF), bf16)],
        compiler_params=pltpu.CompilerParams(vmem_limit_bytes=8 << 20),
        cost_estimate=pl.CostEstimate(flops=3 * 10**8, bytes_accessed=10**6, transcendentals=10**6))(info, q_own, packed, kv)


def pages_kernel(slots, pool, pages, held, sems, out_sem):
    copies = [
        pltpu.make_async_copy(pool.at[slots[i]], held.at[i], sems.at[i]) for i in range(DEC_SLOTS + HIST_SLOTS)
    ]
    for copy in copies:
        copy.start()
    for copy in copies:
        copy.wait()
    out = pltpu.make_async_copy(held, pages, out_sem)
    out.start()
    out.wait()


def take_pages(slots, pool):
    shape = (DEC_SLOTS + HIST_SLOTS, PAGE_TOKENS, 4 * HEAD_SIZE)
    return pl.pallas_call(
        pages_kernel,
        name="take_pages",
        out_shape=jax.ShapeDtypeStruct(shape, bf16),
        in_specs=[SMEM, HBM],
        out_specs=HBM,
        scratch_shapes=[
            pltpu.VMEM(shape, bf16),
            pltpu.SemaphoreType.DMA((DEC_SLOTS + HIST_SLOTS,)),
            pltpu.SemaphoreType.DMA,
        ],
        compiler_params=pltpu.CompilerParams(vmem_limit_bytes=12 << 20),
        cost_estimate=pl.CostEstimate(flops=0, bytes_accessed=22 * 10**6, transcendentals=0),
    )(slots, pool)


def local_kernel(info, q_own, kv_own, packed, bias_private, bias_new, pages_hbm, out_pre, out_dec, stat_dec, qs, ks, pages, sems):
    old = pltpu.make_async_copy(pages_hbm.at[DEC_SLOTS:], pages.at[DEC_SLOTS:], sems.at[0])
    old.start()
    cached = pltpu.make_async_copy(pages_hbm.at[:DEC_SLOTS], pages.at[:DEC_SLOTS], sems.at[1])
    cached.start()
    core = info[0]; start = info[2]; place = info[3]
    q_copy = pltpu.make_async_copy(q_own, qs.at[core], sems.at[2])
    q_copy.start()
    kv_copy = pltpu.make_async_copy(kv_own, ks.at[core], sems.at[3])
    kv_copy.start()
    qs[1 - core] = packed[0:QROWS, :]
    for b in range(4):
        ks[1 - core, b * 128 : (b + 1) * 128, :] = packed[QROWS:, b * 256 : (b + 1) * 256]
    history = HIST_SLOTS * PAGE_TOKENS
    seen = jnp.where(lax.broadcasted_iota(jnp.int32, (1, history), 1) < start, 0.0, negative_large)
    rows = lax.broadcasted_iota(jnp.int32, (PRE, PRE), 0)
    cols = lax.broadcasted_iota(jnp.int32, (PRE, PRE), 1)
    causal = jnp.where(cols <= rows, 0.0, negative_large)
    causal = jnp.concatenate([causal]*HEADS_AT_ONCE, axis=0)
    c2 = scale*LOG2E
    ones_h = jnp.ones((history, HEAD_SIZE), bf16)
    ones_n = jnp.ones((PRE, HEAD_SIZE), bf16)
    q_copy.wait()
    kv_copy.wait()
    old.wait()
    for s in range(KEY_VALUE_HEADS):
        old_keys = pages[DEC_SLOTS:, :, s * HEAD_SIZE : (s + 1) * HEAD_SIZE].reshape(history, HEAD_SIZE)
        old_values = pages[DEC_SLOTS:, :, (2 + s) * HEAD_SIZE : (3 + s) * HEAD_SIZE].reshape(history, HEAD_SIZE)
        old_values = jnp.concatenate([old_values, ones_h], axis=1)
        new_keys = ks[s, 0:PRE, 0:HEAD_SIZE]
        new_values = jnp.concatenate([ks[s, 0:PRE, HEAD_SIZE:], ones_n], axis=1)
        for h in range(0, GROUP, HEADS_AT_ONCE):
            query = jnp.concatenate([qs[s, 0:PRE, (h+j) * HEAD_SIZE : (h+j + 1) * HEAD_SIZE] for j in range(HEADS_AT_ONCE)], axis=0)
            first = dot_t(query, old_keys) + seen
            second = dot_t(query, new_keys) + causal
            top = jnp.maximum(jnp.max(first, axis=-1, keepdims=True), jnp.max(second, axis=-1, keepdims=True))
            first = jnp.exp2((first - top) * c2)
            second = jnp.exp2((second - top) * c2)
            result = dot(first.astype(bf16), old_values) + dot(second.astype(bf16), new_values)
            done = (result[:, :HEAD_SIZE] / result[:, HEAD_SIZE:]).astype(bf16)
            for j in range(HEADS_AT_ONCE):
                head = s * GROUP + h + j
                out_pre[:, head * HEAD_SIZE : (head + 1) * HEAD_SIZE] = done[j*PRE:(j+1)*PRE]
    private = DEC_SLOTS * PAGE_TOKENS
    R = GROUP*DEC
    row = lax.broadcasted_iota(jnp.int32, (R, GROUP*LINE), 0)
    col = lax.broadcasted_iota(jnp.int32, (R, GROUP*LINE), 1)
    pick = (row >> 2 == col >> 6) & ((col & 63) == place * DEC + (row & 3))
    pick = jnp.where(pick, 1.0, 0.0).astype(bf16)
    cached.wait()
    for s in range(KEY_VALUE_HEADS):
        old_keys = pages[:DEC_SLOTS, :, s * HEAD_SIZE : (s + 1) * HEAD_SIZE].reshape(private, HEAD_SIZE)
        old_values = pages[:DEC_SLOTS, :, (2 + s) * HEAD_SIZE : (3 + s) * HEAD_SIZE].reshape(private, HEAD_SIZE)
        new_keys = ks[s, :, 0:HEAD_SIZE]
        new_values = ks[s, :, HEAD_SIZE:]
        line = jnp.concatenate([qs[s, PRE:QROWS, h * HEAD_SIZE : (h + 1) * HEAD_SIZE] for h in range(GROUP)], axis=0)
        query = dot(pick, line).astype(bf16)
        first = (dot_t(query, old_keys).reshape(R//8, 8, private) + bias_private[...][None]).reshape(R, private)
        second = (dot_t(query, new_keys).reshape(R//8, 8, ROWS) + bias_new[...][None]).reshape(R, ROWS)
        top = jnp.maximum(jnp.max(first, axis=-1, keepdims=True), jnp.max(second, axis=-1, keepdims=True))
        first = jnp.exp2((first - top) * c2)
        second = jnp.exp2((second - top) * c2)
        total = jnp.sum(first, axis=-1, keepdims=True) + jnp.sum(second, axis=-1, keepdims=True)
        result = dot(first.astype(bf16), old_values) + dot(second.astype(bf16), new_values)
        out_dec[s*R:(s+1)*R, :] = result / total
        stat_dec[s*R:(s+1)*R, :] = jnp.broadcast_to(top * scale + jnp.log(total), (R, HEAD_SIZE))

def local_attention(info, q_own, kv_own, packed, bias_private, bias_new, pages):
    return pl.pallas_call(
        local_kernel, name="local",
        out_shape=(jax.ShapeDtypeStruct((PRE, QUERY_HEADS * HEAD_SIZE), bf16), jax.ShapeDtypeStruct((64, HEAD_SIZE), f32), jax.ShapeDtypeStruct((64, HEAD_SIZE), f32)),
        in_specs=[SMEM, ANY, ANY, VMEM, VMEM, VMEM, HBM], out_specs=(VMEM, VMEM, VMEM),
        scratch_shapes=[pltpu.VMEM((2, QROWS, HALF), bf16), pltpu.VMEM((2, ROWS, 2 * HEAD_SIZE), bf16), pltpu.VMEM((DEC_SLOTS + HIST_SLOTS, PAGE_TOKENS, 4 * HEAD_SIZE), bf16), pltpu.SemaphoreType.DMA((4,))],
        compiler_params=pltpu.CompilerParams(vmem_limit_bytes=50 << 20),
        cost_estimate=pl.CostEstimate(flops=10**10, bytes_accessed=8 * 10**6, transcendentals=3 * 10**6),
    )(info, q_own, kv_own, packed, bias_private, bias_new, pages)


def finish_kernel(groups, shared, local, local_stat, out):
    row = lax.broadcasted_iota(jnp.int32, (DEC, STAT + 128), 0)
    chosen = jnp.zeros((DEC, STAT + 128), f32)
    for r in range(DEC):
        chosen = jnp.where(row == r, shared[groups[r]].astype(f32), chosen)
    for head in range(QUERY_HEADS):
        rows = slice(head*DEC,(head+1)*DEC)
        at = slice(head * HEAD_SIZE, (head + 1) * HEAD_SIZE)
        at_stat = STAT + head
        far = (
            chosen[:, at_stat : at_stat + 1]
            + chosen[:, at_stat + QUERY_HEADS : at_stat + QUERY_HEADS + 1]
            + chosen[:, at_stat + 2 * QUERY_HEADS : at_stat + 2 * QUERY_HEADS + 1]
        )
        near = local_stat[rows, 0:1]
        top = jnp.maximum(far, near)
        far = jnp.exp(far - top); near = jnp.exp(near - top)
        whole = far + near
        out[:, at] = (chosen[:, at] * (far/whole) + local[rows, :] * (near/whole)).astype(bf16)
def finish(groups, shared, local, local_stat):
    return pl.pallas_call(finish_kernel, name="finish", out_shape=jax.ShapeDtypeStruct((DEC, QUERY_HEADS * HEAD_SIZE), bf16),
        in_specs=[SMEM, VMEM, VMEM, VMEM], out_specs=VMEM, compiler_params=pltpu.CompilerParams(vmem_limit_bytes=8 << 20))(groups, shared, local, local_stat)


def small_lookup(entries, indices):
    matches = indices[..., None] == jnp.arange(entries.shape[0], dtype=jnp.int32)
    return jnp.sum(jnp.where(matches, entries, 0), axis=-1)


def rms_scaled(values, gain):
    widened = values.astype(f32)
    factor = lax.rsqrt(jnp.mean(widened * widened, axis=-1, keepdims=True) + epsilon)
    return (widened * factor * gain.astype(f32)).astype(bf16)


def weight_block(w_query, key_value_weight):
    def cut(array, c, width, start=0):
        return array[:, start + c * width : start + (c + 1) * width]

    halves = [
        jnp.concatenate(
            [
                cut(w_query, c, HALF),
                cut(key_value_weight, c, HEAD_SIZE),
                cut(key_value_weight, c, HEAD_SIZE, 2 * HEAD_SIZE),
            ],
            axis=1,
        )
        for c in range(2)
    ]
    return jnp.stack(halves, axis=0)


def main_column(block):
    sent = jnp.broadcast_to(block[None, :, None], (2, 2, 4, 16, WIDE)).reshape(16, 16, WIDE)
    return lax.all_to_all(sent, ("zh", "c", "zl"), 0, 0, tiled=True)


def on_device(
    x_pre, x_dec, rec_hidden, norm_gain, w_query, key_value_weight, cache_pool, shared_kv,
    dec_len, dec_table, dec_group, prefix_len, pre_start, pre_table, rec_req, rec_off,
):
    core = lax.axis_index("c")
    place = lax.axis_index("zl") * 4 + lax.axis_index("y")
    lengths = dec_len[0]
    page_table = dec_table[0]
    groups = dec_group[0]
    prefix_line = prefix_len[0]
    request = rec_req[0]
    within = rec_off[0]

    column = main_column(weight_block(w_query, key_value_weight))
    weights = lax.all_gather(column.reshape(256, WIDE), ("x", "y"), axis=0, tiled=True)
    weights = weights.reshape(16, 2, 2, 4, 16, WIDE)

    dec_pos = small_lookup(prefix_line, groups) + lengths
    parts = jnp.stack([dec_pos // 64, dec_pos % 64], axis=1).astype(bf16)
    extra = jnp.concatenate([x_dec, parts, jnp.zeros((DEC, 126), bf16)], axis=1)
    normed_pre = rms_scaled(x_pre, norm_gain)
    normed_rec = rms_scaled(rec_hidden, norm_gain)

    counts = (lengths + PAGE_TOKENS - 1) // PAGE_TOKENS
    ends = jnp.cumsum(counts)
    firsts = ends - counts
    slot = jnp.arange(DEC_SLOTS, dtype=jnp.int32)
    slot_request = jnp.sum((slot[:, None] >= ends[None, :]).astype(jnp.int32), axis=1)
    used = slot_request < DEC
    slot_request = jnp.minimum(slot_request, DEC - 1)
    slot_page = jnp.where(used, slot - small_lookup(firsts, slot_request), 0)
    dec_pages = small_lookup(page_table.reshape(-1), slot_request * page_table.shape[1] + slot_page)
    slots = jnp.concatenate([dec_pages, pre_table[0]], axis=0)

    pages = take_pages(slots, cache_pool)

    line = lax.all_to_all(
        jnp.broadcast_to(extra[None], (16, DEC, MODEL + 128)), DP, 0, 0, tiled=True
    ).reshape(LINE, MODEL + 128)
    line_parts = line[:, MODEL : MODEL + 2].astype(jnp.int32)
    line_pos = line_parts[:, 0] * 64 + line_parts[:, 1]
    normed_line = rms_scaled(line[:, :MODEL], norm_gain)
    pre_pos = pre_start[0] + jnp.arange(PRE, dtype=jnp.int32)
    rec_pos = small_lookup(prefix_line, small_lookup(groups, request)) + within
    positions = jnp.concatenate([pre_pos, line_pos, rec_pos], axis=0)
    half_dim = HEAD_SIZE // 2
    frequency = theta_base ** (-jnp.arange(half_dim, dtype=f32) * 2.0 / HEAD_SIZE)
    angles = positions.astype(f32)[:, None] * frequency
    cosines = jnp.cos(angles)
    sines = jnp.sin(angles)
    table = jnp.concatenate([cosines, cosines, -sines, sines], axis=1)
    swap = [(0, 1), (1, 0)]
    own = (normed_pre, normed_line, normed_rec)
    other = [lax.ppermute(v, "c", swap) for v in own]
    other_table = lax.ppermute(table, "c", swap)

    key_pos = slot_page[:, None] * PAGE_TOKENS + jnp.arange(PAGE_TOKENS, dtype=jnp.int32)[None, :]
    valid = used[:, None] & (key_pos < small_lookup(lengths, slot_request)[:, None])
    rec_slot = small_lookup(firsts, request) + within // PAGE_TOKENS
    slot_hot = (rec_slot[None, :] == slot[:, None]).astype(bf16)
    token_hot = (within[:, None] % PAGE_TOKENS == jnp.arange(PAGE_TOKENS, dtype=jnp.int32)[None, :]).astype(bf16)
    replaced = jnp.dot(slot_hot, token_hot, preferred_element_type=f32) > 0.5
    kept = (valid & ~replaced).reshape(-1)
    eight = jnp.arange(8, dtype=jnp.int32) % DEC
    key_request = jnp.repeat(slot_request, PAGE_TOKENS)
    bias_private = jnp.where(kept[None, :] & (key_request[None, :] == eight[:, None]), 0.0, negative_large)
    new_request = jnp.concatenate(
        [jnp.full((PRE,), -1, jnp.int32), jnp.arange(LINE, dtype=jnp.int32) - place * DEC, request], axis=0
    )
    bias_new = jnp.where(new_request[None, :] == eight[:, None], 0.0, negative_large)
    own_prefix = small_lookup(prefix_line, place[None])[0]
    info = jnp.stack([core, own_prefix, pre_start[0], place]).astype(jnp.int32)

    weights, table, other_table, pages, bias_private, bias_new, info = lax.optimization_barrier(
        (weights, table, other_table, pages, bias_private, bias_new, info)
    )
    q_own, kv_own, packed = project(weights, own, other, table, other_table)
    packed = lax.ppermute(packed, "c", swap)
    shared_part = shared_attention(info, q_own, packed, shared_kv)
    shared_part = lax.all_to_all(shared_part, DP, 0, 0, tiled=True)
    out_pre, dec_part, dec_stat = local_attention(
        info, q_own, kv_own, packed, bias_private, bias_new, pages
    )
    out_dec = finish(groups, shared_part, dec_part, dec_stat)
    return (out_pre, out_dec)


def solution(mesh):
    split = Mesh(mesh.devices.reshape(2, 4, 2, 4, 4), AXES)
    first = P(AXES, None)
    second = P(AXES, None, None)
    return jax.shard_map(
        on_device,
        mesh=split,
        in_specs=(
            first, first, first, P(), first, first, second, first,
            first, second, first, P(("zh", "x", "c"), None), P(AXES), first, first, first,
        ),
        out_specs=(first, first),
        check_vma=False,
    )
```

```python
import functools

import jax
import jax.numpy as jnp
from jax import lax
from jax.experimental import pallas as pl
from jax.experimental.pallas import tpu as pltpu
from jax.sharding import Mesh
from jax.sharding import PartitionSpec as P

QUERY_HEADS = 16
KEY_VALUE_HEADS = 2
GROUP = QUERY_HEADS // KEY_VALUE_HEADS
HEAD_SIZE = 128
PAGE_TOKENS = 64
PRE = 128
DEC = 4
REC = 320
LINE = 64
ROWS = PRE + LINE + REC
QROWS = PRE + LINE
DEC_SLOTS = 68
HIST_SLOTS = 16
HALF = GROUP * HEAD_SIZE
WIDE = HALF + 2 * HEAD_SIZE
MODEL = 4096
SPAN = 512
STAT = QUERY_HEADS * HEAD_SIZE
MAIN = 896
SIDE = WIDE - MAIN
HEADS_AT_ONCE = 2
LOG2E = 1.4426950408889634

AXES = ("zh", "x", "c", "zl", "y")
DP = ("zl", "y")

theta_base = 5000000.0
epsilon = 1e-05
negative_large = -1e30
scale = HEAD_SIZE**-0.5

f32 = jnp.float32
bf16 = jnp.bfloat16
ANY = pl.BlockSpec(memory_space=pl.ANY)
VMEM = pl.BlockSpec(memory_space=pltpu.VMEM)
HBM = pl.BlockSpec(memory_space=pltpu.HBM)
SMEM = pl.BlockSpec(memory_space=pltpu.SMEM)


def dot_t(a, b):
    return lax.dot_general(a, b, (((1,), (1,)), ((), ())), preferred_element_type=f32)


def dot(a, b):
    return lax.dot_general(a, b, (((1,), (0,)), ((), ())), preferred_element_type=f32)


def turned(values, tab):
    return values * tab[:, :HEAD_SIZE] + pltpu.roll(values, HEAD_SIZE // 2, 1) * tab[:, HEAD_SIZE:]


def project_kernel(
    info, main_hbm, z0, up1, down1, up2, down2, up3, down3, up4, down4,
    own_pre, own_line, own_rec, other_pre, other_line, other_rec, tab_own, tab_oth,
    q_own, kv_own, packed, main, side, x, main_sem, side_sem, x_sem,
):
    here = info[4]
    side_copies = []
    for i, (block, far) in enumerate(zip((z0, up1, down1, up2, down2, up3, down3), (0, -1, 1, -2, 2, -3, 3))):
        z = (here + far) & 7
        side_copies.append(pltpu.make_async_copy(block, side.at[z >> 2, :, :, z & 3], side_sem.at[i]))
    z = (here + 4) & 7
    side_copies.append(pltpu.make_async_copy(up4, side.at[z >> 2, 0:2, :, z & 3], side_sem.at[7]))
    side_copies.append(pltpu.make_async_copy(down4, side.at[z >> 2, 2:4, :, z & 3], side_sem.at[8]))
    groups = [(0, 512), (512, MAIN)]
    main_copies = []
    for k, (lo, hi) in enumerate(groups):
        for xi in range(4):
            for yi in range(4):
                main_copies.append(
                    pltpu.make_async_copy(
                        main_hbm.at[xi * 4 + yi, :, :, :, :, lo:hi],
                        main.at[:, xi, :, :, yi, :, lo:hi],
                        main_sem.at[k, xi * 4 + yi],
                    )
                )
    x_copies = []
    at = 0
    for part in (own_pre, own_line, other_pre, other_line, own_rec, other_rec):
        x_copies.append(pltpu.make_async_copy(part, x.at[at : at + part.shape[0]], x_sem.at[len(x_copies)]))
        at += part.shape[0]
    for copy in x_copies[:4] + main_copies + side_copies + x_copies[4:]:
        copy.start()
    for copy in x_copies[:4]:
        copy.wait()

    def store_queries(acc, first_head):
        for h in range(acc.shape[1] // HEAD_SIZE):
            at = slice((first_head + h) * HEAD_SIZE, (first_head + h + 1) * HEAD_SIZE)
            part = acc[:, h * HEAD_SIZE : (h + 1) * HEAD_SIZE]
            q_own[:, at] = turned(part[:QROWS], tab_own[0:QROWS, :]).astype(bf16)
            packed[0:QROWS, at] = turned(part[QROWS:], tab_oth[0:QROWS, :]).astype(bf16)

    main_flat = main.reshape(MODEL, MAIN)
    for k, (lo, hi) in enumerate(groups):
        for copy in main_copies[k * 16 : (k + 1) * 16]:
            copy.wait()
        for c0 in range(lo, hi, 256):
            c1 = min(c0 + 256, hi)
            store_queries(dot(x[0 : 2 * QROWS, :], main_flat[:, c0:c1]), c0 // HEAD_SIZE)
    for copy in side_copies + x_copies[4:]:
        copy.wait()
    side_flat = side.reshape(MODEL, SIDE)
    acc = dot(x[...], side_flat[:, SIDE - 256 :])
    for own in (True, False):
        tab = (tab_own if own else tab_oth)[...]
        first = acc[0:QROWS] if own else acc[QROWS : 2 * QROWS]
        rest = acc[2 * QROWS : 2 * QROWS + REC] if own else acc[2 * QROWS + REC :]
        both = jnp.concatenate([first, rest], axis=0)
        keys = turned(both[:, :HEAD_SIZE], tab).astype(bf16)
        values = both[:, HEAD_SIZE:].astype(bf16)
        if own:
            kv_own[:, :HEAD_SIZE] = keys
            kv_own[:, HEAD_SIZE:] = values
        else:
            for b in range(4):
                rows = slice(b * 128, (b + 1) * 128)
                packed[QROWS:, b * 256 : b * 256 + 128] = keys[rows]
                packed[QROWS:, b * 256 + 128 : (b + 1) * 256] = values[rows]
    store_queries(dot(x[0 : 2 * QROWS, :], side_flat[:, : SIDE - 256]), MAIN // HEAD_SIZE)


def project(info, main, side, own, other, tab_own, tab_oth):
    return pl.pallas_call(
        project_kernel,
        name="project",
        out_shape=(
            jax.ShapeDtypeStruct((QROWS, HALF), bf16),
            jax.ShapeDtypeStruct((ROWS, 2 * HEAD_SIZE), bf16),
            jax.ShapeDtypeStruct((QROWS + 128, HALF), bf16),
        ),
        in_specs=[SMEM] + [ANY] * 16 + [VMEM] * 2,
        out_specs=(VMEM, VMEM, VMEM),
        scratch_shapes=[
            pltpu.VMEM((2, 4, 2, 4, 4, 16, MAIN), bf16),
            pltpu.VMEM((2, 4, 2, 4, 4, 16, SIDE), bf16),
            pltpu.VMEM((2 * ROWS, MODEL), bf16),
            pltpu.SemaphoreType.DMA((2, 16)),
            pltpu.SemaphoreType.DMA((9,)),
            pltpu.SemaphoreType.DMA((6,)),
        ],
        compiler_params=pltpu.CompilerParams(vmem_limit_bytes=50 << 20),
        cost_estimate=pl.CostEstimate(flops=6 * 10**9, bytes_accessed=20 * 10**6, transcendentals=0),
    )(info, main, *side, *own, *other, tab_own, tab_oth)


def shared_kernel(info, q_own, packed, kv, out, qs):
    core = info[0]
    qs[core] = q_own[PRE:QROWS, :]
    qs[1 - core] = packed[PRE:QROWS, :]
    limit = info[1]
    bias = jnp.where(lax.broadcasted_iota(jnp.int32, (1, SPAN), 1) < limit, 0.0, negative_large)
    lane = lax.broadcasted_iota(jnp.int32, (LINE, HEAD_SIZE), 1)
    stats = jnp.zeros((LINE, HEAD_SIZE), f32)
    ones = jnp.ones((SPAN, HEAD_SIZE), bf16)
    c2 = scale*LOG2E
    for s in range(KEY_VALUE_HEADS):
        keys = kv[:, s * HEAD_SIZE : (s + 1) * HEAD_SIZE]
        values = jnp.concatenate([kv[:, (2 + s) * HEAD_SIZE : (3 + s) * HEAD_SIZE], ones], axis=1)
        query = jnp.concatenate([qs[s, :, h * HEAD_SIZE : (h + 1) * HEAD_SIZE] for h in range(GROUP)], axis=0)
        scores = dot_t(query, keys) + bias
        top = jnp.max(scores, axis=-1, keepdims=True)
        weights = jnp.exp2((scores - top) * c2)
        result = dot(weights.astype(bf16), values)
        total = result[:, HEAD_SIZE:]
        done = result[:, :HEAD_SIZE] / total
        level = top * scale + jnp.log(total)
        for h in range(GROUP):
            head = s * GROUP + h
            out[:, :, head * HEAD_SIZE : (head + 1) * HEAD_SIZE] = done[h*LINE:(h+1)*LINE].reshape(16,4,HEAD_SIZE).astype(bf16)
            stats = jnp.where(lane == head, level[h*LINE:(h+1)*LINE], stats)
    high = stats.astype(bf16).astype(f32)
    left = stats - high
    middle = left.astype(bf16).astype(f32)
    low = left - middle
    parts = high + pltpu.roll(middle, QUERY_HEADS, 1) + pltpu.roll(low, 2 * QUERY_HEADS, 1)
    out[:, :, STAT:] = parts.reshape(16, 4, HEAD_SIZE).astype(bf16)
def shared_attention(info, q_own, packed, kv):
    return pl.pallas_call(shared_kernel, name="shared", out_shape=jax.ShapeDtypeStruct((16, 4, STAT + 128), bf16),
        in_specs=[SMEM, VMEM, VMEM, VMEM], out_specs=VMEM, scratch_shapes=[pltpu.VMEM((2, LINE, HALF), bf16)],
        compiler_params=pltpu.CompilerParams(vmem_limit_bytes=8 << 20),
        cost_estimate=pl.CostEstimate(flops=3 * 10**8, bytes_accessed=10**6, transcendentals=10**6))(info, q_own, packed, kv)


def pages_kernel(slots, pool, pages, held, sems, out_sem):
    copies = [
        pltpu.make_async_copy(pool.at[slots[i]], held.at[i], sems.at[i]) for i in range(DEC_SLOTS + HIST_SLOTS)
    ]
    for copy in copies:
        copy.start()
    for copy in copies:
        copy.wait()
    out = pltpu.make_async_copy(held, pages, out_sem)
    out.start()
    out.wait()


def take_pages(slots, pool):
    shape = (DEC_SLOTS + HIST_SLOTS, PAGE_TOKENS, 4 * HEAD_SIZE)
    return pl.pallas_call(
        pages_kernel,
        name="take_pages",
        out_shape=jax.ShapeDtypeStruct(shape, bf16),
        in_specs=[SMEM, HBM],
        out_specs=HBM,
        scratch_shapes=[
            pltpu.VMEM(shape, bf16),
            pltpu.SemaphoreType.DMA((DEC_SLOTS + HIST_SLOTS,)),
            pltpu.SemaphoreType.DMA,
        ],
        compiler_params=pltpu.CompilerParams(vmem_limit_bytes=12 << 20),
        cost_estimate=pl.CostEstimate(flops=0, bytes_accessed=22 * 10**6, transcendentals=0),
    )(slots, pool)


def local_kernel(info, q_own, kv_own, packed, bias_private, bias_new, pages_hbm, out_pre, out_dec, stat_dec, qs, ks, pages, sems):
    old = pltpu.make_async_copy(pages_hbm.at[DEC_SLOTS:], pages.at[DEC_SLOTS:], sems.at[0])
    old.start()
    cached = pltpu.make_async_copy(pages_hbm.at[:DEC_SLOTS], pages.at[:DEC_SLOTS], sems.at[1])
    cached.start()
    core = info[0]; start = info[2]; place = info[3]
    q_copy = pltpu.make_async_copy(q_own, qs.at[core], sems.at[2])
    q_copy.start()
    kv_copy = pltpu.make_async_copy(kv_own, ks.at[core], sems.at[3])
    kv_copy.start()
    qs[1 - core] = packed[0:QROWS, :]
    for b in range(4):
        ks[1 - core, b * 128 : (b + 1) * 128, :] = packed[QROWS:, b * 256 : (b + 1) * 256]
    history = HIST_SLOTS * PAGE_TOKENS
    seen = jnp.where(lax.broadcasted_iota(jnp.int32, (1, history), 1) < start, 0.0, negative_large)
    rows = lax.broadcasted_iota(jnp.int32, (PRE, PRE), 0)
    cols = lax.broadcasted_iota(jnp.int32, (PRE, PRE), 1)
    causal = jnp.where(cols <= rows, 0.0, negative_large)
    causal = jnp.concatenate([causal]*HEADS_AT_ONCE, axis=0)
    c2 = scale*LOG2E
    ones_h = jnp.ones((history, HEAD_SIZE), bf16)
    ones_n = jnp.ones((PRE, HEAD_SIZE), bf16)
    q_copy.wait()
    kv_copy.wait()
    old.wait()
    for s in range(KEY_VALUE_HEADS):
        old_keys = pages[DEC_SLOTS:, :, s * HEAD_SIZE : (s + 1) * HEAD_SIZE].reshape(history, HEAD_SIZE)
        old_values = pages[DEC_SLOTS:, :, (2 + s) * HEAD_SIZE : (3 + s) * HEAD_SIZE].reshape(history, HEAD_SIZE)
        old_values = jnp.concatenate([old_values, ones_h], axis=1)
        new_keys = ks[s, 0:PRE, 0:HEAD_SIZE]
        new_values = jnp.concatenate([ks[s, 0:PRE, HEAD_SIZE:], ones_n], axis=1)
        for h in range(0, GROUP, HEADS_AT_ONCE):
            query = jnp.concatenate([qs[s, 0:PRE, (h+j) * HEAD_SIZE : (h+j + 1) * HEAD_SIZE] for j in range(HEADS_AT_ONCE)], axis=0)
            first = dot_t(query, old_keys) + seen
            second = dot_t(query, new_keys) + causal
            top = jnp.maximum(jnp.max(first, axis=-1, keepdims=True), jnp.max(second, axis=-1, keepdims=True))
            first = jnp.exp2((first - top) * c2)
            second = jnp.exp2((second - top) * c2)
            result = dot(first.astype(bf16), old_values) + dot(second.astype(bf16), new_values)
            done = (result[:, :HEAD_SIZE] / result[:, HEAD_SIZE:]).astype(bf16)
            for j in range(HEADS_AT_ONCE):
                head = s * GROUP + h + j
                out_pre[:, head * HEAD_SIZE : (head + 1) * HEAD_SIZE] = done[j*PRE:(j+1)*PRE]
    private = DEC_SLOTS * PAGE_TOKENS
    R = GROUP*DEC
    row = lax.broadcasted_iota(jnp.int32, (R, GROUP*LINE), 0)
    col = lax.broadcasted_iota(jnp.int32, (R, GROUP*LINE), 1)
    pick = (row >> 2 == col >> 6) & ((col & 63) == place * DEC + (row & 3))
    pick = jnp.where(pick, 1.0, 0.0).astype(bf16)
    cached.wait()
    for s in range(KEY_VALUE_HEADS):
        old_keys = pages[:DEC_SLOTS, :, s * HEAD_SIZE : (s + 1) * HEAD_SIZE].reshape(private, HEAD_SIZE)
        old_values = pages[:DEC_SLOTS, :, (2 + s) * HEAD_SIZE : (3 + s) * HEAD_SIZE].reshape(private, HEAD_SIZE)
        new_keys = ks[s, :, 0:HEAD_SIZE]
        new_values = ks[s, :, HEAD_SIZE:]
        line = jnp.concatenate([qs[s, PRE:QROWS, h * HEAD_SIZE : (h + 1) * HEAD_SIZE] for h in range(GROUP)], axis=0)
        query = dot(pick, line).astype(bf16)
        first = (dot_t(query, old_keys).reshape(R//8, 8, private) + bias_private[...][None]).reshape(R, private)
        second = (dot_t(query, new_keys).reshape(R//8, 8, ROWS) + bias_new[...][None]).reshape(R, ROWS)
        top = jnp.maximum(jnp.max(first, axis=-1, keepdims=True), jnp.max(second, axis=-1, keepdims=True))
        first = jnp.exp2((first - top) * c2)
        second = jnp.exp2((second - top) * c2)
        total = jnp.sum(first, axis=-1, keepdims=True) + jnp.sum(second, axis=-1, keepdims=True)
        result = dot(first.astype(bf16), old_values) + dot(second.astype(bf16), new_values)
        out_dec[s*R:(s+1)*R, :] = result / total
        stat_dec[s*R:(s+1)*R, :] = jnp.broadcast_to(top * scale + jnp.log(total), (R, HEAD_SIZE))

def local_attention(info, q_own, kv_own, packed, bias_private, bias_new, pages):
    return pl.pallas_call(
        local_kernel, name="local",
        out_shape=(jax.ShapeDtypeStruct((PRE, QUERY_HEADS * HEAD_SIZE), bf16), jax.ShapeDtypeStruct((64, HEAD_SIZE), f32), jax.ShapeDtypeStruct((64, HEAD_SIZE), f32)),
        in_specs=[SMEM, ANY, ANY, VMEM, VMEM, VMEM, HBM], out_specs=(VMEM, VMEM, VMEM),
        scratch_shapes=[pltpu.VMEM((2, QROWS, HALF), bf16), pltpu.VMEM((2, ROWS, 2 * HEAD_SIZE), bf16), pltpu.VMEM((DEC_SLOTS + HIST_SLOTS, PAGE_TOKENS, 4 * HEAD_SIZE), bf16), pltpu.SemaphoreType.DMA((4,))],
        compiler_params=pltpu.CompilerParams(vmem_limit_bytes=50 << 20),
        cost_estimate=pl.CostEstimate(flops=10**10, bytes_accessed=8 * 10**6, transcendentals=3 * 10**6),
    )(info, q_own, kv_own, packed, bias_private, bias_new, pages)


def finish_kernel(groups, shared, local, local_stat, out):
    row = lax.broadcasted_iota(jnp.int32, (DEC, STAT + 128), 0)
    chosen = jnp.zeros((DEC, STAT + 128), f32)
    for r in range(DEC):
        chosen = jnp.where(row == r, shared[groups[r]].astype(f32), chosen)
    for head in range(QUERY_HEADS):
        rows = slice(head*DEC,(head+1)*DEC)
        at = slice(head * HEAD_SIZE, (head + 1) * HEAD_SIZE)
        at_stat = STAT + head
        far = (
            chosen[:, at_stat : at_stat + 1]
            + chosen[:, at_stat + QUERY_HEADS : at_stat + QUERY_HEADS + 1]
            + chosen[:, at_stat + 2 * QUERY_HEADS : at_stat + 2 * QUERY_HEADS + 1]
        )
        near = local_stat[rows, 0:1]
        top = jnp.maximum(far, near)
        far = jnp.exp(far - top); near = jnp.exp(near - top)
        whole = far + near
        out[:, at] = (chosen[:, at] * (far/whole) + local[rows, :] * (near/whole)).astype(bf16)
def finish(groups, shared, local, local_stat):
    return pl.pallas_call(finish_kernel, name="finish", out_shape=jax.ShapeDtypeStruct((DEC, QUERY_HEADS * HEAD_SIZE), bf16),
        in_specs=[SMEM, VMEM, VMEM, VMEM], out_specs=VMEM, compiler_params=pltpu.CompilerParams(vmem_limit_bytes=8 << 20))(groups, shared, local, local_stat)


def small_lookup(entries, indices):
    matches = indices[..., None] == jnp.arange(entries.shape[0], dtype=jnp.int32)
    return jnp.sum(jnp.where(matches, entries, 0), axis=-1)


def rms_scaled(values, gain):
    widened = values.astype(f32)
    factor = lax.rsqrt(jnp.mean(widened * widened, axis=-1, keepdims=True) + epsilon)
    return (widened * factor * gain.astype(f32)).astype(bf16)


def along_z(step):
    pairs = []
    for i in range(256):
        z = (i // 128) * 4 + (i // 4) % 4
        to = (z + step) % 8
        pairs.append((i, i % 128 - (i // 4) % 4 * 4 + (to // 4) * 128 + (to % 4) * 4))
    return pairs


def weight_block(w_query, key_value_weight):
    def cut(array, c, width, start=0):
        return array[:, start + c * width : start + (c + 1) * width]

    halves = [
        jnp.concatenate(
            [
                cut(w_query, c, HALF),
                cut(key_value_weight, c, HEAD_SIZE),
                cut(key_value_weight, c, HEAD_SIZE, 2 * HEAD_SIZE),
            ],
            axis=1,
        )
        for c in range(2)
    ]
    return jnp.stack(halves, axis=0)


def main_column(block):
    sent = jnp.broadcast_to(block[None, :, None], (2, 2, 4, 16, MAIN)).reshape(16, 16, MAIN)
    return lax.all_to_all(sent, ("zh", "c", "zl"), 0, 0, tiled=True)


def side_plane(block):
    sent = jnp.broadcast_to(block[None, :, None], (4, 2, 4, 16, SIDE)).reshape(32, 16, SIDE)
    return lax.all_to_all(sent, ("x", "c", "y"), 0, 0, tiled=True).reshape(4, 2, 4, 16, SIDE)


def ring_step(up, down):
    return lax.ppermute(up, AXES, along_z(1)), lax.ppermute(down, AXES, along_z(-1))


def on_device(
    x_pre, x_dec, rec_hidden, norm_gain, w_query, key_value_weight, cache_pool, shared_kv,
    dec_len, dec_table, dec_group, prefix_len, pre_start, pre_table, rec_req, rec_off,
):
    core = lax.axis_index("c")
    place = lax.axis_index("zl") * 4 + lax.axis_index("y")
    lengths = dec_len[0]
    page_table = dec_table[0]
    groups = dec_group[0]
    prefix_line = prefix_len[0]
    request = rec_req[0]
    within = rec_off[0]

    block = weight_block(w_query, key_value_weight)
    column = main_column(block[:, :, :MAIN])
    rest, column = lax.optimization_barrier((block[:, :, MAIN:], column))
    main = lax.all_gather(column.reshape(256, MAIN), ("x", "y"), axis=0, tiled=True)
    main = main.reshape(16, 2, 2, 4, 16, MAIN)

    dec_pos = small_lookup(prefix_line, groups) + lengths
    parts = jnp.stack([dec_pos // 64, dec_pos % 64], axis=1).astype(bf16)
    extra = jnp.concatenate([x_dec, parts, jnp.zeros((DEC, 126), bf16)], axis=1)
    counts = (lengths + PAGE_TOKENS - 1) // PAGE_TOKENS
    ends = jnp.cumsum(counts)
    firsts = ends - counts
    slot = jnp.arange(DEC_SLOTS, dtype=jnp.int32)
    slot_request = jnp.sum((slot[:, None] >= ends[None, :]).astype(jnp.int32), axis=1)
    used = slot_request < DEC
    slot_request = jnp.minimum(slot_request, DEC - 1)
    slot_page = jnp.where(used, slot - small_lookup(firsts, slot_request), 0)
    dec_pages = small_lookup(page_table.reshape(-1), slot_request * page_table.shape[1] + slot_page)
    slots = jnp.concatenate([dec_pages, pre_table[0]], axis=0)

    plane = side_plane(rest)
    pages = take_pages(slots, cache_pool)
    plane, pages, extra, x_pre, rec_hidden = lax.optimization_barrier((plane, pages, extra, x_pre, rec_hidden))
    line = lax.all_to_all(
        jnp.broadcast_to(extra[None], (16, DEC, MODEL + 128)), DP, 0, 0, tiled=True
    ).reshape(LINE, MODEL + 128)
    up1, down1 = ring_step(plane, plane)
    normed_pre = rms_scaled(x_pre, norm_gain)
    up1, down1, normed_pre = lax.optimization_barrier((up1, down1, normed_pre))
    up2, down2 = ring_step(up1, down1)
    normed_rec = rms_scaled(rec_hidden, norm_gain)
    up2, down2, normed_rec, line = lax.optimization_barrier((up2, down2, normed_rec, line))
    line_parts = line[:, MODEL : MODEL + 2].astype(jnp.int32)
    line_pos = line_parts[:, 0] * 64 + line_parts[:, 1]
    normed_line = rms_scaled(line[:, :MODEL], norm_gain)
    up3, down3 = ring_step(up2, down2)
    up4, down4 = ring_step(up3[:2], down3[2:])
    side = (plane, up1, down1, up2, down2, up3, down3, up4, down4)

    pre_pos = pre_start[0] + jnp.arange(PRE, dtype=jnp.int32)
    rec_pos = small_lookup(prefix_line, small_lookup(groups, request)) + within
    positions = jnp.concatenate([pre_pos, line_pos, rec_pos], axis=0)
    half_dim = HEAD_SIZE // 2
    frequency = theta_base ** (-jnp.arange(half_dim, dtype=f32) * 2.0 / HEAD_SIZE)
    angles = positions.astype(f32)[:, None] * frequency
    cosines = jnp.cos(angles)
    sines = jnp.sin(angles)
    table = jnp.concatenate([cosines, cosines, -sines, sines], axis=1)
    swap = [(0, 1), (1, 0)]
    own = (normed_pre, normed_line, normed_rec)
    other = [lax.ppermute(v, "c", swap) for v in own]
    other_table = lax.ppermute(table, "c", swap)

    key_pos = slot_page[:, None] * PAGE_TOKENS + jnp.arange(PAGE_TOKENS, dtype=jnp.int32)[None, :]
    valid = used[:, None] & (key_pos < small_lookup(lengths, slot_request)[:, None])
    rec_slot = small_lookup(firsts, request) + within // PAGE_TOKENS
    slot_hot = (rec_slot[None, :] == slot[:, None]).astype(bf16)
    token_hot = (within[:, None] % PAGE_TOKENS == jnp.arange(PAGE_TOKENS, dtype=jnp.int32)[None, :]).astype(bf16)
    replaced = jnp.dot(slot_hot, token_hot, preferred_element_type=f32) > 0.5
    kept = (valid & ~replaced).reshape(-1)
    eight = jnp.arange(8, dtype=jnp.int32) % DEC
    key_request = jnp.repeat(slot_request, PAGE_TOKENS)
    bias_private = jnp.where(kept[None, :] & (key_request[None, :] == eight[:, None]), 0.0, negative_large)
    new_request = jnp.concatenate(
        [jnp.full((PRE,), -1, jnp.int32), jnp.arange(LINE, dtype=jnp.int32) - place * DEC, request], axis=0
    )
    bias_new = jnp.where(new_request[None, :] == eight[:, None], 0.0, negative_large)
    own_prefix = small_lookup(prefix_line, place[None])[0]
    depth = lax.axis_index("zh") * 4 + lax.axis_index("zl")
    info = jnp.stack([core, own_prefix, pre_start[0], place, depth]).astype(jnp.int32)

    main, table, other_table, bias_private, bias_new, info = lax.optimization_barrier(
        (main, table, other_table, bias_private, bias_new, info)
    )
    q_own, kv_own, packed = project(info, main, side, own, other, table, other_table)
    packed = lax.ppermute(packed, "c", swap)
    shared_part = shared_attention(info, q_own, packed, shared_kv)
    shared_part = lax.all_to_all(shared_part, DP, 0, 0, tiled=True)
    out_pre, dec_part, dec_stat = local_attention(
        info, q_own, kv_own, packed, bias_private, bias_new, pages
    )
    out_dec = finish(groups, shared_part, dec_part, dec_stat)
    return (out_pre, out_dec)


def solution(mesh):
    split = Mesh(mesh.devices.reshape(2, 4, 2, 4, 4), AXES)
    first = P(AXES, None)
    second = P(AXES, None, None)
    return jax.shard_map(
        on_device,
        mesh=split,
        in_specs=(
            first, first, first, P(), first, first, second, first,
            first, second, first, P(("zh", "x", "c"), None), P(AXES), first, first, first,
        ),
        out_specs=(first, first),
        check_vma=False,
    )
```
